32 devices in a mesh: ctx: 16 (over z, y, core), head: 2 (over x).
Axes of the slice: x: 2, y: 2, z: 4, core: 2. Of those that a mesh axis runs over, the one named last changes fastest.
Arguments:
- query_in: bfloat16 [2048, 2048], P('ctx', 'head'), may hold values from -6 to 6
- key_in: bfloat16 [2048, 2, 2048], P('ctx', None, 'head'), may hold values from -6 to 6
- value_in: bfloat16 [2048, 2, 2048], P('ctx', None, 'head'), may hold values from -6 to 6
- beta_logit: float32 [2048, 2, 16], P('ctx', None, 'head'), may hold values from -6 to 8
- query_conv: float32 [4, 2048], P(None, 'head'), may hold values from -2.5 to 2.5
- key_conv: float32 [4, 2, 2048], P(None, None, 'head'), may hold values from -2.5 to 2.5
- value_conv: float32 [4, 2, 2048], P(None, None, 'head'), may hold values from -2.5 to 2.5
- norm_gain: float32 [2048], P('head'), may hold values from 0.1 to 1.9
- out_weight: bfloat16 [2048, 2048], P('head'), may hold values from -0.125 to 0.125
- grad_out: bfloat16 [2048, 2048], P('ctx'), may hold values from -6 to 6
Outputs:
- layer_out: bfloat16 [2048, 2048], P(('ctx', 'head'))
- grad_query: float32 [2048, 2048], P('ctx', 'head')
- grad_key: float32 [2048, 2, 2048], P('ctx', None, 'head')
- grad_value: float32 [2048, 2, 2048], P('ctx', None, 'head')
- grad_beta: float32 [2048, 2, 16], P('ctx', None, 'head')
The draws below stay inside these ranges and needn't reach their ends.
All inputs are finite; a program needn't handle non-finite values.
Results may differ from the reference program's by a relative error of at most 0.014.
Values may be sent and summed in bfloat16 or wider, within the bound.
No kernel may reach another device: no remote copies, remote signals or barrier semaphores. Data moves between devices by JAX's collectives and lax.ppermute only.
A program may use at most 128 MiB of HBM per device.

```python
import jax
import jax.numpy as jnp
from jax import lax

D = 2048
H = 16
DK = 128
DV = 128
NH = 2
KW = 4
GROUP = 64
TOKENS = 2048


def draw_beta_logit(key, part):
    pick_key, keep_key, fast_key = jax.random.split(key, 3)
    slow_heads = jax.random.uniform(pick_key, (H,)) < 0.5
    fast_values = jnp.clip(1.5 * jax.random.normal(fast_key, (TOKENS, NH, H)), -6.0, 6.0)
    keep_values = jax.random.uniform(keep_key, (TOKENS, NH, H), minval=5.0, maxval=8.0)
    return jnp.where(slow_heads[None, None, :], keep_values, fast_values).astype(jnp.float32)


def levels(key, extent, shards, least, high):
    loudness, own = 1.0, jax.random.fold_in(key, 6)
    for position, blocks in shards:
        heights = jnp.exp(jax.random.uniform(jax.random.fold_in(own, position), (blocks,), jnp.float32, least / len(shards), high / len(shards)))
        loudness = loudness * jnp.repeat(heights, extent[position] // blocks).reshape([-1 if axis == position else 1 for axis in range(len(extent))])
    return loudness


def centred(own_key, dims, width, reach, cuts=(), kind=jnp.bfloat16):
    result = width * jax.random.normal(own_key, dims, jnp.float32)
    if cuts:
        result = result * levels(own_key, dims, cuts, -0.22, 0.18)
    return jnp.clip(result, -reach, reach).astype(kind)


def setup_inputs(seed: int = 0) -> dict:
    arg_keys = jax.random.split(jax.random.key(seed), 11)
    query_in = centred(arg_keys[0], (TOKENS, H * DK), 1.0, 6.0, ((0, 16), (1, 2)))
    key_in = centred(arg_keys[1], (TOKENS, NH, H * DK), 1.0, 6.0, ((0, 16), (2, 2)))
    value_in = centred(arg_keys[2], (TOKENS, NH, H * DV), 1.0, 6.0, ((0, 16), (2, 2)))
    beta_logit = draw_beta_logit(jax.random.fold_in(arg_keys[10], 71), 0)
    query_conv = centred(arg_keys[4], (KW, H * DK), 0.5, 2.5, ((1, 2),), jnp.float32)
    key_conv = centred(arg_keys[5], (KW, NH, H * DK), 0.5, 2.5, ((2, 2),), jnp.float32)
    value_conv = centred(arg_keys[6], (KW, NH, H * DV), 0.5, 2.5, ((2, 2),), jnp.float32)
    norm_gain = jnp.clip(1.0 + 0.18 * jax.random.normal(arg_keys[7], (H * DV,), jnp.float32), 0.1, 1.9)
    out_weight = centred(arg_keys[8], (H * DV, D), (H * DV) ** -0.5, 0.125, ((0, 2),))
    grad_out = centred(arg_keys[9], (TOKENS, D), 1.0, 6.0, ((0, 16),))
    return dict(query_in=query_in, key_in=key_in, value_in=value_in, beta_logit=beta_logit, query_conv=query_conv, key_conv=key_conv, value_conv=value_conv, norm_gain=norm_gain, out_weight=out_weight, grad_out=grad_out)


highest = lax.Precision.HIGHEST
epsilon = 1e-06

def causal_conv(raw_rows, edge_rows, kernel):
    padded = jnp.concatenate([edge_rows, raw_rows], axis=0)
    length = raw_rows.shape[0]
    summed = sum((kernel[offset] * padded[offset:offset + length] for offset in range(kernel.shape[0])))
    return jax.nn.silu(summed)

def unit_norm(values):
    return values * lax.rsqrt(lax.optimization_barrier(jnp.sum(values * values, axis=-1, keepdims=True)) + epsilon)

def prepare(query_raw, key_raw, value_raw, beta_raw, edge_query, edge_key, edge_value, query_conv, key_conv, value_conv):
    token_count = query_raw.shape[0]
    slot_count = key_raw.shape[1]
    head_count = query_raw.shape[1] // DK
    blocks = token_count // GROUP
    block_rows = GROUP * slot_count
    queries = unit_norm(causal_conv(query_raw, edge_query, query_conv).reshape(token_count, head_count, DK))
    key_all = unit_norm(causal_conv(key_raw, edge_key, key_conv).reshape(token_count, slot_count, head_count, DK))
    value_all = causal_conv(value_raw, edge_value, value_conv).reshape(token_count, slot_count, head_count, DV)
    strength = 2.0 * jax.nn.sigmoid(beta_raw)
    queries = queries.reshape(blocks, GROUP, head_count, DK).transpose(0, 2, 1, 3)
    key_rows = key_all.reshape(blocks, block_rows, head_count, DK).transpose(0, 2, 1, 3)
    value_rows = value_all.reshape(blocks, block_rows, head_count, DV).transpose(0, 2, 1, 3)
    strength = strength.reshape(blocks, block_rows, head_count).transpose(0, 2, 1)
    gram = jnp.einsum('nhcd,nhed->nhce', key_rows, key_rows, precision=highest)
    system = jnp.eye(block_rows, dtype=gram.dtype) + jnp.tril(gram * strength[..., :, None], -1)
    right_side = strength[..., None] * jnp.concatenate([key_rows, value_rows], axis=-1)
    solved = lax.linalg.triangular_solve(system, right_side, left_side=True, lower=True, unit_diagonal=True)
    w_rows = solved[..., :DK]
    u_rows = solved[..., DK:]
    token_pos = jnp.arange(GROUP)[:, None]
    row_pos = jnp.arange(block_rows)[None, :]
    visible = (row_pos <= slot_count * token_pos + slot_count - 1).astype(gram.dtype)
    scores = jnp.einsum('nhtd,nhcd->nhtc', queries, key_rows, precision=highest) * visible
    mapped_query = queries - jnp.einsum('nhtc,nhcd->nhtd', scores, w_rows, precision=highest)
    local_out = jnp.einsum('nhtc,nhce->nhte', scores, u_rows, precision=highest)
    transition = jnp.eye(DK, dtype=gram.dtype) - jnp.einsum('nhcd,nhce->nhde', key_rows, w_rows, precision=highest)
    written = jnp.einsum('nhcd,nhce->nhde', key_rows, u_rows, precision=highest)
    return (mapped_query, local_out, transition, written)

def state_pass(terms, start_state):

    def advance(current, block_terms):
        mapped_query, local_out, transition, written = block_terms
        out_rows = jnp.einsum('htd,hde->hte', mapped_query, current, precision=highest) + local_out
        return (jnp.einsum('hde,hef->hdf', transition, current, precision=highest) + written, out_rows)
    return lax.scan(advance, start_state, terms)

def finish(outs, gain):
    block_count, head_count, group_len, value_size = outs.shape
    merged = outs.transpose(0, 2, 1, 3).reshape(block_count * group_len, head_count, value_size)
    scale = lax.rsqrt(lax.optimization_barrier(jnp.mean(merged * merged, axis=-1, keepdims=True)) + epsilon)
    normed = merged * scale * gain.reshape(head_count, value_size)
    return normed.reshape(block_count * group_len, head_count * value_size)

def reference(query_in, key_in, value_in, beta_logit, query_conv, key_conv, value_conv, norm_gain, out_weight, grad_out):
    rim_len = KW - 1
    edge_query = jnp.zeros((rim_len, H * DK), jnp.float32)
    edge_key = jnp.zeros((rim_len, NH, H * DK), jnp.float32)
    edge_value = jnp.zeros((rim_len, NH, H * DV), jnp.float32)

    def forward(query_raw, key_raw, value_raw, beta_raw):
        terms = prepare(query_raw, key_raw, value_raw, beta_raw, edge_query, edge_key, edge_value, query_conv, key_conv, value_conv)
        final, outs = state_pass(terms, jnp.zeros((H, DK, DV), jnp.float32))
        return finish(outs, norm_gain)
    normed, pull = jax.vjp(forward, query_in.astype(jnp.float32), key_in.astype(jnp.float32), value_in.astype(jnp.float32), beta_logit)
    normed_bf = normed.astype(jnp.bfloat16)
    layer_out = jnp.dot(normed_bf.astype(jnp.float32), out_weight.astype(jnp.float32), preferred_element_type=jnp.float32).astype(jnp.bfloat16)
    grad_normed = jnp.dot(grad_out.astype(jnp.float32), out_weight.T.astype(jnp.float32), preferred_element_type=jnp.float32).astype(jnp.bfloat16)
    grad_normed = lax.optimization_barrier(grad_normed).astype(jnp.float32)
    grads = pull(grad_normed)
    return (layer_out, grads[0], grads[1], grads[2], grads[3])
```

```python
import functools

import jax
import jax.numpy as jnp
from jax import lax
from jax.experimental import pallas as pl
from jax.experimental.pallas import tpu as pltpu
from jax.sharding import PartitionSpec as P

HEAD = 128
TAPS = 4
RIM = TAPS - 1
EPS = 1e-06
F32 = jnp.float32
BF16 = jnp.bfloat16

ROWS_COLS = (((1,), (0,)), ((), ()))
ROWS_ROWS = (((1,), (1,)), ((), ()))
COLS_COLS = (((0,), (0,)), ((), ()))


def two(x):
    high = x.astype(BF16)
    return high, (x - high.astype(F32)).astype(BF16)


def one(x):
    return (x.astype(BF16),)


def mm(left, right, dims=ROWS_COLS):
    total = None
    for i, a in enumerate(left):
        for j, b in enumerate(right):
            if i + j < 2:
                part = lax.dot_general(a, b, dims, preferred_element_type=F32)
                total = part if total is None else total + part
    return total


def token_order(rows, cols):
    tokens = rows[0]
    r = lax.broadcasted_iota(jnp.int32, (rows[1], cols), 0)
    c = lax.broadcasted_iota(jnp.int32, (rows[1], cols), 1)
    return r % tokens, r // tokens, c % tokens, c // tokens


def before(tokens, slots):
    rt, rj, ct, cj = token_order((tokens, tokens * slots), tokens * slots)
    return slots * ct + cj < slots * rt + rj


def level_pairs(tokens, slots, level):
    rt, rj, ct, cj = token_order((tokens, tokens * slots), tokens * slots)
    if level < 0:
        return (rt == ct) & (cj < rj)
    return ((rt >> (level + 1)) == (ct >> (level + 1))) & (((rt >> level) & 1) == 1) & (((ct >> level) & 1) == 0)


def visible(tokens, slots):
    rt, _, ct, _ = token_order((tokens, tokens), tokens * slots)
    return ct <= rt


def conv_rows(x, tail, weight, pad):
    tokens = x.shape[0]
    pad[pl.ds(8 - RIM, RIM), :] = tail
    pad[pl.ds(8, tokens), :] = x
    total = None
    for i in range(TAPS):
        part = weight[i : i + 1] * pad[pl.ds(8 - RIM + i, tokens), :]
        total = part if total is None else total + part
    return total


def conv_back(grad, weight, pad):
    tokens = grad.shape[0]
    pad[pl.ds(0, 8), :] = jnp.zeros((8, HEAD), F32)
    pad[pl.ds(8, tokens), :] = grad
    pad[pl.ds(8 + tokens, 8), :] = jnp.zeros((8, HEAD), F32)
    inner, rim = None, None
    for i in range(TAPS):
        part = weight[i : i + 1] * pad[pl.ds(8 + RIM - i, tokens), :]
        edge = weight[i : i + 1] * pad[pl.ds(RIM - i, 8), :]
        inner = part if inner is None else inner + part
        rim = edge if rim is None else rim + edge
    return inner, rim


def sigmoid(x):
    return 1.0 / (1.0 + jnp.exp(-x))


def unit(values):
    scale = lax.rsqrt(jnp.sum(values * values, axis=-1, keepdims=True) + EPS)
    return values * scale, scale


def beta_rows(tile, slots):
    return [tile[3 * j : 3 * j + 1] + tile[3 * j + 1 : 3 * j + 2] + tile[3 * j + 2 : 3 * j + 3] for j in range(slots)]


def column(rows):
    tokens = rows[0].shape[1]
    eye = (
        lax.broadcasted_iota(jnp.int32, (tokens, tokens), 0) == lax.broadcasted_iota(jnp.int32, (tokens, tokens), 1)
    )
    return jnp.concatenate([jnp.sum(jnp.where(eye, row, 0.0), axis=1, keepdims=True) for row in rows], axis=0)


def load_kv(ref, n, tokens, slots):
    xs = [ref[n, pl.ds(a * tokens, tokens), :].astype(F32) for a in range(2 * slots)]
    base = 2 * slots * tokens
    betas = beta_rows(ref[n, pl.ds(base, 16), :].astype(F32), slots)
    tails = ref[n, pl.ds(base + 16, 16), :].astype(F32)
    return xs, betas, [tails[4 * a + 1 : 4 * a + 4] for a in range(2 * slots)]


def tap_rows(wts, slots, kind, slot):
    if kind == 0:
        return wts[0:TAPS]
    first = TAPS + (kind - 1) * TAPS * slots
    return jnp.concatenate([wts[first + i * slots + slot : first + i * slots + slot + 1] for i in range(TAPS)], axis=0)


def keys_kernel(per, tokens, slots, hid, kv_ref, wts_ref, kn_ref, wu_ref, ti_ref, a_ref, mc_ref, end_ref, pad, carry):
    step = pl.program_id(0)
    rows = tokens * slots
    wts = wts_ref[...]
    ir = lax.broadcasted_iota(jnp.int32, (HEAD, 2 * HEAD), 0)
    ic = lax.broadcasted_iota(jnp.int32, (HEAD, 2 * HEAD), 1)

    @pl.when(step == 0)
    def _():
        carry[...] = (ir == ic).astype(F32)

    keys, rights, systems = [], [], []
    order = before(tokens, slots)
    for n in range(per):
        xs, betas, tails = load_kv(kv_ref, n, tokens, slots)
        parts = []
        for a in range(2 * slots):
            kind, slot = 1 + a // slots, a % slots
            s = conv_rows(xs[a], tails[a], tap_rows(wts, slots, kind, slot), pad.at[n * 2 * slots + a])
            c = s * sigmoid(s)
            parts.append(unit(c)[0] if kind == 1 else c)
        k = jnp.concatenate(parts[:slots], axis=0)
        v = jnp.concatenate(parts[slots:], axis=0)
        strength = 2.0 * sigmoid(column(betas))
        kn_ref[n] = k
        k2 = two(k)
        gram = mm(k2, k2, ROWS_ROWS)
        systems.append(two(jnp.where(order, gram * strength, 0.0)))
        rights.append(two(strength * jnp.concatenate([k, v], axis=1)))
        keys.append(k2)
    eye = (
        lax.broadcasted_iota(jnp.int32, (rows, rows), 0) == lax.broadcasted_iota(jnp.int32, (rows, rows), 1)
    ).astype(F32)
    zero = jnp.zeros((rows, rows), BF16)
    pairs = level_pairs(tokens, slots, -1)
    inverse = [
        eye - jnp.where(pairs, system[0].astype(F32) + system[1].astype(F32), 0.0) for system in systems
    ]
    level = 0
    while (1 << level) < tokens:
        pairs = level_pairs(tokens, slots, level)
        split = [two(x) for x in inverse]
        crossed = [
            mm(tuple(jnp.where(pairs, part, zero) for part in system), x) for system, x in zip(systems, split)
        ]
        inverse = [x - mm(s, two(y)) for x, s, y in zip(inverse, split, crossed)]
        level += 1
    wus = []
    for n in range(per):
        ti_ref[n] = inverse[n]
        wus.append(mm(two(inverse[n]), rights[n]))
        wu_ref[n] = wus[n]
    maps = [mm(keys[n], two(wus[n]), COLS_COLS) for n in range(per)]
    state = carry[...]
    for n in range(per):
        mc_ref[n] = state
        a = (ir == ic)[:, :HEAD].astype(F32) - maps[n][:, :HEAD]
        a_ref[n] = a
        moved = mm(two(a), two(state))
        state = jnp.where(ic < HEAD, moved, moved + maps[n])
    carry[...] = state
    end_ref[...] = state


def queries_kernel(per, tokens, slots, hid, qg_ref, wts_ref, kn_ref, wu_ref, q_ref, sc_ref, qm_ref, ol_ref, pad):
    wts = wts_ref[...]
    seen = visible(tokens, slots)
    for n in range(per):
        x = qg_ref[n, pl.ds(0, tokens), :].astype(F32)
        tail = qg_ref[n, pl.ds(2 * tokens, 16), :].astype(F32)[1:4]
        s = conv_rows(x, tail, tap_rows(wts, slots, 0, 0), pad.at[n])
        q = unit(s * sigmoid(s))[0]
        scores = jnp.where(seen, mm(two(q), two(kn_ref[n]), ROWS_ROWS), 0.0)
        mapped = mm(two(scores), two(wu_ref[n]))
        q_ref[n] = q
        sc_ref[n] = scores
        qm_ref[n] = q - mapped[:, :HEAD]
        ol_ref[n] = mapped[:, HEAD:]


def outs_kernel(
    count, tokens, slots, hid, qg_ref, wts_ref, start_ref, mc_ref, qm_ref, ol_ref, a_ref,
    nm_ref, dr_ref, st_ref, mb_ref, end_ref,
):
    gain = wts_ref[...][TAPS + 2 * TAPS * slots : TAPS + 2 * TAPS * slots + 1]
    start = two(start_ref[...])
    states = [
        mm(two(mc_ref[n, :, pl.ds(0, HEAD)]), start) + mc_ref[n, :, pl.ds(HEAD, HEAD)] for n in range(count)
    ]
    mapped = [two(qm_ref[n]) for n in range(count)]
    raws = [mm(mapped[n], two(states[n])) + ol_ref[n] for n in range(count)]
    local = []
    for n in range(count):
        st_ref[n] = states[n]
        raw = raws[n]
        scale = lax.rsqrt(jnp.mean(raw * raw, axis=-1, keepdims=True) + EPS)
        hat = raw * scale
        nm_ref[n] = (hat * gain).astype(BF16)
        dn = qg_ref[n, pl.ds(tokens, tokens), :].astype(F32) * gain
        dr = scale * (dn - hat * jnp.mean(dn * hat, axis=-1, keepdims=True))
        dr_ref[n] = dr
        local.append(mm(mapped[n], two(dr), COLS_COLS))
    ir = lax.broadcasted_iota(jnp.int32, (HEAD, 2 * HEAD), 0)
    ic = lax.broadcasted_iota(jnp.int32, (HEAD, 2 * HEAD), 1)
    state = (ir == ic).astype(F32)
    for n in range(count - 1, -1, -1):
        mb_ref[n] = state
        moved = mm(two(a_ref[n]), two(state), COLS_COLS)
        state = moved + jnp.concatenate([jnp.zeros((HEAD, HEAD), F32), local[n]], axis=1)
    end_ref[...] = state


def query_grads_kernel(
    per, tokens, slots, hid, qg_ref, wts_ref, kn_ref, wu_ref, q_ref, sc_ref, dr_ref, st_ref,
    d_ref, dk_ref, dd_ref, gq_ref, pad,
):
    wts = wts_ref[...]
    seen = visible(tokens, slots)
    for n in range(per):
        state, dr, k2 = two(st_ref[n]), two(dr_ref[n]), two(kn_ref[n])
        d = wu_ref[n, :, pl.ds(HEAD, HEAD)] - mm(two(wu_ref[n, :, pl.ds(0, HEAD)]), state)
        d_ref[n] = d
        ds = two(jnp.where(seen, mm(dr, two(d), ROWS_ROWS), 0.0))
        dq = mm(dr, state, ROWS_ROWS) + mm(ds, k2)
        dk_ref[n] = mm(ds, two(q_ref[n]), COLS_COLS)
        dd_ref[n] = mm(two(sc_ref[n]), dr, COLS_COLS)
        x = qg_ref[n, pl.ds(0, tokens), :].astype(F32)
        tail = qg_ref[n, pl.ds(2 * tokens, 16), :].astype(F32)[1:4]
        taps = tap_rows(wts, slots, 0, 0)
        s = conv_rows(x, tail, taps, pad.at[n])
        sg = sigmoid(s)
        q, scale = unit(s * sg)
        dc = scale * (dq - q * jnp.sum(q * dq, axis=-1, keepdims=True))
        inner, rim = conv_back(dc * sg * (1.0 + s * (1.0 - sg)), taps, pad.at[n])
        gq_ref[n, pl.ds(0, tokens), :] = inner.astype(BF16)
        gq_ref[n, pl.ds(tokens, 16), :] = jnp.concatenate([rim, jnp.zeros((8, HEAD), F32)], axis=0).astype(BF16)


def key_grads_kernel(
    per, tokens, slots, hid, kv_ref, wts_ref, end_ref, mb_ref, kn_ref, ti_ref, d_ref, dk_ref, dd_ref, st_ref,
    out_ref, pad,
):
    wts = wts_ref[...]
    order = before(tokens, slots)
    end = two(end_ref[...])
    rows = tokens * slots
    for n in range(per):
        g = mm(two(mb_ref[n, :, pl.ds(0, HEAD)]), end) + mb_ref[n, :, pl.ds(HEAD, HEAD)]
        g2, k, d = two(g), kn_ref[n], d_ref[n]
        k2, d2 = two(k), two(d)
        dd = dd_ref[n] + mm(k2, g2)
        y = mm(two(ti_ref[n]), two(dd), COLS_COLS)
        xs, betas, tails = load_kv(kv_ref, n, tokens, slots)
        strength = 2.0 * sigmoid(column(betas))
        de = strength * y
        de2 = two(de)
        dgram = jnp.where(order, mm(de2, d2, ROWS_ROWS), 0.0)
        dk = dk_ref[n] + mm(d2, g2, ROWS_ROWS) - mm(de2, two(st_ref[n]), ROWS_ROWS)
        dk = dk - mm(two(dgram + dgram.T), k2)
        ones = (jnp.ones((8, HEAD), BF16),)
        dot = mm(ones, two(y * d), ROWS_ROWS)
        base = 2 * slots * tokens
        marks = []
        for j in range(slots):
            gb = dot[0:1, j * tokens : (j + 1) * tokens] * sigmoid(-betas[j])
            high = gb.astype(BF16).astype(F32)
            marks += [high, gb - high]
        marks.append(jnp.zeros((16 - 2 * slots, tokens), F32))
        out_ref[n, pl.ds(base, 16), :] = jnp.concatenate(marks, axis=0).astype(BF16)
        rims = []
        for a in range(2 * slots):
            kind, slot = 1 + a // slots, a % slots
            taps = tap_rows(wts, slots, kind, slot)
            s = conv_rows(xs[a], tails[a], taps, pad.at[n])
            sg = sigmoid(s)
            if kind == 1:
                mine = k[slot * tokens : (slot + 1) * tokens]
                c = s * sg
                scale = lax.rsqrt(jnp.sum(c * c, axis=-1, keepdims=True) + EPS)
                part = dk[slot * tokens : (slot + 1) * tokens]
                dc = scale * (part - mine * jnp.sum(mine * part, axis=-1, keepdims=True))
            else:
                dc = de[slot * tokens : (slot + 1) * tokens]
            inner, rim = conv_back(dc * sg * (1.0 + s * (1.0 - sg)), taps, pad.at[n])
            out_ref[n, pl.ds(a * tokens, tokens), :] = inner.astype(BF16)
            rims.append(rim)
        out_ref[n, pl.ds(base + 16, 8 * 2 * slots), :] = jnp.concatenate(rims, axis=0).astype(BF16)


def call(kernel, hid, grid, ins, outs, scratch=(), flops=0):
    def spec(shape, per):
        if per == "weights":
            return pl.BlockSpec((shape[0], HEAD), lambda i, h: (0, h[0]))
        if per is None:
            return pl.BlockSpec(shape, lambda i, h: (0,) * len(shape))
        return pl.BlockSpec((per,) + tuple(shape[1:]), lambda i, h: (i,) + (0,) * (len(shape) - 1))

    moved = sum(a.size * a.dtype.itemsize for a, _ in ins)
    moved += sum(functools.reduce(lambda x, y: x * y, s, 1) * jnp.dtype(d).itemsize for s, d, _ in outs)
    return pl.pallas_call(
        kernel,
        grid_spec=pltpu.PrefetchScalarGridSpec(
            num_scalar_prefetch=1,
            grid=grid,
            in_specs=[spec(a.shape, per) for a, per in ins],
            out_specs=[spec(s, per) for s, _, per in outs],
            scratch_shapes=list(scratch),
        ),
        out_shape=[jax.ShapeDtypeStruct(s, d) for s, d, _ in outs],
        compiler_params=pltpu.CompilerParams(
            dimension_semantics=("arbitrary",) * len(grid), vmem_limit_bytes=48 << 20
        ),
        cost_estimate=pl.CostEstimate(flops=flops, bytes_accessed=moved, transcendentals=0),
    )(hid, *[a for a, _ in ins])


def shards(
    query_in,
    key_in,
    value_in,
    beta_logit,
    query_conv,
    key_conv,
    value_conv,
    norm_gain,
    out_weight,
    grad_out,
):
    tokens, slots = key_in.shape[0], key_in.shape[1]
    width = query_in.shape[1]
    heads = width // HEAD
    shard_count = lax.axis_size("ctx")
    place = lax.axis_index("ctx")
    groups = shard_count // heads
    group_lists = [[b * heads + i for i in range(heads)] for b in range(groups)]
    rows = tokens * slots
    hid = (place % heads).astype(jnp.int32).reshape(1)

    def exchange(x):
        return lax.all_to_all(x, "ctx", 0, 0, axis_index_groups=group_lists, tiled=True)

    def by_head(x):
        return x.reshape(x.shape[0], heads, HEAD).transpose(1, 0, 2)

    tail = jnp.concatenate(
        [query_in[-RIM:].reshape(RIM, 1, width), key_in[-RIM:], value_in[-RIM:]], axis=1
    )
    tail = lax.ppermute(tail, "ctx", [(i, i + 1) for i in range(shard_count - 1)])
    tail = tail.reshape(RIM, 1 + 2 * slots, heads, HEAD).transpose(2, 1, 0, 3)
    tail = jnp.pad(tail, ((0, 0), (0, 0), (1, 0), (0, 0)))
    high = lax.reduce_precision(beta_logit, 8, 7)
    rest = beta_logit - high
    middle = lax.reduce_precision(rest, 8, 7)
    betas = jnp.stack([high, middle, rest - middle], axis=2)
    betas = betas.transpose(3, 1, 2, 0).reshape(heads, 3 * slots, tokens).astype(BF16)
    betas = jnp.pad(betas, ((0, 0), (0, 16 - 3 * slots), (0, 0)))
    kv_tail = jnp.pad(tail[:, 1:].reshape(heads, 8 * slots, HEAD), ((0, 0), (0, 16 - 8 * slots), (0, 0)))
    packed_kv = jnp.concatenate(
        [by_head(key_in[:, j]) for j in range(slots)]
        + [by_head(value_in[:, j]) for j in range(slots)]
        + [betas, kv_tail],
        axis=1,
    )
    kv = exchange(packed_kv)
    grad_normed = jnp.dot(grad_out, out_weight.T, preferred_element_type=F32).astype(BF16)
    q_tail = jnp.pad(tail[:, 0], ((0, 0), (0, 12), (0, 0)))
    qg = exchange(jnp.concatenate([by_head(query_in), by_head(grad_normed), q_tail], axis=1))

    wts = jnp.concatenate(
        [
            query_conv,
            key_conv.reshape(TAPS * slots, width),
            value_conv.reshape(TAPS * slots, width),
            norm_gain.reshape(1, width),
            jnp.zeros((-(1 + TAPS + 2 * TAPS * slots) % 8, width), F32),
        ],
        axis=0,
    )
    g = heads
    per = 2 if g % 2 == 0 else 1
    grid = (g // per,)
    unit_flops = 2 * rows * rows * rows * g
    pads = pltpu.VMEM((per * 2 * slots, tokens + 16, HEAD), F32)
    kn, wu, ti, amap, mc, end = call(
        functools.partial(keys_kernel, per, tokens, slots),
        hid,
        grid,
        [(kv, per), (wts, "weights")],
        [
            ((g, rows, HEAD), F32, per),
            ((g, rows, 2 * HEAD), F32, per),
            ((g, rows, rows), F32, per),
            ((g, HEAD, HEAD), F32, per),
            ((g, HEAD, 2 * HEAD), F32, per),
            ((HEAD, 2 * HEAD), F32, None),
        ],
        [pads, pltpu.VMEM((HEAD, 2 * HEAD), F32)],
        flops=48 * unit_flops,
    )

    def across(last, towards):
        if groups == 1:
            return jnp.zeros((HEAD, HEAD), F32)
        if groups == 2:
            moves = [(i, i + towards * heads) for i in range(shard_count) if 0 <= i + towards * heads < shard_count]
            return lax.ppermute(last[:, HEAD:], "ctx", moves)
        every = lax.all_gather(last, "ctx")
        group, head = place // heads, place % heads
        ahead = group if towards > 0 else groups - 1 - group

        def advance(i, state):
            source = i if towards > 0 else groups - 1 - i
            item = lax.dynamic_index_in_dim(every, source * heads + head, 0, False)
            return jnp.dot(item[:, :HEAD], state, precision=lax.Precision.HIGHEST) + item[:, HEAD:]

        return lax.fori_loop(0, ahead, advance, jnp.zeros((HEAD, HEAD), F32))

    start = across(end, 1)
    small_pads = pltpu.VMEM((per, tokens + 16, HEAD), F32)
    q, sc, qm, ol = call(
        functools.partial(queries_kernel, per, tokens, slots),
        hid,
        grid,
        [(qg, per), (wts, "weights"), (kn, per), (wu, per)],
        [
            ((g, tokens, HEAD), F32, per),
            ((g, tokens, rows), F32, per),
            ((g, tokens, HEAD), F32, per),
            ((g, tokens, HEAD), F32, per),
        ],
        [small_pads],
        flops=3 * unit_flops,
    )
    normed, dr, st, mb, back_end = call(
        functools.partial(outs_kernel, g, tokens, slots),
        hid,
        (1,),
        [(qg, None), (wts, "weights"), (start, None), (mc, None), (qm, None), (ol, None), (amap, None)],
        [
            ((g, tokens, HEAD), BF16, None),
            ((g, tokens, HEAD), F32, None),
            ((g, HEAD, HEAD), F32, None),
            ((g, HEAD, 2 * HEAD), F32, None),
            ((HEAD, 2 * HEAD), F32, None),
        ],
        flops=2 * unit_flops,
    )
    finish = across(back_end, -1)
    d, dk, dd, gq = call(
        functools.partial(query_grads_kernel, per, tokens, slots),
        hid,
        grid,
        [(qg, per), (wts, "weights"), (kn, per), (wu, per), (q, per), (sc, per), (dr, per), (st, per)],
        [
            ((g, rows, HEAD), F32, per),
            ((g, rows, HEAD), F32, per),
            ((g, rows, HEAD), F32, per),
            ((g, tokens + 16, HEAD), BF16, per),
        ],
        [small_pads],
        flops=4 * unit_flops,
    )
    nq = exchange(jnp.concatenate([normed, gq], axis=1))
    normed_bf = nq[:, :tokens].transpose(1, 0, 2).reshape(tokens, width)
    partial = jnp.dot(normed_bf, out_weight, preferred_element_type=F32)
    head_count = lax.axis_size("head")
    if head_count == 2:
        half = tokens // 2
        mine = lax.axis_index("head")
        pieces = partial.reshape(2, half, partial.shape[1])
        kept = lax.dynamic_index_in_dim(pieces, mine, 0, False)
        sent = lax.dynamic_index_in_dim(pieces, 1 - mine, 0, False).astype(BF16)
        layer_out = (kept + lax.ppermute(sent, "head", [(0, 1), (1, 0)]).astype(F32)).astype(BF16)
    else:
        layer_out = lax.psum_scatter(partial.astype(BF16), "head", scatter_dimension=0, tiled=True)

    block = 2 * slots * tokens + 16 + 16 * slots
    (gkv,) = call(
        functools.partial(key_grads_kernel, per, tokens, slots),
        hid,
        grid,
        [
            (kv, per), (wts, "weights"), (finish, None), (mb, per), (kn, per), (ti, per), (d, per), (dk, per),
            (dd, per), (st, per),
        ],
        [((g, block, HEAD), BF16, per)],
        [small_pads],
        flops=8 * unit_flops,
    )
    grads = exchange(gkv)

    base = 2 * slots * tokens + 16
    rims = jnp.concatenate(
        [nq[:, 2 * tokens + 8 - RIM : 2 * tokens + 8]]
        + [grads[:, base + 8 * a + 8 - RIM : base + 8 * a + 8] for a in range(2 * slots)],
        axis=1,
    )
    rims = lax.ppermute(rims, "ctx", [(i, i - 1) for i in range(1, shard_count)]).astype(F32)

    def laid(block, a):
        edge = jnp.pad(rims[:, a * RIM : (a + 1) * RIM], ((0, 0), (tokens - RIM, 0), (0, 0)))
        return (block.astype(F32) + edge).transpose(1, 0, 2).reshape(tokens, width)

    grad_query = laid(nq[:, tokens : 2 * tokens], 0)
    parts = [laid(grads[:, a * tokens : (a + 1) * tokens], 1 + a) for a in range(2 * slots)]
    grad_key = jnp.stack(parts[:slots], axis=1)
    grad_value = jnp.stack(parts[slots:], axis=1)
    marks = grads[:, 2 * slots * tokens : 2 * slots * tokens + 2 * slots].astype(F32)
    marks = marks.reshape(heads, slots, 2, tokens).sum(axis=2)
    grad_beta = marks.transpose(2, 1, 0)
    return (layer_out, grad_query, grad_key, grad_value, grad_beta)


def solution(mesh):
    placed = (
        P("ctx", "head"),
        P("ctx", None, "head"),
        P("ctx", None, "head"),
        P("ctx", None, "head"),
        P(None, "head"),
        P(None, None, "head"),
        P(None, None, "head"),
        P("head"),
        P("head", None),
        P("ctx", None),
    )
    return jax.shard_map(
        shards,
        mesh=mesh,
        in_specs=placed,
        out_specs=(
            P(("ctx", "head"), None),
            P("ctx", "head"),
            P("ctx", None, "head"),
            P("ctx", None, "head"),
            P("ctx", None, "head"),
        ),
        check_vma=False,
    )
```

```python
import functools

import jax
import jax.numpy as jnp
from jax import lax
from jax.experimental import pallas as pl
from jax.experimental.pallas import tpu as pltpu
from jax.sharding import PartitionSpec as P

HEAD = 128
TAPS = 4
RIM = TAPS - 1
EDGE = 16
EPS = 1e-06
F32 = jnp.float32
BF16 = jnp.bfloat16

ROWS_COLS = (((1,), (0,)), ((), ()))
ROWS_ROWS = (((1,), (1,)), ((), ()))
COLS_COLS = (((0,), (0,)), ((), ()))


def two(x):
    high = x.astype(BF16)
    return high, (x - high.astype(F32)).astype(BF16)


def dot(a, b, dims):
    return lax.dot_general(a, b, dims, preferred_element_type=F32)


def mm(left, right, dims=ROWS_COLS):
    (ah, al), (bh, bl) = left, right
    ka, kb = dims[0][0][0], dims[0][1][0]
    nb = 1 - kb
    depth, cols = ah.shape[ka], bh.shape[nb]
    if depth <= HEAD:
        a = jnp.concatenate([ah, al], axis=ka)
        high, low = jnp.concatenate([bh, bh], axis=kb), jnp.concatenate([bl, bl], axis=kb)
        if cols <= HEAD:
            out = dot(a, jnp.concatenate([high, low], axis=nb), dims)
            return out[:, :cols] + out[:, cols:]
        return dot(a, high, dims) + dot(a, low, dims)
    if cols <= HEAD:
        out = dot(ah, jnp.concatenate([bh, bl], axis=nb), dims)
        return out[:, :cols] + out[:, cols:] + dot(al, bh, dims)
    return dot(ah, bh, dims) + dot(ah, bl, dims) + dot(al, bh, dims)


def grid_of(rows, cols):
    return lax.broadcasted_iota(jnp.int32, (rows, cols), 0), lax.broadcasted_iota(jnp.int32, (rows, cols), 1)


def before(rows):
    r, c = grid_of(rows, rows)
    return c < r


def level_pairs(rows, level):
    r, c = grid_of(rows, rows)
    return ((r >> (level + 1)) == (c >> (level + 1))) & (((r >> level) & 1) == 1) & (((c >> level) & 1) == 0)


def visible(tokens, slots):
    t, c = grid_of(tokens, tokens * slots)
    return c < slots * (t + 1)


def times(pattern, x):
    if pattern.shape[0] == 1:
        return pattern * x
    return (x.reshape(-1, 8, HEAD) * pattern[None]).reshape(x.shape)


def conv_rows(x, edge, taps, pad, stride):
    rows = x.shape[0]
    pad[pl.ds(0, EDGE), :] = edge
    pad[pl.ds(EDGE, rows), :] = x
    total = None
    for i in range(TAPS):
        part = times(taps[i], pad[pl.ds(EDGE - stride * (RIM - i), rows), :])
        total = part if total is None else total + part
    return total


def conv_back(grad, taps, pad, stride):
    rows = grad.shape[0]
    pad[pl.ds(8, 8), :] = jnp.zeros((8, HEAD), F32)
    pad[pl.ds(EDGE, rows), :] = grad
    pad[pl.ds(EDGE + rows, 8), :] = jnp.zeros((8, HEAD), F32)
    inner, rim = None, None
    for i in range(TAPS):
        part = times(taps[i], pad[pl.ds(EDGE + stride * (RIM - i), rows), :])
        edge = times(taps[i], pad[pl.ds(8 + stride * (RIM - i), 8), :])
        inner = part if inner is None else inner + part
        rim = edge if rim is None else rim + edge
    return inner, rim


def sigmoid(x):
    return 1.0 / (1.0 + jnp.exp(-x))


def unit(values):
    scale = lax.rsqrt(jnp.sum(values * values, axis=-1, keepdims=True) + EPS)
    return values * scale, scale


def beta_rows(tile, slots):
    return [tile[3 * j : 3 * j + 1] + tile[3 * j + 1 : 3 * j + 2] + tile[3 * j + 2 : 3 * j + 3] for j in range(slots)]


def places(tokens, slots, j):
    r, t = grid_of(tokens * slots, tokens)
    return r == slots * t + j


def column(rows, tokens, slots):
    spread = jnp.zeros((tokens * slots, tokens), F32)
    for j in range(slots):
        spread = jnp.where(places(tokens, slots, j), rows[j], spread)
    return jnp.sum(spread, axis=1, keepdims=True)


def slot_taps(wts, kind):
    return [wts[8 * (TAPS * kind + i) : 8 * (TAPS * kind + i + 1)] for i in range(TAPS)]


def query_taps(wts):
    return [wts[16 * TAPS + i : 16 * TAPS + i + 1] for i in range(TAPS)]


def gain_row(wts):
    return wts[17 * TAPS : 17 * TAPS + 1]


def edges(ref, first, rows, per, tail, halo):
    @pl.when(pl.program_id(0) == 0)
    def _():
        halo[...] = tail

    found = [halo[...]] + [ref[n, pl.ds(first + rows - EDGE, EDGE), :].astype(F32) for n in range(per - 1)]
    halo[...] = ref[per - 1, pl.ds(first + rows - EDGE, EDGE), :].astype(F32)
    return found


def inverse_kernel(per, tokens, slots, hid, kb_ref, tail_ref, wts_ref, kn_ref, ti_ref, pad, halo):
    rows = tokens * slots
    taps = slot_taps(wts_ref[...], 0)
    tops = edges(kb_ref, 0, rows, per, tail_ref[pl.ds(0, EDGE), :].astype(F32), halo)
    order = before(rows)
    blocks = rows // HEAD
    grams = []
    for n in range(per):
        s = conv_rows(kb_ref[n, pl.ds(0, rows), :].astype(F32), tops[n], taps, pad.at[n], slots)
        k = unit(s * sigmoid(s))[0]
        kn_ref[n] = k
        betas = beta_rows(kb_ref[n, pl.ds(rows, EDGE), :].astype(F32), slots)
        strength = 2.0 * sigmoid(column(betas, tokens, slots))
        k2 = two(k)
        grams.append(jnp.where(order, mm(k2, k2, ROWS_ROWS) * strength, 0.0))
    r, c = grid_of(HEAD, HEAD)
    eye = (r == c).astype(F32)
    zero = jnp.zeros((HEAD, HEAD), BF16)
    diagonal = [
        gram[b * HEAD : (b + 1) * HEAD, b * HEAD : (b + 1) * HEAD] for gram in grams for b in range(blocks)
    ]
    systems = [two(x) for x in diagonal]
    pairs = level_pairs(HEAD, 0)
    inverse = [eye - jnp.where(pairs, x, 0.0) for x in diagonal]
    level = 1
    while (1 << level) < HEAD:
        pairs = level_pairs(HEAD, level)
        split = [two(x) for x in inverse]
        crossed = [mm(tuple(jnp.where(pairs, p, zero) for p in s), x) for s, x in zip(systems, split)]
        inverse = [x - mm(s, two(y)) for x, s, y in zip(inverse, split, crossed)]
        level += 1
    for n in range(per):
        done = inverse[n * blocks : (n + 1) * blocks]
        size = HEAD
        while len(done) > 1:
            merged = []
            for b in range(0, len(done), 2):
                top, low = done[b], done[b + 1]
                cross = grams[n][(b + 1) * size : (b + 2) * size, b * size : (b + 1) * size]
                cross = mm(two(low), two(mm(two(cross), two(top))))
                merged.append(
                    jnp.concatenate(
                        [
                            jnp.concatenate([top, jnp.zeros_like(top)], axis=1),
                            jnp.concatenate([-cross, low], axis=1),
                        ],
                        axis=0,
                    )
                )
            done = merged
            size *= 2
        ti_ref[n] = done[0]


def maps_kernel(
    per, tokens, slots, hid, vq_ref, beta_ref, tail_ref, wts_ref, kn_ref, ti_ref,
    wu_ref, a_ref, mc_ref, end_ref, pad, halo, carry,
):
    rows = tokens * slots
    taps = slot_taps(wts_ref[...], 1)
    ir, ic = grid_of(HEAD, 2 * HEAD)

    @pl.when(pl.program_id(0) == 0)
    def _():
        carry[...] = (ir == ic).astype(F32)

    tops = edges(vq_ref, 0, rows, per, tail_ref[pl.ds(EDGE, EDGE), :].astype(F32), halo)
    maps = []
    for n in range(per):
        s = conv_rows(vq_ref[n, pl.ds(0, rows), :].astype(F32), tops[n], taps, pad.at[n], slots)
        v = s * sigmoid(s)
        betas = beta_rows(beta_ref[n].astype(F32), slots)
        strength = 2.0 * sigmoid(column(betas, tokens, slots))
        k = kn_ref[n]
        wu = mm(two(ti_ref[n]), two(strength * jnp.concatenate([k, v], axis=1)))
        wu_ref[n] = wu
        maps.append(mm(two(k), two(wu), COLS_COLS))
    state = carry[...]
    for n in range(per):
        mc_ref[n] = state
        a = (ir == ic)[:, :HEAD].astype(F32) - maps[n][:, :HEAD]
        a_ref[n] = a
        moved = mm(two(a), two(state))
        state = jnp.where(ic < HEAD, moved, moved + maps[n])
    carry[...] = state
    end_ref[...] = state


def queries_kernel(
    per, tokens, slots, hid, vq_ref, tail_ref, wts_ref, kn_ref, wu_ref, q_ref, sc_ref, qm_ref, ol_ref, pad, halo
):
    rows = tokens * slots
    taps = query_taps(wts_ref[...])
    tops = edges(vq_ref, rows, tokens, per, tail_ref[pl.ds(2 * EDGE, EDGE), :].astype(F32), halo)
    seen = visible(tokens, slots)
    for n in range(per):
        s = conv_rows(vq_ref[n, pl.ds(rows, tokens), :].astype(F32), tops[n], taps, pad.at[n], 1)
        q = unit(s * sigmoid(s))[0]
        scores = jnp.where(seen, mm(two(q), two(kn_ref[n]), ROWS_ROWS), 0.0)
        mapped = mm(two(scores), two(wu_ref[n]))
        q_ref[n] = q
        sc_ref[n] = scores
        qm_ref[n] = q - mapped[:, :HEAD]
        ol_ref[n] = mapped[:, HEAD:]


def outs_kernel(
    count, tokens, slots, hid, vq_ref, wts_ref, start_ref, mc_ref, qm_ref, ol_ref, a_ref,
    nm_ref, dr_ref, st_ref, mb_ref, end_ref,
):
    rows = tokens * slots
    gain = gain_row(wts_ref[...])
    start = two(start_ref[...])
    states = [
        mm(two(mc_ref[n, :, pl.ds(0, HEAD)]), start) + mc_ref[n, :, pl.ds(HEAD, HEAD)] for n in range(count)
    ]
    mapped = [two(qm_ref[n]) for n in range(count)]
    raws = [mm(mapped[n], two(states[n])) + ol_ref[n] for n in range(count)]
    local = []
    for n in range(count):
        st_ref[n] = states[n]
        raw = raws[n]
        scale = lax.rsqrt(jnp.mean(raw * raw, axis=-1, keepdims=True) + EPS)
        hat = raw * scale
        nm_ref[n] = (hat * gain).astype(BF16)
        dn = vq_ref[n, pl.ds(rows + tokens, tokens), :].astype(F32) * gain
        dr = scale * (dn - hat * jnp.mean(dn * hat, axis=-1, keepdims=True))
        dr_ref[n] = dr
        local.append(mm(mapped[n], two(dr), COLS_COLS))
    ir, ic = grid_of(HEAD, 2 * HEAD)
    state = (ir == ic).astype(F32)
    for n in range(count - 1, -1, -1):
        mb_ref[n] = state
        moved = mm(two(a_ref[n]), two(state), COLS_COLS)
        state = moved + jnp.concatenate([jnp.zeros((HEAD, HEAD), F32), local[n]], axis=1)
    end_ref[...] = state


def query_grads_kernel(
    per, tokens, slots, hid, vq_ref, tail_ref, wts_ref, kn_ref, wu_ref, q_ref, sc_ref, dr_ref, st_ref,
    d_ref, dk_ref, dd_ref, gq_ref, pad, halo,
):
    rows = tokens * slots
    taps = query_taps(wts_ref[...])
    tops = edges(vq_ref, rows, tokens, per, tail_ref[pl.ds(2 * EDGE, EDGE), :].astype(F32), halo)
    seen = visible(tokens, slots)
    for n in range(per):
        state, dr, k2 = two(st_ref[n]), two(dr_ref[n]), two(kn_ref[n])
        d = wu_ref[n, :, pl.ds(HEAD, HEAD)] - mm(two(wu_ref[n, :, pl.ds(0, HEAD)]), state)
        d_ref[n] = d
        ds = two(jnp.where(seen, mm(dr, two(d), ROWS_ROWS), 0.0))
        dq = mm(dr, state, ROWS_ROWS) + mm(ds, k2)
        dk_ref[n] = mm(ds, two(q_ref[n]), COLS_COLS)
        dd_ref[n] = mm(two(sc_ref[n]), dr, COLS_COLS)
        s = conv_rows(vq_ref[n, pl.ds(rows, tokens), :].astype(F32), tops[n], taps, pad.at[n], 1)
        sg = sigmoid(s)
        q, scale = unit(s * sg)
        dc = scale * (dq - q * jnp.sum(q * dq, axis=-1, keepdims=True))
        inner, rim = conv_back(dc * sg * (1.0 + s * (1.0 - sg)), taps, pad.at[n], 1)
        gq_ref[n, pl.ds(0, tokens), :] = inner.astype(BF16)
        gq_ref[n, pl.ds(tokens, EDGE), :] = jnp.concatenate([rim, jnp.zeros((8, HEAD), F32)], axis=0).astype(BF16)


def value_grads_kernel(
    per, tokens, slots, hid, vq_ref, beta_ref, tail_ref, wts_ref, end_ref, mb_ref, kn_ref, ti_ref, d_ref, dd_ref,
    g_ref, de_ref, gv_ref, pad, halo,
):
    rows = tokens * slots
    taps = slot_taps(wts_ref[...], 1)
    tops = edges(vq_ref, 0, rows, per, tail_ref[pl.ds(EDGE, EDGE), :].astype(F32), halo)
    end = two(end_ref[...])
    for n in range(per):
        g = mm(two(mb_ref[n, :, pl.ds(0, HEAD)]), end) + mb_ref[n, :, pl.ds(HEAD, HEAD)]
        g_ref[n] = g
        dd = dd_ref[n] + mm(two(kn_ref[n]), two(g))
        y = mm(two(ti_ref[n]), two(dd), COLS_COLS)
        betas = beta_rows(beta_ref[n].astype(F32), slots)
        de = 2.0 * sigmoid(column(betas, tokens, slots)) * y
        de_ref[n] = de
        along = jnp.sum(y * d_ref[n], axis=1, keepdims=True)
        marks = []
        for j in range(slots):
            gb = jnp.sum(jnp.where(places(tokens, slots, j), along, 0.0), axis=0, keepdims=True) * sigmoid(-betas[j])
            high = gb.astype(BF16).astype(F32)
            marks += [high, gb - high]
        marks.append(jnp.zeros((EDGE - 2 * slots, tokens), F32))
        s = conv_rows(vq_ref[n, pl.ds(0, rows), :].astype(F32), tops[n], taps, pad.at[n], slots)
        sg = sigmoid(s)
        inner, rim = conv_back(de * sg * (1.0 + s * (1.0 - sg)), taps, pad.at[n], slots)
        gv_ref[n, pl.ds(0, rows), :] = inner.astype(BF16)
        gv_ref[n, pl.ds(rows, EDGE), :] = jnp.concatenate(marks, axis=0).astype(BF16)
        gv_ref[n, pl.ds(rows + EDGE, EDGE), :] = jnp.concatenate([rim, jnp.zeros((8, HEAD), F32)], axis=0).astype(BF16)


def key_grads_kernel(
    per, tokens, slots, hid, kb_ref, tail_ref, wts_ref, kn_ref, d_ref, dk_ref, de_ref, st_ref, g_ref,
    gk_ref, pad, halo,
):
    rows = tokens * slots
    taps = slot_taps(wts_ref[...], 0)
    tops = edges(kb_ref, 0, rows, per, tail_ref[pl.ds(0, EDGE), :].astype(F32), halo)
    order = before(rows)
    for n in range(per):
        k = kn_ref[n]
        k2, d2, de2 = two(k), two(d_ref[n]), two(de_ref[n])
        dgram = jnp.where(order, mm(de2, d2, ROWS_ROWS), 0.0)
        dk = dk_ref[n] + mm(d2, two(g_ref[n]), ROWS_ROWS) - mm(de2, two(st_ref[n]), ROWS_ROWS)
        dk = dk - mm(two(dgram + dgram.T), k2)
        s = conv_rows(kb_ref[n, pl.ds(0, rows), :].astype(F32), tops[n], taps, pad.at[n], slots)
        sg = sigmoid(s)
        scale = unit(s * sg)[1]
        dc = scale * (dk - k * jnp.sum(k * dk, axis=-1, keepdims=True))
        inner, rim = conv_back(dc * sg * (1.0 + s * (1.0 - sg)), taps, pad.at[n], slots)
        gk_ref[n, pl.ds(0, rows), :] = inner.astype(BF16)
        gk_ref[n, pl.ds(rows, EDGE), :] = jnp.concatenate([rim, jnp.zeros((8, HEAD), F32)], axis=0).astype(BF16)


def call(kernel, hid, steps, ins, outs, scratch=(), us=1.0):
    def spec(shape, per):
        if per == "weights":
            return pl.BlockSpec((shape[0], HEAD), lambda i, h: (0, h[0]))
        if per is None:
            return pl.BlockSpec(shape, lambda i, h: (0,) * len(shape))
        if isinstance(per, tuple):
            count, first = per
            return pl.BlockSpec((count, EDGE, HEAD), lambda i, h: (i, first // EDGE, 0))
        return pl.BlockSpec((per,) + tuple(shape[1:]), lambda i, h: (i,) + (0,) * (len(shape) - 1))

    return pl.pallas_call(
        kernel,
        grid_spec=pltpu.PrefetchScalarGridSpec(
            num_scalar_prefetch=1,
            grid=(steps,),
            in_specs=[spec(a.shape, per) for a, per in ins],
            out_specs=[spec(s, per) for s, _, per in outs],
            scratch_shapes=list(scratch),
        ),
        out_shape=[jax.ShapeDtypeStruct(s, d) for s, d, _ in outs],
        compiler_params=pltpu.CompilerParams(dimension_semantics=("arbitrary",), vmem_limit_bytes=24 << 20),
        cost_estimate=pl.CostEstimate(flops=int(us * 1.1e9), bytes_accessed=1 << 16, transcendentals=0),
    )(hid, *[a for a, _ in ins])


def shards(
    query_in,
    key_in,
    value_in,
    beta_logit,
    query_conv,
    key_conv,
    value_conv,
    norm_gain,
    out_weight,
    grad_out,
):
    tokens, slots = key_in.shape[0], key_in.shape[1]
    width = query_in.shape[1]
    heads = width // HEAD
    shard_count = lax.axis_size("ctx")
    place = lax.axis_index("ctx")
    groups = shard_count // heads
    group_lists = [[b * heads + i for i in range(heads)] for b in range(groups)]
    rows = tokens * slots
    g = heads
    hid = (place % heads).astype(jnp.int32).reshape(1)

    def exchange(x):
        return lax.all_to_all(x, "ctx", 0, 0, axis_index_groups=group_lists, tiled=True)

    def by_head(x):
        return x.reshape(x.shape[0], heads, HEAD).transpose(1, 0, 2)

    def slots_by_head(x):
        return x.reshape(x.shape[0], slots, heads, HEAD).transpose(2, 0, 1, 3).reshape(heads, -1, HEAD)

    high = lax.reduce_precision(beta_logit, 8, 7)
    rest = beta_logit - high
    middle = lax.reduce_precision(rest, 8, 7)
    betas = jnp.stack([high, middle, rest - middle], axis=2)
    betas = betas.transpose(3, 1, 2, 0).reshape(heads, 3 * slots, tokens).astype(BF16)
    betas = jnp.pad(betas, ((0, 0), (0, EDGE - 3 * slots), (0, 0)))
    kb = exchange(jnp.concatenate([slots_by_head(key_in), betas], axis=1))

    last = EDGE // slots
    tail = jnp.concatenate(
        [slots_by_head(key_in[-last:]), slots_by_head(value_in[-last:]), by_head(query_in[-EDGE:])], axis=1
    )
    tail = jnp.concatenate([tail] * groups, axis=0)
    tail = lax.all_to_all(tail, "ctx", 0, 0, tiled=True)
    group = place // heads
    tail = lax.dynamic_index_in_dim(tail, jnp.maximum(group * heads - 1, 0), 0, False)
    tail = jnp.where(group > 0, tail, jnp.zeros_like(tail))

    grad_normed = jnp.dot(grad_out, out_weight.T, preferred_element_type=F32).astype(BF16)
    vq = exchange(
        jnp.concatenate([slots_by_head(value_in), by_head(query_in), by_head(grad_normed)], axis=1)
    )

    wts = jnp.concatenate(
        [
            jnp.tile(key_conv, (1, 8 // slots, 1)).reshape(8 * TAPS, width),
            jnp.tile(value_conv, (1, 8 // slots, 1)).reshape(8 * TAPS, width),
            query_conv,
            norm_gain.reshape(1, width),
            jnp.zeros((3, width), F32),
        ],
        axis=0,
    )
    per = 2 if g % 2 == 0 else 1
    steps = g // per

    def pad(n):
        return [pltpu.VMEM((per, n + EDGE + 8, HEAD), F32), pltpu.VMEM((EDGE, HEAD), F32)]

    kn, ti = call(
        functools.partial(inverse_kernel, per, tokens, slots),
        hid,
        steps,
        [(kb, per), (tail, None), (wts, "weights")],
        [((g, rows, HEAD), F32, per), ((g, rows, rows), F32, per)],
        pad(rows),
        us=16.0,
    )
    beta = (kb, (per, rows))
    wu, amap, mc, end = call(
        functools.partial(maps_kernel, per, tokens, slots),
        hid,
        steps,
        [(vq, per), beta, (tail, None), (wts, "weights"), (kn, per), (ti, per)],
        [
            ((g, rows, 2 * HEAD), F32, per),
            ((g, HEAD, HEAD), F32, per),
            ((g, HEAD, 2 * HEAD), F32, per),
            ((HEAD, 2 * HEAD), F32, None),
        ],
        pad(rows) + [pltpu.VMEM((HEAD, 2 * HEAD), F32)],
        us=8.0,
    )

    def across(last, towards):
        if groups == 1:
            return jnp.zeros((HEAD, HEAD), F32)
        if groups == 2:
            moves = [(i, i + towards * heads) for i in range(shard_count) if 0 <= i + towards * heads < shard_count]
            return lax.ppermute(last[:, HEAD:], "ctx", moves)
        every = lax.all_gather(last, "ctx")
        head = place % heads
        ahead = group if towards > 0 else groups - 1 - group

        def advance(i, state):
            source = i if towards > 0 else groups - 1 - i
            item = lax.dynamic_index_in_dim(every, source * heads + head, 0, False)
            return jnp.dot(item[:, :HEAD], state, precision=lax.Precision.HIGHEST) + item[:, HEAD:]

        return lax.fori_loop(0, ahead, advance, jnp.zeros((HEAD, HEAD), F32))

    start = across(end, 1)
    q, sc, qm, ol = call(
        functools.partial(queries_kernel, per, tokens, slots),
        hid,
        steps,
        [(vq, per), (tail, None), (wts, "weights"), (kn, per), (wu, per)],
        [
            ((g, tokens, HEAD), F32, per),
            ((g, tokens, rows), F32, per),
            ((g, tokens, HEAD), F32, per),
            ((g, tokens, HEAD), F32, per),
        ],
        pad(tokens),
        us=8.0,
    )
    normed, dr, st, mb, back_end = call(
        functools.partial(outs_kernel, g, tokens, slots),
        hid,
        1,
        [(vq, None), (wts, "weights"), (start, None), (mc, None), (qm, None), (ol, None), (amap, None)],
        [
            ((g, tokens, HEAD), BF16, None),
            ((g, tokens, HEAD), F32, None),
            ((g, HEAD, HEAD), F32, None),
            ((g, HEAD, 2 * HEAD), F32, None),
            ((HEAD, 2 * HEAD), F32, None),
        ],
        us=4.0,
    )
    finish = across(back_end, -1)
    d, dk, dd, gq = call(
        functools.partial(query_grads_kernel, per, tokens, slots),
        hid,
        steps,
        [
            (vq, per), (tail, None), (wts, "weights"), (kn, per), (wu, per), (q, per), (sc, per), (dr, per), (st, per),
        ],
        [
            ((g, rows, HEAD), F32, per),
            ((g, rows, HEAD), F32, per),
            ((g, rows, HEAD), F32, per),
            ((g, tokens + EDGE, HEAD), BF16, per),
        ],
        pad(tokens),
        us=20.0,
    )
    nq = exchange(jnp.concatenate([normed, gq], axis=1))
    gs, de, gv = call(
        functools.partial(value_grads_kernel, per, tokens, slots),
        hid,
        steps,
        [
            (vq, per), beta, (tail, None), (wts, "weights"), (finish, None), (mb, per), (kn, per), (ti, per),
            (d, per), (dd, per),
        ],
        [
            ((g, HEAD, HEAD), F32, per),
            ((g, rows, HEAD), F32, per),
            ((g, rows + 2 * EDGE, HEAD), BF16, per),
        ],
        pad(rows),
        us=8.0,
    )
    gv = exchange(gv)
    (gk,) = call(
        functools.partial(key_grads_kernel, per, tokens, slots),
        hid,
        steps,
        [
            (kb, per), (tail, None), (wts, "weights"), (kn, per), (d, per), (dk, per), (de, per), (st, per), (gs, per),
        ],
        [((g, rows + EDGE, HEAD), BF16, per)],
        pad(rows),
        us=12.0,
    )
    gk = exchange(gk)

    normed_bf = nq[:, :tokens].transpose(1, 0, 2).reshape(tokens, width)
    partial = jnp.dot(normed_bf, out_weight, preferred_element_type=F32)
    if lax.axis_size("head") == 2:
        half = tokens // 2
        mine = lax.axis_index("head")
        pieces = partial.reshape(2, half, partial.shape[1])
        kept = lax.dynamic_index_in_dim(pieces, mine, 0, False)
        sent = lax.dynamic_index_in_dim(pieces, 1 - mine, 0, False).astype(BF16)
        layer_out = (kept + lax.ppermute(sent, "head", [(0, 1), (1, 0)]).astype(F32)).astype(BF16)
    else:
        layer_out = lax.psum_scatter(partial.astype(BF16), "head", scatter_dimension=0, tiled=True)

    edge = RIM * slots
    rims = jnp.concatenate(
        [
            gk[:, rows + 8 - edge : rows + 8],
            gv[:, rows + EDGE + 8 - edge : rows + EDGE + 8],
            nq[:, 2 * tokens + 8 - RIM : 2 * tokens + 8],
        ],
        axis=1,
    )
    rims = lax.ppermute(rims, "ctx", [(i, i - 1) for i in range(1, shard_count)]).astype(F32)

    def slots_back(block, rim):
        block = block.reshape(heads, tokens, slots, HEAD).astype(F32)
        rim = jnp.pad(rim.reshape(heads, RIM, slots, HEAD), ((0, 0), (tokens - RIM, 0), (0, 0), (0, 0)))
        return (block + rim).transpose(1, 2, 0, 3).reshape(tokens, slots, width)

    grad_key = slots_back(gk[:, :rows], rims[:, :edge])
    grad_value = slots_back(gv[:, :rows], rims[:, edge : 2 * edge])
    rim_query = jnp.pad(rims[:, 2 * edge :], ((0, 0), (tokens - RIM, 0), (0, 0)))
    grad_query = (nq[:, tokens : 2 * tokens].astype(F32) + rim_query).transpose(1, 0, 2).reshape(tokens, width)
    marks = gv[:, rows : rows + 2 * slots].astype(F32)
    grad_beta = marks.reshape(heads, slots, 2, tokens).sum(axis=2).transpose(2, 1, 0)
    return (layer_out, grad_query, grad_key, grad_value, grad_beta)


def solution(mesh):
    placed = (
        P("ctx", "head"),
        P("ctx", None, "head"),
        P("ctx", None, "head"),
        P("ctx", None, "head"),
        P(None, "head"),
        P(None, None, "head"),
        P(None, None, "head"),
        P("head"),
        P("head", None),
        P("ctx", None),
    )
    return jax.shard_map(
        shards,
        mesh=mesh,
        in_specs=placed,
        out_specs=(
            P(("ctx", "head"), None),
            P("ctx", "head"),
            P("ctx", None, "head"),
            P("ctx", None, "head"),
            P("ctx", None, "head"),
        ),
        check_vma=False,
    )
```

```python
import functools

import jax
import jax.numpy as jnp
from jax import lax
from jax.experimental import pallas as pl
from jax.experimental.pallas import tpu as pltpu
from jax.sharding import PartitionSpec as P

HEAD = 128
TAPS = 4
RIM = TAPS - 1
EDGE = 16
EPS = 1e-06
F32 = jnp.float32
BF16 = jnp.bfloat16

ROWS_COLS = (((1,), (0,)), ((), ()))
ROWS_ROWS = (((1,), (1,)), ((), ()))
COLS_COLS = (((0,), (0,)), ((), ()))


def two(x):
    high = x.astype(BF16)
    return high, (x - high.astype(F32)).astype(BF16)


def dot(a, b, dims):
    return lax.dot_general(a, b, dims, preferred_element_type=F32)


def mm(left, right, dims=ROWS_COLS):
    (ah, al), (bh, bl) = left, right
    ka, kb = dims[0][0][0], dims[0][1][0]
    nb = 1 - kb
    depth, cols = ah.shape[ka], bh.shape[nb]
    if depth <= HEAD:
        a = jnp.concatenate([ah, al], axis=ka)
        high, low = jnp.concatenate([bh, bh], axis=kb), jnp.concatenate([bl, bl], axis=kb)
        if cols <= HEAD:
            out = dot(a, jnp.concatenate([high, low], axis=nb), dims)
            return out[:, :cols] + out[:, cols:]
        return dot(a, high, dims) + dot(a, low, dims)
    if cols <= HEAD:
        out = dot(ah, jnp.concatenate([bh, bl], axis=nb), dims)
        return out[:, :cols] + out[:, cols:] + dot(al, bh, dims)
    return dot(ah, bh, dims) + dot(ah, bl, dims) + dot(al, bh, dims)


def grid_of(rows, cols):
    return lax.broadcasted_iota(jnp.int32, (rows, cols), 0), lax.broadcasted_iota(jnp.int32, (rows, cols), 1)


def before(rows):
    r, c = grid_of(rows, rows)
    return c < r


def level_pairs(rows, level):
    r, c = grid_of(rows, rows)
    return ((r >> (level + 1)) == (c >> (level + 1))) & (((r >> level) & 1) == 1) & (((c >> level) & 1) == 0)


def visible(tokens, slots):
    t, c = grid_of(tokens, tokens * slots)
    return c < slots * (t + 1)


def times(pattern, x):
    if pattern.shape[0] == 1:
        return pattern * x
    return (x.reshape(-1, 8, HEAD) * pattern[None]).reshape(x.shape)


def conv_rows(x, edge, taps, pad, stride):
    rows = x.shape[0]
    pad[pl.ds(0, EDGE), :] = edge
    pad[pl.ds(EDGE, rows), :] = x
    total = None
    for i in range(TAPS):
        part = times(taps[i], pad[pl.ds(EDGE - stride * (RIM - i), rows), :])
        total = part if total is None else total + part
    return total


def conv_back(grad, taps, pad, stride):
    rows = grad.shape[0]
    pad[pl.ds(8, 8), :] = jnp.zeros((8, HEAD), F32)
    pad[pl.ds(EDGE, rows), :] = grad
    pad[pl.ds(EDGE + rows, 8), :] = jnp.zeros((8, HEAD), F32)
    inner, rim = None, None
    for i in range(TAPS):
        part = times(taps[i], pad[pl.ds(EDGE + stride * (RIM - i), rows), :])
        edge = times(taps[i], pad[pl.ds(8 + stride * (RIM - i), 8), :])
        inner = part if inner is None else inner + part
        rim = edge if rim is None else rim + edge
    return inner, rim


def sigmoid(x):
    return 1.0 / (1.0 + jnp.exp(-x))


def silu(s):
    sg = sigmoid(s)
    return s * sg, sg * (1.0 + s * (1.0 - sg))


def unit(values):
    scale = lax.rsqrt(jnp.sum(values * values, axis=-1, keepdims=True) + EPS)
    return values * scale, scale


def beta_rows(tile, slots):
    return [tile[3 * j : 3 * j + 1] + tile[3 * j + 1 : 3 * j + 2] + tile[3 * j + 2 : 3 * j + 3] for j in range(slots)]


def places(tokens, slots, j):
    r, t = grid_of(tokens * slots, tokens)
    return r == slots * t + j


def column(rows, tokens, slots):
    spread = jnp.zeros((tokens * slots, tokens), F32)
    for j in range(slots):
        spread = jnp.where(places(tokens, slots, j), rows[j], spread)
    return jnp.sum(spread, axis=1, keepdims=True)


def slot_taps(wts, kind):
    return [wts[8 * (TAPS * kind + i) : 8 * (TAPS * kind + i + 1)] for i in range(TAPS)]


def query_taps(wts):
    return [wts[16 * TAPS + i : 16 * TAPS + i + 1] for i in range(TAPS)]


def gain_row(wts):
    return wts[17 * TAPS : 17 * TAPS + 1]


def edges(ref, first, rows, per, tail, halo):
    @pl.when(pl.program_id(0) == 0)
    def _():
        halo[...] = tail

    found = [halo[...]] + [ref[n, pl.ds(first + rows - EDGE, EDGE), :].astype(F32) for n in range(per - 1)]
    halo[...] = ref[per - 1, pl.ds(first + rows - EDGE, EDGE), :].astype(F32)
    return found


def inverse_kernel(per, tokens, slots, hid, kb_ref, tail_ref, wts_ref, kn_ref, ti_ref, fk_ref, pad, halo):
    rows = tokens * slots
    taps = slot_taps(wts_ref[...], 0)
    tops = edges(kb_ref, 0, rows, per, tail_ref[pl.ds(0, EDGE), :].astype(F32), halo)
    order = before(rows)
    blocks = rows // HEAD
    grams = []
    for n in range(per):
        s = conv_rows(kb_ref[n, pl.ds(0, rows), :].astype(F32), tops[n], taps, pad.at[n], slots)
        c, slope = silu(s)
        k, scale = unit(c)
        kn_ref[n] = k
        fk_ref[n] = scale * slope
        betas = beta_rows(kb_ref[n, pl.ds(rows, EDGE), :].astype(F32), slots)
        strength = 2.0 * sigmoid(column(betas, tokens, slots))
        k2 = two(k)
        grams.append(jnp.where(order, mm(k2, k2, ROWS_ROWS) * strength, 0.0))
    r, c = grid_of(HEAD, HEAD)
    eye = (r == c).astype(F32)
    zero = jnp.zeros((HEAD, HEAD), BF16)
    diagonal = [
        gram[b * HEAD : (b + 1) * HEAD, b * HEAD : (b + 1) * HEAD] for gram in grams for b in range(blocks)
    ]
    systems = [two(x) for x in diagonal]
    pairs = level_pairs(HEAD, 0)
    inverse = [eye - jnp.where(pairs, x, 0.0) for x in diagonal]
    level = 1
    while (1 << level) < HEAD:
        pairs = level_pairs(HEAD, level)
        split = [two(x) for x in inverse]
        crossed = [mm(tuple(jnp.where(pairs, p, zero) for p in s), x) for s, x in zip(systems, split)]
        inverse = [x - mm(s, two(y)) for x, s, y in zip(inverse, split, crossed)]
        level += 1
    for n in range(per):
        done = inverse[n * blocks : (n + 1) * blocks]
        size = HEAD
        while len(done) > 1:
            merged = []
            for b in range(0, len(done), 2):
                top, low = done[b], done[b + 1]
                cross = grams[n][(b + 1) * size : (b + 2) * size, b * size : (b + 1) * size]
                cross = mm(two(low), two(mm(two(cross), two(top))))
                merged.append(
                    jnp.concatenate(
                        [
                            jnp.concatenate([top, jnp.zeros_like(top)], axis=1),
                            jnp.concatenate([-cross, low], axis=1),
                        ],
                        axis=0,
                    )
                )
            done = merged
            size *= 2
        ti_ref[n] = done[0]


def maps_kernel(
    per, tokens, slots, hid, vq_ref, beta_ref, tail_ref, wts_ref, kn_ref, ti_ref,
    wu_ref, a_ref, mc_ref, end_ref, fv_ref, pad, halo, carry,
):
    rows = tokens * slots
    taps = slot_taps(wts_ref[...], 1)
    ir, ic = grid_of(HEAD, 2 * HEAD)

    @pl.when(pl.program_id(0) == 0)
    def _():
        carry[...] = (ir == ic).astype(F32)

    tops = edges(vq_ref, 0, rows, per, tail_ref[pl.ds(EDGE, EDGE), :].astype(F32), halo)
    maps = []
    for n in range(per):
        s = conv_rows(vq_ref[n, pl.ds(0, rows), :].astype(F32), tops[n], taps, pad.at[n], slots)
        v, fv_ref[n] = silu(s)
        betas = beta_rows(beta_ref[n].astype(F32), slots)
        strength = 2.0 * sigmoid(column(betas, tokens, slots))
        k = kn_ref[n]
        wu = mm(two(ti_ref[n]), two(strength * jnp.concatenate([k, v], axis=1)))
        wu_ref[n] = wu
        maps.append(mm(two(k), two(wu), COLS_COLS))
    state = carry[...]
    for n in range(per):
        mc_ref[n] = state
        a = (ir == ic)[:, :HEAD].astype(F32) - maps[n][:, :HEAD]
        a_ref[n] = a
        moved = mm(two(a), two(state))
        state = jnp.where(ic < HEAD, moved, moved + maps[n])
    carry[...] = state
    end_ref[...] = state


def queries_kernel(
    per, tokens, slots, hid, vq_ref, tail_ref, wts_ref, kn_ref, wu_ref, q_ref, sc_ref, qm_ref, ol_ref, fq_ref, pad, halo
):
    rows = tokens * slots
    taps = query_taps(wts_ref[...])
    tops = edges(vq_ref, rows, tokens, per, tail_ref[pl.ds(2 * EDGE, EDGE), :].astype(F32), halo)
    seen = visible(tokens, slots)
    for n in range(per):
        s = conv_rows(vq_ref[n, pl.ds(rows, tokens), :].astype(F32), tops[n], taps, pad.at[n], 1)
        c, slope = silu(s)
        q, scale = unit(c)
        fq_ref[n] = scale * slope
        scores = jnp.where(seen, mm(two(q), two(kn_ref[n]), ROWS_ROWS), 0.0)
        mapped = mm(two(scores), two(wu_ref[n]))
        q_ref[n] = q
        sc_ref[n] = scores
        qm_ref[n] = q - mapped[:, :HEAD]
        ol_ref[n] = mapped[:, HEAD:]


def outs_kernel(
    count, tokens, slots, hid, vq_ref, wts_ref, start_ref, mc_ref, qm_ref, ol_ref, a_ref,
    nm_ref, dr_ref, st_ref, mb_ref, end_ref,
):
    rows = tokens * slots
    gain = gain_row(wts_ref[...])
    start = two(start_ref[...])
    states = [
        mm(two(mc_ref[n, :, pl.ds(0, HEAD)]), start) + mc_ref[n, :, pl.ds(HEAD, HEAD)] for n in range(count)
    ]
    mapped = [two(qm_ref[n]) for n in range(count)]
    raws = [mm(mapped[n], two(states[n])) + ol_ref[n] for n in range(count)]
    local = []
    for n in range(count):
        st_ref[n] = states[n]
        raw = raws[n]
        scale = lax.rsqrt(jnp.mean(raw * raw, axis=-1, keepdims=True) + EPS)
        hat = raw * scale
        nm_ref[n] = (hat * gain).astype(BF16)
        dn = vq_ref[n, pl.ds(rows + tokens, tokens), :].astype(F32) * gain
        dr = scale * (dn - hat * jnp.mean(dn * hat, axis=-1, keepdims=True))
        dr_ref[n] = dr
        local.append(mm(mapped[n], two(dr), COLS_COLS))
    ir, ic = grid_of(HEAD, 2 * HEAD)
    state = (ir == ic).astype(F32)
    for n in range(count - 1, -1, -1):
        mb_ref[n] = state
        moved = mm(two(a_ref[n]), two(state), COLS_COLS)
        state = moved + jnp.concatenate([jnp.zeros((HEAD, HEAD), F32), local[n]], axis=1)
    end_ref[...] = state


def query_grads_kernel(
    per, tokens, slots, hid, wts_ref, kn_ref, wu_ref, q_ref, sc_ref, dr_ref, st_ref, fq_ref, nm_ref,
    d_ref, dk_ref, dd_ref, nq_ref, pad,
):
    taps = query_taps(wts_ref[...])
    seen = visible(tokens, slots)
    for n in range(per):
        q = q_ref[n]
        state, dr, k2 = two(st_ref[n]), two(dr_ref[n]), two(kn_ref[n])
        d = wu_ref[n, :, pl.ds(HEAD, HEAD)] - mm(two(wu_ref[n, :, pl.ds(0, HEAD)]), state)
        d_ref[n] = d
        ds = two(jnp.where(seen, mm(dr, two(d), ROWS_ROWS), 0.0))
        dq = mm(dr, state, ROWS_ROWS) + mm(ds, k2)
        dk_ref[n] = mm(ds, two(q), COLS_COLS)
        dd_ref[n] = mm(two(sc_ref[n]), dr, COLS_COLS)
        inner, rim = conv_back(fq_ref[n] * (dq - q * jnp.sum(q * dq, axis=-1, keepdims=True)), taps, pad.at[n], 1)
        nq_ref[n, pl.ds(0, tokens), :] = nm_ref[n]
        nq_ref[n, pl.ds(tokens, tokens), :] = inner.astype(BF16)
        nq_ref[n, pl.ds(2 * tokens, EDGE), :] = jnp.concatenate([rim, jnp.zeros((8, HEAD), F32)], axis=0).astype(BF16)


def grads_kernel(
    per, tokens, slots, hid, beta_ref, wts_ref, end_ref, mb_ref, kn_ref, ti_ref, d_ref, dk_ref, dd_ref, st_ref,
    fk_ref, fv_ref, out_ref, pad,
):
    rows = tokens * slots
    wts = wts_ref[...]
    order = before(rows)
    end = two(end_ref[...])
    for n in range(per):
        k, d = kn_ref[n], d_ref[n]
        k2, d2 = two(k), two(d)
        g2 = two(mm(two(mb_ref[n, :, pl.ds(0, HEAD)]), end) + mb_ref[n, :, pl.ds(HEAD, HEAD)])
        y = mm(two(ti_ref[n]), two(dd_ref[n] + mm(k2, g2)), COLS_COLS)
        betas = beta_rows(beta_ref[n].astype(F32), slots)
        de = 2.0 * sigmoid(column(betas, tokens, slots)) * y
        de2 = two(de)
        dgram = jnp.where(order, mm(de2, d2, ROWS_ROWS), 0.0)
        dk = dk_ref[n] + mm(d2, g2, ROWS_ROWS) - mm(de2, two(st_ref[n]), ROWS_ROWS)
        dk = dk - mm(two(dgram + dgram.T), k2)
        along = jnp.sum(y * d, axis=1, keepdims=True)
        marks = []
        for j in range(slots):
            gb = jnp.sum(jnp.where(places(tokens, slots, j), along, 0.0), axis=0, keepdims=True) * sigmoid(-betas[j])
            high = gb.astype(BF16).astype(F32)
            marks += [high, gb - high]
        marks.append(jnp.zeros((EDGE - 2 * slots, tokens), F32))
        value, value_rim = conv_back(fv_ref[n] * de, slot_taps(wts, 1), pad.at[2 * n], slots)
        part = fk_ref[n] * (dk - k * jnp.sum(k * dk, axis=-1, keepdims=True))
        key, key_rim = conv_back(part, slot_taps(wts, 0), pad.at[2 * n + 1], slots)
        out_ref[n, pl.ds(0, rows), :] = key.astype(BF16)
        out_ref[n, pl.ds(rows, rows), :] = value.astype(BF16)
        out_ref[n, pl.ds(2 * rows, EDGE), :] = jnp.concatenate(marks, axis=0).astype(BF16)
        out_ref[n, pl.ds(2 * rows + EDGE, EDGE), :] = jnp.concatenate([key_rim, value_rim], axis=0).astype(BF16)


def unpack_kernel(tokens, slots, got_ref, rim_ref, gk_ref, gv_ref):
    rows = tokens * slots
    for a, out_ref in enumerate((gk_ref, gv_ref)):
        main = got_ref[0, pl.ds(a * rows, rows), :].astype(F32)
        last = main[rows - 8 :] + rim_ref[0, pl.ds(8 * a, 8), :].astype(F32)
        out_ref[...] = jnp.concatenate([main[: rows - 8], last], axis=0).reshape(tokens, slots, HEAD)


def unpack_query_kernel(tokens, got_ref, rim_ref, gq_ref):
    main = got_ref[0, pl.ds(tokens, tokens), :].astype(F32)
    last = main[tokens - 8 :] + rim_ref[0, pl.ds(0, 8), :].astype(F32)
    gq_ref[...] = jnp.concatenate([main[: tokens - 8], last], axis=0)


def call(kernel, hid, steps, ins, outs, scratch=(), us=1.0, grant=24):
    def spec(shape, per):
        if per == "weights":
            return pl.BlockSpec((shape[0], HEAD), lambda i, h: (0, h[0]))
        if per is None:
            return pl.BlockSpec(shape, lambda i, h: (0,) * len(shape))
        if isinstance(per, tuple):
            count, first = per
            return pl.BlockSpec((count, EDGE, HEAD), lambda i, h: (i, first // EDGE, 0))
        return pl.BlockSpec((per,) + tuple(shape[1:]), lambda i, h: (i,) + (0,) * (len(shape) - 1))

    return pl.pallas_call(
        kernel,
        grid_spec=pltpu.PrefetchScalarGridSpec(
            num_scalar_prefetch=1,
            grid=(steps,),
            in_specs=[spec(a.shape, per) for a, per in ins],
            out_specs=[spec(s, per) for s, _, per in outs],
            scratch_shapes=list(scratch),
        ),
        out_shape=[pltpu.HBM(s, d) if len(s) == 3 else jax.ShapeDtypeStruct(s, d) for s, d, _ in outs],
        compiler_params=pltpu.CompilerParams(dimension_semantics=("arbitrary",), vmem_limit_bytes=grant << 20),
        cost_estimate=pl.CostEstimate(flops=int(us * 1.1e9), bytes_accessed=1 << 16, transcendentals=0),
    )(hid, *[pltpu.with_memory_space_constraint(a, pltpu.HBM) if a.dtype == F32 and a.ndim == 3 else a for a, _ in ins])


def shards(
    query_in,
    key_in,
    value_in,
    beta_logit,
    query_conv,
    key_conv,
    value_conv,
    norm_gain,
    out_weight,
    grad_out,
):
    tokens, slots = key_in.shape[0], key_in.shape[1]
    width = query_in.shape[1]
    heads = width // HEAD
    shard_count = lax.axis_size("ctx")
    place = lax.axis_index("ctx")
    groups = shard_count // heads
    group_lists = [[b * heads + i for i in range(heads)] for b in range(groups)]
    rows = tokens * slots
    g = heads
    hid = (place % heads).astype(jnp.int32).reshape(1)

    def exchange(x):
        return lax.all_to_all(x, "ctx", 0, 0, axis_index_groups=group_lists, tiled=True)

    def by_head(x):
        return x.reshape(x.shape[0], heads, HEAD).transpose(1, 0, 2)

    def slots_by_head(x):
        return x.reshape(x.shape[0], slots, heads, HEAD).transpose(2, 0, 1, 3).reshape(heads, -1, HEAD)

    high = lax.reduce_precision(beta_logit, 8, 7)
    rest = beta_logit - high
    middle = lax.reduce_precision(rest, 8, 7)
    betas = jnp.stack([high, middle, rest - middle], axis=2)
    betas = betas.transpose(3, 1, 2, 0).reshape(heads, 3 * slots, tokens).astype(BF16)
    betas = jnp.pad(betas, ((0, 0), (0, EDGE - 3 * slots), (0, 0)))
    last = EDGE // slots
    kb = exchange(
        jnp.concatenate(
            [slots_by_head(key_in), betas, slots_by_head(value_in[-last:]), by_head(query_in[-EDGE:])], axis=1
        )
    )

    group = place // heads
    tail = jnp.concatenate([kb[g - 1, rows - EDGE : rows], kb[g - 1, rows + EDGE :]], axis=0)
    tail = lax.ppermute(tail, "ctx", [(i, i + heads) for i in range(shard_count - heads)])

    grad_normed = jnp.dot(grad_out, out_weight.T, preferred_element_type=F32).astype(BF16)
    vq = exchange(
        jnp.concatenate([slots_by_head(value_in), by_head(query_in), by_head(grad_normed)], axis=1)
    )

    wts = jnp.concatenate(
        [
            jnp.tile(key_conv, (1, 8 // slots, 1)).reshape(8 * TAPS, width),
            jnp.tile(value_conv, (1, 8 // slots, 1)).reshape(8 * TAPS, width),
            query_conv,
            norm_gain.reshape(1, width),
            jnp.zeros((3, width), F32),
        ],
        axis=0,
    )
    per = 2 if g % 2 == 0 else 1
    steps = g // per

    def pad(n):
        return [pltpu.VMEM((per, n + EDGE + 8, HEAD), F32), pltpu.VMEM((EDGE, HEAD), F32)]

    kn, ti, fk = call(
        functools.partial(inverse_kernel, per, tokens, slots),
        hid,
        steps,
        [(kb, per), (tail, None), (wts, "weights")],
        [((g, rows, HEAD), F32, per), ((g, rows, rows), F32, per), ((g, rows, HEAD), F32, per)],
        pad(rows),
        us=12.0,
    )
    beta = (kb, (per, rows))
    wu, amap, mc, end, fv = call(
        functools.partial(maps_kernel, per, tokens, slots),
        hid,
        steps,
        [(vq, per), beta, (tail, None), (wts, "weights"), (kn, per), (ti, per)],
        [
            ((g, rows, 2 * HEAD), F32, per),
            ((g, HEAD, HEAD), F32, per),
            ((g, HEAD, 2 * HEAD), F32, per),
            ((HEAD, 2 * HEAD), F32, None),
            ((g, rows, HEAD), F32, per),
        ],
        pad(rows) + [pltpu.VMEM((HEAD, 2 * HEAD), F32)],
        us=8.0,
    )

    def across(last, towards):
        if groups == 1:
            return jnp.zeros((HEAD, HEAD), F32)
        if groups == 2:
            moves = [(i, i + towards * heads) for i in range(shard_count) if 0 <= i + towards * heads < shard_count]
            return lax.ppermute(last[:, HEAD:], "ctx", moves)
        every = lax.all_gather(last, "ctx")
        head = place % heads
        ahead = group if towards > 0 else groups - 1 - group

        def advance(i, state):
            source = i if towards > 0 else groups - 1 - i
            item = lax.dynamic_index_in_dim(every, source * heads + head, 0, False)
            return jnp.dot(item[:, :HEAD], state, precision=lax.Precision.HIGHEST) + item[:, HEAD:]

        return lax.fori_loop(0, ahead, advance, jnp.zeros((HEAD, HEAD), F32))

    start = across(end, 1)
    q, sc, qm, ol, fq = call(
        functools.partial(queries_kernel, per, tokens, slots),
        hid,
        steps,
        [(vq, per), (tail, None), (wts, "weights"), (kn, per), (wu, per)],
        [
            ((g, tokens, HEAD), F32, per),
            ((g, tokens, rows), F32, per),
            ((g, tokens, HEAD), F32, per),
            ((g, tokens, HEAD), F32, per),
            ((g, tokens, HEAD), F32, per),
        ],
        pad(tokens),
        us=8.0,
    )
    normed, dr, st, mb, back_end = call(
        functools.partial(outs_kernel, g, tokens, slots),
        hid,
        1,
        [(vq, None), (wts, "weights"), (start, None), (mc, None), (qm, None), (ol, None), (amap, None)],
        [
            ((g, tokens, HEAD), BF16, None),
            ((g, tokens, HEAD), F32, None),
            ((g, HEAD, HEAD), F32, None),
            ((g, HEAD, 2 * HEAD), F32, None),
            ((HEAD, 2 * HEAD), F32, None),
        ],
        us=4.0,
    )
    finish = across(back_end, -1)
    d, dk, dd, nq = call(
        functools.partial(query_grads_kernel, per, tokens, slots),
        hid,
        steps,
        [
            (wts, "weights"), (kn, per), (wu, per), (q, per), (sc, per), (dr, per), (st, per), (fq, per), (normed, per),
        ],
        [
            ((g, rows, HEAD), F32, per),
            ((g, rows, HEAD), F32, per),
            ((g, rows, HEAD), F32, per),
            ((g, 2 * tokens + EDGE, HEAD), BF16, per),
        ],
        pad(tokens)[:1],
        us=20.0,
    )
    nq = exchange(nq)
    (grads,) = call(
        functools.partial(grads_kernel, per, tokens, slots),
        hid,
        steps,
        [
            beta, (wts, "weights"), (finish, None), (mb, per), (kn, per), (ti, per), (d, per), (dk, per), (dd, per),
            (st, per), (fk, per), (fv, per),
        ],
        [((g, 2 * rows + 2 * EDGE, HEAD), BF16, per)],
        [pltpu.VMEM((2 * per, rows + EDGE + 8, HEAD), F32)],
        us=20.0,
    )
    grads = exchange(grads)

    normed_bf = nq[:, :tokens].transpose(1, 0, 2).reshape(tokens, width)
    partial = jnp.dot(normed_bf, out_weight, preferred_element_type=F32)
    if lax.axis_size("head") == 2:
        half = tokens // 2
        mine = lax.axis_index("head")
        pieces = partial.reshape(2, half, partial.shape[1])
        kept = lax.dynamic_index_in_dim(pieces, mine, 0, False)
        sent = lax.dynamic_index_in_dim(pieces, 1 - mine, 0, False).astype(BF16)
        layer_out = (kept + lax.ppermute(sent, "head", [(0, 1), (1, 0)]).astype(F32)).astype(BF16)
    else:
        layer_out = lax.psum_scatter(partial.astype(BF16), "head", scatter_dimension=0, tiled=True)

    back = [(i, i - 1) for i in range(1, shard_count)]
    query_rim = lax.ppermute(nq[:, 2 * tokens :], "ctx", back)
    rim = lax.ppermute(grads[:, 2 * rows + EDGE :], "ctx", back)
    part = lambda x: pl.BlockSpec((1,) + x.shape[1:], lambda h: (h, 0, 0))
    grad_query = pl.pallas_call(
        functools.partial(unpack_query_kernel, tokens),
        grid=(heads,),
        in_specs=[part(nq), part(query_rim)],
        out_specs=pl.BlockSpec((tokens, HEAD), lambda h: (0, h)),
        out_shape=jax.ShapeDtypeStruct((tokens, width), F32),
        compiler_params=pltpu.CompilerParams(vmem_limit_bytes=8 << 20),
    )(nq, query_rim)
    grad_key, grad_value = pl.pallas_call(
        functools.partial(unpack_kernel, tokens, slots),
        grid=(heads,),
        in_specs=[part(grads), part(rim)],
        out_specs=[pl.BlockSpec((tokens, slots, HEAD), lambda h: (0, 0, h))] * 2,
        out_shape=[jax.ShapeDtypeStruct((tokens, slots, width), F32)] * 2,
        compiler_params=pltpu.CompilerParams(vmem_limit_bytes=8 << 20),
    )(grads, rim)
    marks = grads[:, 2 * rows : 2 * rows + 2 * slots].astype(F32)
    grad_beta = marks.reshape(heads, slots, 2, tokens).sum(axis=2).transpose(2, 1, 0)
    return (layer_out, grad_query, grad_key, grad_value, grad_beta)


def solution(mesh):
    placed = (
        P("ctx", "head"),
        P("ctx", None, "head"),
        P("ctx", None, "head"),
        P("ctx", None, "head"),
        P(None, "head"),
        P(None, None, "head"),
        P(None, None, "head"),
        P("head"),
        P("head", None),
        P("ctx", None),
    )
    return jax.shard_map(
        shards,
        mesh=mesh,
        in_specs=placed,
        out_specs=(
            P(("ctx", "head"), None),
            P("ctx", "head"),
            P("ctx", None, "head"),
            P("ctx", None, "head"),
            P("ctx", None, "head"),
        ),
        check_vma=False,
    )
```

```python
import functools

import jax
import jax.numpy as jnp
from jax import lax
from jax.experimental import pallas as pl
from jax.experimental.pallas import tpu as pltpu
from jax.sharding import PartitionSpec as P

HEAD = 128
TAPS = 4
RIM = TAPS - 1
EDGE = 16
EPS = 1e-06
F32 = jnp.float32
BF16 = jnp.bfloat16

ROWS_COLS = (((1,), (0,)), ((), ()))
ROWS_ROWS = (((1,), (1,)), ((), ()))
COLS_COLS = (((0,), (0,)), ((), ()))


def two(x):
    high = x.astype(BF16)
    return high, (x - high.astype(F32)).astype(BF16)


def dot(a, b, dims):
    return lax.dot_general(a, b, dims, preferred_element_type=F32)


def mm(left, right, dims=ROWS_COLS):
    (ah, al), (bh, bl) = left, right
    ka, kb = dims[0][0][0], dims[0][1][0]
    nb = 1 - kb
    depth, cols = ah.shape[ka], bh.shape[nb]
    if depth <= HEAD:
        a = jnp.concatenate([ah, al], axis=ka)
        high, low = jnp.concatenate([bh, bh], axis=kb), jnp.concatenate([bl, bl], axis=kb)
        if cols <= HEAD:
            out = dot(a, jnp.concatenate([high, low], axis=nb), dims)
            return out[:, :cols] + out[:, cols:]
        return dot(a, high, dims) + dot(a, low, dims)
    if cols <= HEAD:
        out = dot(ah, jnp.concatenate([bh, bl], axis=nb), dims)
        return out[:, :cols] + out[:, cols:] + dot(al, bh, dims)
    return dot(ah, bh, dims) + dot(ah, bl, dims) + dot(al, bh, dims)


def grid_of(rows, cols):
    return lax.broadcasted_iota(jnp.int32, (rows, cols), 0), lax.broadcasted_iota(jnp.int32, (rows, cols), 1)


def before(rows):
    r, c = grid_of(rows, rows)
    return c < r


def level_pairs(rows, level):
    r, c = grid_of(rows, rows)
    return ((r >> (level + 1)) == (c >> (level + 1))) & (((r >> level) & 1) == 1) & (((c >> level) & 1) == 0)


def visible(tokens, slots):
    t, c = grid_of(tokens, tokens * slots)
    return c < slots * (t + 1)


def times(pattern, x):
    if pattern.shape[0] == 1:
        return pattern * x
    return (x.reshape(-1, 8, HEAD) * pattern[None]).reshape(x.shape)


def conv_rows(x, edge, taps, pad, stride):
    rows = x.shape[0]
    pad[pl.ds(0, EDGE), :] = edge
    pad[pl.ds(EDGE, rows), :] = x
    total = None
    for i in range(TAPS):
        part = times(taps[i], pad[pl.ds(EDGE - stride * (RIM - i), rows), :])
        total = part if total is None else total + part
    return total


def conv_back(grad, taps, pad, stride):
    rows = grad.shape[0]
    pad[pl.ds(8, 8), :] = jnp.zeros((8, HEAD), F32)
    pad[pl.ds(EDGE, rows), :] = grad
    pad[pl.ds(EDGE + rows, 8), :] = jnp.zeros((8, HEAD), F32)
    inner, rim = None, None
    for i in range(TAPS):
        part = times(taps[i], pad[pl.ds(EDGE + stride * (RIM - i), rows), :])
        edge = times(taps[i], pad[pl.ds(8 + stride * (RIM - i), 8), :])
        inner = part if inner is None else inner + part
        rim = edge if rim is None else rim + edge
    return inner, rim


def sigmoid(x):
    return 1.0 / (1.0 + jnp.exp(-x))


def silu(s):
    sg = sigmoid(s)
    return s * sg, sg * (1.0 + s * (1.0 - sg))


def unit(values):
    scale = lax.rsqrt(jnp.sum(values * values, axis=-1, keepdims=True) + EPS)
    return values * scale, scale


def beta_rows(tile, slots):
    return [tile[3 * j : 3 * j + 1] + tile[3 * j + 1 : 3 * j + 2] + tile[3 * j + 2 : 3 * j + 3] for j in range(slots)]


def places(tokens, slots, j):
    r, t = grid_of(tokens * slots, tokens)
    return r == slots * t + j


def column(rows, tokens, slots):
    spread = jnp.zeros((tokens * slots, tokens), F32)
    for j in range(slots):
        spread = jnp.where(places(tokens, slots, j), rows[j], spread)
    return jnp.sum(spread, axis=1, keepdims=True)


def slot_taps(wts, kind):
    return [wts[8 * (TAPS * kind + i) : 8 * (TAPS * kind + i + 1)] for i in range(TAPS)]


def query_taps(wts):
    return [wts[16 * TAPS + i : 16 * TAPS + i + 1] for i in range(TAPS)]


def gain_row(wts):
    return wts[17 * TAPS : 17 * TAPS + 1]


def edges(ref, first, rows, per, tail, prev_ref):
    prev = jnp.where(pl.program_id(0) == 0, tail, prev_ref[0].astype(F32))
    return [prev] + [ref[n, pl.ds(first + rows - EDGE, EDGE), :].astype(F32) for n in range(per - 1)]


def inverse_kernel(per, tokens, slots, hid, kb_ref, prev_ref, tail_ref, wts_ref, kn_ref, ti_ref, fk_ref, pad):
    rows = tokens * slots
    taps = slot_taps(wts_ref[...], 0)
    tops = edges(kb_ref, 0, rows, per, tail_ref[pl.ds(0, EDGE), :].astype(F32), prev_ref)
    order = before(rows)
    blocks = rows // HEAD
    grams = []
    for n in range(per):
        s = conv_rows(kb_ref[n, pl.ds(0, rows), :].astype(F32), tops[n], taps, pad.at[n], slots)
        c, slope = silu(s)
        k, scale = unit(c)
        kn_ref[n] = k
        fk_ref[n] = scale * slope
        betas = beta_rows(kb_ref[n, pl.ds(rows, EDGE), :].astype(F32), slots)
        strength = 2.0 * sigmoid(column(betas, tokens, slots))
        k2 = two(k)
        grams.append(jnp.where(order, mm(k2, k2, ROWS_ROWS) * strength, 0.0))
    r, c = grid_of(HEAD, HEAD)
    eye = (r == c).astype(F32)
    zero = jnp.zeros((HEAD, HEAD), BF16)
    diagonal = [
        gram[b * HEAD : (b + 1) * HEAD, b * HEAD : (b + 1) * HEAD] for gram in grams for b in range(blocks)
    ]
    systems = [two(x) for x in diagonal]
    pairs = level_pairs(HEAD, 0)
    inverse = [eye - jnp.where(pairs, x, 0.0) for x in diagonal]
    level = 1
    while (1 << level) < HEAD:
        pairs = level_pairs(HEAD, level)
        split = [two(x) for x in inverse]
        crossed = [mm(tuple(jnp.where(pairs, p, zero) for p in s), x) for s, x in zip(systems, split)]
        inverse = [x - mm(s, two(y)) for x, s, y in zip(inverse, split, crossed)]
        level += 1
    for n in range(per):
        done = inverse[n * blocks : (n + 1) * blocks]
        size = HEAD
        while len(done) > 1:
            merged = []
            for b in range(0, len(done), 2):
                top, low = done[b], done[b + 1]
                cross = grams[n][(b + 1) * size : (b + 2) * size, b * size : (b + 1) * size]
                cross = mm(two(low), two(mm(two(cross), two(top))))
                merged.append(
                    jnp.concatenate(
                        [
                            jnp.concatenate([top, jnp.zeros_like(top)], axis=1),
                            jnp.concatenate([-cross, low], axis=1),
                        ],
                        axis=0,
                    )
                )
            done = merged
            size *= 2
        ti_ref[n] = done[0]


def maps_kernel(
    per, tokens, slots, hid, vq_ref, prev_ref, beta_ref, tail_ref, wts_ref, kn_ref, ti_ref,
    wu_ref, a_ref, mc_ref, fv_ref, end_ref, pad, carry,
):
    rows = tokens * slots
    taps = slot_taps(wts_ref[...], 1)
    ir, ic = grid_of(HEAD, 2 * HEAD)

    @pl.when(pl.program_id(0) == 0)
    def _():
        carry[...] = (ir == ic).astype(F32)

    tail = tail_ref[pl.ds(EDGE, EDGE), :].astype(F32)
    tops = edges(vq_ref, 0, rows, per, tail, prev_ref)
    maps = []
    for n in range(per):
        s = conv_rows(vq_ref[n, pl.ds(0, rows), :].astype(F32), tops[n], taps, pad.at[n], slots)
        v, fv_ref[n] = silu(s)
        betas = beta_rows(beta_ref[n].astype(F32), slots)
        strength = 2.0 * sigmoid(column(betas, tokens, slots))
        k = kn_ref[n]
        wu = mm(two(ti_ref[n]), two(strength * jnp.concatenate([k, v], axis=1)))
        wu_ref[n] = wu
        maps.append(mm(two(k), two(wu), COLS_COLS))
    state = carry[...]
    for n in range(per):
        mc_ref[n] = state
        a = (ir == ic)[:, :HEAD].astype(F32) - maps[n][:, :HEAD]
        a_ref[n] = a
        moved = mm(two(a), two(state))
        state = jnp.where(ic < HEAD, moved, moved + maps[n])
    carry[...] = state
    end_ref[...] = state


def queries_kernel(
    per, tokens, slots, hid, vq_ref, prev_ref, tail_ref, wts_ref, kn_ref, wu_ref,
    q_ref, sc_ref, qm_ref, ol_ref, fq_ref, pad,
):
    rows = tokens * slots
    taps = query_taps(wts_ref[...])
    tail = tail_ref[pl.ds(2 * EDGE, EDGE), :].astype(F32)
    tops = edges(vq_ref, rows, tokens, per, tail, prev_ref)
    seen = visible(tokens, slots)
    for n in range(per):
        s = conv_rows(vq_ref[n, pl.ds(rows, tokens), :].astype(F32), tops[n], taps, pad.at[n], 1)
        c, slope = silu(s)
        q, scale = unit(c)
        fq_ref[n] = scale * slope
        scores = jnp.where(seen, mm(two(q), two(kn_ref[n]), ROWS_ROWS), 0.0)
        mapped = mm(two(scores), two(wu_ref[n]))
        q_ref[n] = q
        sc_ref[n] = scores
        qm_ref[n] = q - mapped[:, :HEAD]
        ol_ref[n] = mapped[:, HEAD:]


def outs_kernel(
    per, count, tokens, slots, hid, vq_ref, wts_ref, start_ref, kn_ref, mc_ref, qm_ref, ol_ref, a_ref, wu_ref, q_ref,
    sc_ref, fq_ref, st_ref, mb_ref, d_ref, dk_ref, dd_ref, nq_ref, end_ref, pad, local,
):
    step = pl.program_id(0)
    rows = tokens * slots
    wts = wts_ref[...]
    gain = gain_row(wts)
    taps = query_taps(wts)
    seen = visible(tokens, slots)
    start = two(start_ref[...])
    states = [mm(two(mc_ref[n, :, pl.ds(0, HEAD)]), start) + mc_ref[n, :, pl.ds(HEAD, HEAD)] for n in range(per)]
    halves = [two(x) for x in states]
    mapped = [two(qm_ref[n]) for n in range(per)]
    raws = [mm(mapped[n], halves[n]) + ol_ref[n] for n in range(per)]
    for n in range(per):
        st_ref[n] = states[n]
        raw, state = raws[n], halves[n]
        scale = lax.rsqrt(jnp.mean(raw * raw, axis=-1, keepdims=True) + EPS)
        hat = raw * scale
        nq_ref[n, pl.ds(0, tokens), :] = (hat * gain).astype(BF16)
        dn = vq_ref[n, pl.ds(rows + tokens, tokens), :].astype(F32) * gain
        dr = two(scale * (dn - hat * jnp.mean(dn * hat, axis=-1, keepdims=True)))
        local[step * per + n] = mm(mapped[n], dr, COLS_COLS)
        q, k2 = q_ref[n], two(kn_ref[n])
        d = wu_ref[n, :, pl.ds(HEAD, HEAD)] - mm(two(wu_ref[n, :, pl.ds(0, HEAD)]), state)
        d_ref[n] = d
        ds = two(jnp.where(seen, mm(dr, two(d), ROWS_ROWS), 0.0))
        dq = mm(dr, state, ROWS_ROWS) + mm(ds, k2)
        dk_ref[n] = mm(ds, two(q), COLS_COLS)
        dd_ref[n] = mm(two(sc_ref[n]), dr, COLS_COLS)
        inner, rim = conv_back(fq_ref[n] * (dq - q * jnp.sum(q * dq, axis=-1, keepdims=True)), taps, pad.at[n], 1)
        nq_ref[n, pl.ds(tokens, tokens), :] = inner.astype(BF16)
        nq_ref[n, pl.ds(2 * tokens, EDGE), :] = jnp.concatenate([rim, jnp.zeros((8, HEAD), F32)], axis=0).astype(BF16)

    @pl.when(step == pl.num_programs(0) - 1)
    def _():
        ir, ic = grid_of(HEAD, 2 * HEAD)
        state = (ir == ic).astype(F32)
        for n in range(count - 1, -1, -1):
            mb_ref[n] = state
            moved = mm(two(a_ref[n]), two(state), COLS_COLS)
            state = moved + jnp.concatenate([jnp.zeros((HEAD, HEAD), F32), local[n]], axis=1)
        end_ref[...] = state


def grads_kernel(
    per, tokens, slots, hid, beta_ref, wts_ref, end_ref, mb_ref, kn_ref, ti_ref, d_ref, dk_ref, dd_ref, st_ref,
    fk_ref, fv_ref, out_ref, pad,
):
    rows = tokens * slots
    wts = wts_ref[...]
    order = before(rows)
    end = two(end_ref[...])
    for n in range(per):
        k, d = kn_ref[n], d_ref[n]
        k2, d2 = two(k), two(d)
        g2 = two(mm(two(mb_ref[n, :, pl.ds(0, HEAD)]), end) + mb_ref[n, :, pl.ds(HEAD, HEAD)])
        y = mm(two(ti_ref[n]), two(dd_ref[n] + mm(k2, g2)), COLS_COLS)
        betas = beta_rows(beta_ref[n].astype(F32), slots)
        de = 2.0 * sigmoid(column(betas, tokens, slots)) * y
        de2 = two(de)
        dgram = jnp.where(order, mm(de2, d2, ROWS_ROWS), 0.0)
        dk = dk_ref[n] + mm(d2, g2, ROWS_ROWS) - mm(de2, two(st_ref[n]), ROWS_ROWS)
        dk = dk - mm(two(dgram + dgram.T), k2)
        along = jnp.sum(y * d, axis=1, keepdims=True)
        marks = []
        for j in range(slots):
            gb = jnp.sum(jnp.where(places(tokens, slots, j), along, 0.0), axis=0, keepdims=True) * sigmoid(-betas[j])
            high = gb.astype(BF16).astype(F32)
            marks += [high, gb - high]
        marks.append(jnp.zeros((EDGE - 2 * slots, tokens), F32))
        value, value_rim = conv_back(fv_ref[n] * de, slot_taps(wts, 1), pad.at[2 * n], slots)
        part = fk_ref[n] * (dk - k * jnp.sum(k * dk, axis=-1, keepdims=True))
        key, key_rim = conv_back(part, slot_taps(wts, 0), pad.at[2 * n + 1], slots)
        out_ref[n, pl.ds(0, rows), :] = key.astype(BF16)
        out_ref[n, pl.ds(rows, rows), :] = value.astype(BF16)
        out_ref[n, pl.ds(2 * rows, EDGE), :] = jnp.concatenate(marks, axis=0).astype(BF16)
        out_ref[n, pl.ds(2 * rows + EDGE, EDGE), :] = jnp.concatenate([key_rim, value_rim], axis=0).astype(BF16)


def unpack_kernel(tokens, slots, got_ref, rim_ref, gk_ref, gv_ref):
    rows = tokens * slots
    for a, out_ref in enumerate((gk_ref, gv_ref)):
        main = got_ref[0, pl.ds(a * rows, rows), :].astype(F32)
        last = main[rows - 8 :] + rim_ref[0, pl.ds(8 * a, 8), :].astype(F32)
        out_ref[...] = jnp.concatenate([main[: rows - 8], last], axis=0).reshape(tokens, slots, HEAD)


def unpack_query_kernel(tokens, got_ref, rim_ref, gq_ref):
    main = got_ref[0, pl.ds(tokens, tokens), :].astype(F32)
    last = main[tokens - 8 :] + rim_ref[0, pl.ds(0, 8), :].astype(F32)
    gq_ref[...] = jnp.concatenate([main[: tokens - 8], last], axis=0)


FAR = ("kn", "ti", "fk", "fv", "st", "mb", "d", "dk", "dd")


def call(kernel, hid, steps, live, ins, reads, outs, scratch=(), us=1.0, grant=24):
    def spec(shape, how):
        if how == "weights":
            return pl.BlockSpec((shape[0], HEAD), lambda i, h: (0, h[0]))
        if how is None:
            return pl.BlockSpec(shape, lambda i, h: (0,) * len(shape))
        if isinstance(how, tuple):
            kind, count, row = how
            if kind == "prev":
                return pl.BlockSpec((1, EDGE, HEAD), lambda i, h: (jnp.maximum(i * count - 1, 0), row // EDGE, 0))
            return pl.BlockSpec((count, EDGE, HEAD), lambda i, h: (i, row // EDGE, 0))
        return pl.BlockSpec((how,) + tuple(shape[1:]), lambda i, h: (i,) + (0,) * (len(shape) - 1))

    def home(name):
        return pltpu.HBM if name in FAR else pltpu.VMEM

    operands = [a for a, _ in ins]
    operands += [pltpu.with_memory_space_constraint(live[name], home(name)) for name, _ in reads]
    hows = [how for _, how in ins + reads]
    results = pl.pallas_call(
        kernel,
        grid_spec=pltpu.PrefetchScalarGridSpec(
            num_scalar_prefetch=1,
            grid=(steps,),
            in_specs=[spec(a.shape, how) for a, how in zip(operands, hows)],
            out_specs=[spec(shape, how) for _, shape, _, how in outs],
            scratch_shapes=list(scratch),
        ),
        out_shape=[
            jax.ShapeDtypeStruct(shape, dtype) if name is None else home(name)(shape, dtype)
            for name, shape, dtype, _ in outs
        ],
        compiler_params=pltpu.CompilerParams(dimension_semantics=("arbitrary",), vmem_limit_bytes=grant << 20),
        cost_estimate=pl.CostEstimate(flops=int(us * 1.1e9), bytes_accessed=1 << 16, transcendentals=0),
    )(hid, *operands)
    for (name, _, _, _), result in zip(outs, results):
        if name is not None:
            live[name] = result
    return [r for (name, _, _, _), r in zip(outs, results) if name is None]


def shards(
    query_in,
    key_in,
    value_in,
    beta_logit,
    query_conv,
    key_conv,
    value_conv,
    norm_gain,
    out_weight,
    grad_out,
):
    tokens, slots = key_in.shape[0], key_in.shape[1]
    width = query_in.shape[1]
    heads = width // HEAD
    shard_count = lax.axis_size("ctx")
    place = lax.axis_index("ctx")
    groups = shard_count // heads
    group_lists = [[b * heads + i for i in range(heads)] for b in range(groups)]
    rows = tokens * slots
    g = heads
    hid = (place % heads).astype(jnp.int32).reshape(1)

    def exchange(x):
        return lax.all_to_all(x, "ctx", 0, 0, axis_index_groups=group_lists, tiled=True)

    def by_head(x):
        return x.reshape(x.shape[0], heads, HEAD).transpose(1, 0, 2)

    def slots_by_head(x):
        return x.reshape(x.shape[0], slots, heads, HEAD).transpose(2, 0, 1, 3).reshape(heads, -1, HEAD)

    high = lax.reduce_precision(beta_logit, 8, 7)
    rest = beta_logit - high
    middle = lax.reduce_precision(rest, 8, 7)
    betas = jnp.stack([high, middle, rest - middle], axis=2)
    betas = betas.transpose(3, 1, 2, 0).reshape(heads, 3 * slots, tokens).astype(BF16)
    betas = jnp.pad(betas, ((0, 0), (0, EDGE - 3 * slots), (0, 0)))
    last = EDGE // slots
    kb = exchange(
        jnp.concatenate(
            [slots_by_head(key_in), betas, slots_by_head(value_in[-last:]), by_head(query_in[-EDGE:])], axis=1
        )
    )

    group = place // heads
    tail = jnp.concatenate([kb[g - 1, rows - EDGE : rows], kb[g - 1, rows + EDGE :]], axis=0)
    tail = lax.ppermute(tail, "ctx", [(i, i + heads) for i in range(shard_count - heads)])

    grad_normed = jnp.dot(grad_out, out_weight.T, preferred_element_type=F32).astype(BF16)
    vq = jnp.concatenate([slots_by_head(value_in), by_head(query_in), by_head(grad_normed)], axis=1)
    vq, tail = lax.optimization_barrier((vq, tail))
    vq = exchange(vq)

    wts = jnp.concatenate(
        [
            jnp.tile(key_conv, (1, 8 // slots, 1)).reshape(8 * TAPS, width),
            jnp.tile(value_conv, (1, 8 // slots, 1)).reshape(8 * TAPS, width),
            query_conv,
            norm_gain.reshape(1, width),
            jnp.zeros((3, width), F32),
        ],
        axis=0,
    )
    per = 2 if g % 2 == 0 else 1
    steps = g // per

    def pad(n):
        return [pltpu.VMEM((per, n + EDGE + 8, HEAD), F32)]

    def big(name, *shape, per=per):
        return (name, (g,) + shape, F32, per)

    live = {}
    wide = 4 if g % 4 == 0 else per
    call(
        functools.partial(inverse_kernel, wide, tokens, slots),
        hid,
        g // wide,
        live,
        [(kb, wide), (kb, ("prev", wide, rows - EDGE)), (tail, None), (wts, "weights")],
        [],
        [big("kn", rows, HEAD, per=wide), big("ti", rows, rows, per=wide), big("fk", rows, HEAD, per=wide)],
        scratch=[pltpu.VMEM((wide, rows + EDGE + 8, HEAD), F32)],
        us=9.0,
        grant=40,
    )
    beta = (kb, ("rows", per, rows))
    (end,) = call(
        functools.partial(maps_kernel, per, tokens, slots),
        hid,
        steps,
        live,
        [(vq, per), (vq, ("prev", per, rows - EDGE)), beta, (tail, None), (wts, "weights")],
        [("kn", per), ("ti", per)],
        [
            big("wu", rows, 2 * HEAD), big("a", HEAD, HEAD), big("mc", HEAD, 2 * HEAD), big("fv", rows, HEAD),
            (None, (HEAD, 2 * HEAD), F32, None),
        ],
        scratch=pad(rows) + [pltpu.VMEM((HEAD, 2 * HEAD), F32)],
        us=8.0,
    )

    def across(last, towards):
        if groups == 1:
            return jnp.zeros((HEAD, HEAD), F32)
        if groups == 2:
            moves = [(i, i + towards * heads) for i in range(shard_count) if 0 <= i + towards * heads < shard_count]
            return lax.ppermute(last[:, HEAD:], "ctx", moves)
        every = lax.all_gather(last, "ctx")
        head = place % heads
        ahead = group if towards > 0 else groups - 1 - group

        def advance(i, state):
            source = i if towards > 0 else groups - 1 - i
            item = lax.dynamic_index_in_dim(every, source * heads + head, 0, False)
            return jnp.dot(item[:, :HEAD], state, precision=lax.Precision.HIGHEST) + item[:, HEAD:]

        return lax.fori_loop(0, ahead, advance, jnp.zeros((HEAD, HEAD), F32))

    start = across(end, 1)
    call(
        functools.partial(queries_kernel, per, tokens, slots),
        hid,
        steps,
        live,
        [(vq, per), (vq, ("prev", per, rows + tokens - EDGE)), (tail, None), (wts, "weights")],
        [("kn", per), ("wu", per)],
        [
            big("q", tokens, HEAD), big("sc", tokens, rows), big("qm", tokens, HEAD), big("ol", tokens, HEAD),
            big("fq", tokens, HEAD),
        ],
        scratch=pad(tokens),
        us=8.0,
    )
    nq, back_end = call(
        functools.partial(outs_kernel, per, g, tokens, slots),
        hid,
        steps,
        live,
        [(vq, per), (wts, "weights"), (start, None)],
        [
            ("kn", per), ("mc", per), ("qm", per), ("ol", per), ("a", None), ("wu", per), ("q", per), ("sc", per),
            ("fq", per),
        ],
        [
            big("st", HEAD, HEAD), big("mb", HEAD, 2 * HEAD, per=None), big("d", rows, HEAD), big("dk", rows, HEAD),
            big("dd", rows, HEAD), (None, (g, 2 * tokens + EDGE, HEAD), BF16, per), (None, (HEAD, 2 * HEAD), F32, None),
        ],
        scratch=pad(tokens) + [pltpu.VMEM((g, HEAD, HEAD), F32)],
        us=10.0,
    )
    finish = across(back_end, -1)
    nq = exchange(nq)
    (grads,) = call(
        functools.partial(grads_kernel, per, tokens, slots),
        hid,
        steps,
        live,
        [beta, (wts, "weights"), (finish, None)],
        [(name, per) for name in ("mb", "kn", "ti", "d", "dk", "dd", "st", "fk", "fv")],
        [(None, (g, 2 * rows + 2 * EDGE, HEAD), BF16, per)],
        scratch=[pltpu.VMEM((2 * per, rows + EDGE + 8, HEAD), F32)],
        us=20.0,
    )
    grads = exchange(grads)

    normed_bf = nq[:, :tokens].transpose(1, 0, 2).reshape(tokens, width)
    partial = jnp.dot(normed_bf, out_weight, preferred_element_type=F32)
    if lax.axis_size("head") == 2:
        half = tokens // 2
        mine = lax.axis_index("head")
        pieces = partial.reshape(2, half, partial.shape[1])
        kept = lax.dynamic_index_in_dim(pieces, mine, 0, False)
        sent = lax.dynamic_index_in_dim(pieces, 1 - mine, 0, False).astype(BF16)
        layer_out = (kept + lax.ppermute(sent, "head", [(0, 1), (1, 0)]).astype(F32)).astype(BF16)
    else:
        layer_out = lax.psum_scatter(partial.astype(BF16), "head", scatter_dimension=0, tiled=True)

    back = [(i, i - 1) for i in range(1, shard_count)]
    query_rim = lax.ppermute(nq[:, 2 * tokens :], "ctx", back)
    rim = lax.ppermute(grads[:, 2 * rows + EDGE :], "ctx", back)
    part = lambda x: pl.BlockSpec((1,) + x.shape[1:], lambda h: (h, 0, 0))
    grad_query = pl.pallas_call(
        functools.partial(unpack_query_kernel, tokens),
        grid=(heads,),
        in_specs=[part(nq), part(query_rim)],
        out_specs=pl.BlockSpec((tokens, HEAD), lambda h: (0, h)),
        out_shape=jax.ShapeDtypeStruct((tokens, width), F32),
        compiler_params=pltpu.CompilerParams(vmem_limit_bytes=8 << 20),
    )(nq, query_rim)
    grad_key, grad_value = pl.pallas_call(
        functools.partial(unpack_kernel, tokens, slots),
        grid=(heads,),
        in_specs=[part(grads), part(rim)],
        out_specs=[pl.BlockSpec((tokens, slots, HEAD), lambda h: (0, 0, h))] * 2,
        out_shape=[jax.ShapeDtypeStruct((tokens, slots, width), F32)] * 2,
        compiler_params=pltpu.CompilerParams(vmem_limit_bytes=8 << 20),
    )(grads, rim)
    marks = grads[:, 2 * rows : 2 * rows + 2 * slots].astype(F32)
    grad_beta = marks.reshape(heads, slots, 2, tokens).sum(axis=2).transpose(2, 1, 0)
    return (layer_out, grad_query, grad_key, grad_value, grad_beta)


def solution(mesh):
    placed = (
        P("ctx", "head"),
        P("ctx", None, "head"),
        P("ctx", None, "head"),
        P("ctx", None, "head"),
        P(None, "head"),
        P(None, None, "head"),
        P(None, None, "head"),
        P("head"),
        P("head", None),
        P("ctx", None),
    )
    return jax.shard_map(
        shards,
        mesh=mesh,
        in_specs=placed,
        out_specs=(
            P(("ctx", "head"), None),
            P("ctx", "head"),
            P("ctx", None, "head"),
            P("ctx", None, "head"),
            P("ctx", None, "head"),
        ),
        check_vma=False,
    )
```

```python
import functools

import jax
import jax.numpy as jnp
from jax import lax
from jax.experimental import pallas as pl
from jax.experimental.pallas import tpu as pltpu
from jax.sharding import PartitionSpec as P

HEAD = 128
TAPS = 4
RIM = TAPS - 1
EDGE = 16
EPS = 1e-06
F32 = jnp.float32
BF16 = jnp.bfloat16

ROWS_COLS = (((1,), (0,)), ((), ()))
ROWS_ROWS = (((1,), (1,)), ((), ()))
COLS_COLS = (((0,), (0,)), ((), ()))


def two(x):
    high = x.astype(BF16)
    return high, (x - high.astype(F32)).astype(BF16)


def dot(a, b, dims):
    return lax.dot_general(a, b, dims, preferred_element_type=F32)


def mm(left, right, dims=ROWS_COLS):
    (ah, al), (bh, bl) = left, right
    ka, kb = dims[0][0][0], dims[0][1][0]
    nb = 1 - kb
    depth, cols = ah.shape[ka], bh.shape[nb]
    if depth <= HEAD:
        a = jnp.concatenate([ah, al], axis=ka)
        high, low = jnp.concatenate([bh, bh], axis=kb), jnp.concatenate([bl, bl], axis=kb)
        if cols <= HEAD:
            out = dot(a, jnp.concatenate([high, low], axis=nb), dims)
            return out[:, :cols] + out[:, cols:]
        return dot(a, high, dims) + dot(a, low, dims)
    if cols <= HEAD:
        out = dot(ah, jnp.concatenate([bh, bl], axis=nb), dims)
        return out[:, :cols] + out[:, cols:] + dot(al, bh, dims)
    return dot(ah, bh, dims) + dot(ah, bl, dims) + dot(al, bh, dims)


def mm_half(left, right, dims=ROWS_COLS):
    (ah, al), (bh, _) = left, right
    ka, kb = dims[0][0][0], dims[0][1][0]
    return dot(jnp.concatenate([ah, al], axis=ka), jnp.concatenate([bh, bh], axis=kb), dims)


def grid_of(rows, cols):
    return lax.broadcasted_iota(jnp.int32, (rows, cols), 0), lax.broadcasted_iota(jnp.int32, (rows, cols), 1)


def before(rows):
    r, c = grid_of(rows, rows)
    return c < r


def level_pairs(rows, level):
    r, c = grid_of(rows, rows)
    return ((r >> (level + 1)) == (c >> (level + 1))) & (((r >> level) & 1) == 1) & (((c >> level) & 1) == 0)


def visible(tokens, slots):
    t, c = grid_of(tokens, tokens * slots)
    return c < slots * (t + 1)


def times(pattern, x):
    if pattern.shape[0] == 1:
        return pattern * x
    return (x.reshape(-1, 8, HEAD) * pattern[None]).reshape(x.shape)


def conv_rows(x, edge, taps, pad, stride):
    rows = x.shape[0]
    pad[pl.ds(0, EDGE), :] = edge
    pad[pl.ds(EDGE, rows), :] = x
    total = None
    for i in range(TAPS):
        part = times(taps[i], pad[pl.ds(EDGE - stride * (RIM - i), rows), :])
        total = part if total is None else total + part
    return total


def conv_back(grad, taps, pad, stride):
    rows = grad.shape[0]
    pad[pl.ds(8, 8), :] = jnp.zeros((8, HEAD), F32)
    pad[pl.ds(EDGE, rows), :] = grad
    pad[pl.ds(EDGE + rows, 8), :] = jnp.zeros((8, HEAD), F32)
    inner, rim = None, None
    for i in range(TAPS):
        part = times(taps[i], pad[pl.ds(EDGE + stride * (RIM - i), rows), :])
        edge = times(taps[i], pad[pl.ds(8 + stride * (RIM - i), 8), :])
        inner = part if inner is None else inner + part
        rim = edge if rim is None else rim + edge
    return inner, rim


def sigmoid(x):
    return 1.0 / (1.0 + jnp.exp(-x))


def silu(s):
    sg = sigmoid(s)
    return s * sg, sg * (1.0 + s * (1.0 - sg))


def unit(values):
    scale = lax.rsqrt(jnp.sum(values * values, axis=-1, keepdims=True) + EPS)
    return values * scale, scale


def beta_rows(tile, slots):
    return [tile[3 * j : 3 * j + 1] + tile[3 * j + 1 : 3 * j + 2] + tile[3 * j + 2 : 3 * j + 3] for j in range(slots)]


def places(tokens, slots, j):
    r, t = grid_of(tokens * slots, tokens)
    return r == slots * t + j


def column(rows, tokens, slots):
    spread = jnp.zeros((tokens * slots, tokens), F32)
    for j in range(slots):
        spread = jnp.where(places(tokens, slots, j), rows[j], spread)
    return jnp.sum(spread, axis=1, keepdims=True)


def slot_taps(wts, kind):
    return [wts[8 * (TAPS * kind + i) : 8 * (TAPS * kind + i + 1)] for i in range(TAPS)]


def query_taps(wts):
    return [wts[16 * TAPS + i : 16 * TAPS + i + 1] for i in range(TAPS)]


def gain_row(wts):
    return wts[17 * TAPS : 17 * TAPS + 1]


def edges(ref, first, rows, per, tail, prev_ref):
    prev = jnp.where(pl.program_id(0) == 0, tail, prev_ref[0].astype(F32))
    return [prev] + [ref[n, pl.ds(first + rows - EDGE, EDGE), :].astype(F32) for n in range(per - 1)]


def inverse_kernel(
    per, tokens, slots, hid, kb_ref, prev_ref, tail_ref, wts_ref,
    kh_ref, kl_ref, xh_ref, xl_ref, th_ref, tl_ref, wh_ref, wl_ref, fk_ref, a_ref, m_ref, end_ref, pad, carry,
):
    rows = tokens * slots
    step = pl.program_id(0)
    taps = slot_taps(wts_ref[...], 0)
    tops = edges(kb_ref, 0, rows, per, tail_ref[pl.ds(0, EDGE), :].astype(F32), prev_ref)
    order = before(rows)
    blocks = rows // HEAD
    ir, ic = grid_of(HEAD, HEAD)

    @pl.when(step == 0)
    def _():
        carry[...] = (ir == ic).astype(F32)

    grams, keys, scaled = [], [], []
    for n in range(per):
        s = conv_rows(kb_ref[n, pl.ds(0, rows), :].astype(F32), tops[n], taps, pad.at[n], slots)
        c, slope = silu(s)
        k, scale = unit(c)
        fk_ref[n] = scale * slope
        betas = beta_rows(kb_ref[n, pl.ds(rows, EDGE), :].astype(F32), slots)
        strength = 2.0 * sigmoid(column(betas, tokens, slots))
        k2 = two(k)
        kh_ref[n], kl_ref[n] = k2
        keys.append(k2)
        scaled.append(two(strength * k))
        grams.append(jnp.where(order, mm(k2, k2, ROWS_ROWS) * strength, 0.0))
    eye = (ir == ic).astype(F32)
    zero = jnp.zeros((HEAD, HEAD), BF16)
    diagonal = [
        gram[b * HEAD : (b + 1) * HEAD, b * HEAD : (b + 1) * HEAD] for gram in grams for b in range(blocks)
    ]
    systems = [two(x) for x in diagonal]
    pairs = level_pairs(HEAD, 0)
    inverse = [eye - jnp.where(pairs, x, 0.0) for x in diagonal]
    level = 1
    while (1 << level) < HEAD:
        pairs = level_pairs(HEAD, level)
        split = [two(x) for x in inverse]
        crossed = [mm(tuple(jnp.where(pairs, p, zero) for p in s), x) for s, x in zip(systems, split)]
        inverse = [x - mm(s, two(y)) for x, s, y in zip(inverse, split, crossed)]
        level += 1
    for n in range(per):
        done = inverse[n * blocks : (n + 1) * blocks]
        size = HEAD
        while len(done) > 1:
            merged = []
            for b in range(0, len(done), 2):
                top, low = done[b], done[b + 1]
                cross = grams[n][(b + 1) * size : (b + 2) * size, b * size : (b + 1) * size]
                cross = mm(two(low), two(mm(two(cross), two(top))))
                merged.append(
                    jnp.concatenate(
                        [
                            jnp.concatenate([top, jnp.zeros_like(top)], axis=1),
                            jnp.concatenate([-cross, low], axis=1),
                        ],
                        axis=0,
                    )
                )
            done = merged
            size *= 2
        x2 = two(done[0])
        xh_ref[n], xl_ref[n] = x2
        th_ref[n], tl_ref[n] = x2[0].T, x2[1].T
        w2 = two(mm(x2, scaled[n]))
        wh_ref[n], wl_ref[n] = w2
        a_ref[n] = eye - mm(keys[n], w2, COLS_COLS)
    state = carry[...]
    for n in range(per):
        m_ref[n] = state
        state = mm(two(a_ref[n]), two(state))
    carry[...] = state
    end_ref[...] = state


def maps_kernel(
    per, tokens, slots, hid, vq_ref, prev_ref, beta_ref, tail_ref, wts_ref, kh_ref, kl_ref, xh_ref, xl_ref, a_ref,
    m_ref,
    u_ref, c_ref, an_ref, mn_ref, fv_ref, end_ref, pad, carry,
):
    rows = tokens * slots
    taps = slot_taps(wts_ref[...], 1)

    @pl.when(pl.program_id(0) == 0)
    def _():
        carry[...] = jnp.zeros((HEAD, HEAD), F32)

    tail = tail_ref[pl.ds(EDGE, EDGE), :].astype(F32)
    tops = edges(vq_ref, 0, rows, per, tail, prev_ref)
    maps = []
    for n in range(per):
        s = conv_rows(vq_ref[n, pl.ds(0, rows), :].astype(F32), tops[n], taps, pad.at[n], slots)
        v, fv_ref[n] = silu(s)
        betas = beta_rows(beta_ref[n].astype(F32), slots)
        strength = 2.0 * sigmoid(column(betas, tokens, slots))
        u = mm((xh_ref[n], xl_ref[n]), two(strength * v))
        u_ref[n] = u
        maps.append(mm((kh_ref[n], kl_ref[n]), two(u), COLS_COLS))
    state = carry[...]
    for n in range(per):
        c_ref[n] = state
        an_ref[n], mn_ref[n] = a_ref[n], m_ref[n]
        state = mm(two(a_ref[n]), two(state)) + maps[n]
    carry[...] = state
    end_ref[...] = state


def queries_kernel(
    per, tokens, slots, hid, vq_ref, prev_ref, tail_ref, wts_ref, kh_ref, kl_ref, wh_ref, wl_ref, u_ref,
    q_ref, sc_ref, qm_ref, ol_ref, fq_ref, pad,
):
    rows = tokens * slots
    taps = query_taps(wts_ref[...])
    tail = tail_ref[pl.ds(2 * EDGE, EDGE), :].astype(F32)
    tops = edges(vq_ref, rows, tokens, per, tail, prev_ref)
    seen = visible(tokens, slots)
    for n in range(per):
        s = conv_rows(vq_ref[n, pl.ds(rows, tokens), :].astype(F32), tops[n], taps, pad.at[n], 1)
        c, slope = silu(s)
        q, scale = unit(c)
        fq_ref[n] = scale * slope
        scores = jnp.where(seen, mm(two(q), (kh_ref[n], kl_ref[n]), ROWS_ROWS), 0.0)
        uh, ul = two(u_ref[n])
        both = jnp.concatenate([wh_ref[n], uh], axis=1), jnp.concatenate([wl_ref[n], ul], axis=1)
        mapped = mm(two(scores), both)
        q_ref[n] = q
        sc_ref[n] = scores
        qm_ref[n] = q - mapped[:, :HEAD]
        ol_ref[n] = mapped[:, HEAD:]


def outs_kernel(
    per, tokens, slots, hid, vq_ref, wts_ref, start_ref, m_ref, c_ref, qm_ref, ol_ref, a_ref,
    st_ref, dr_ref, mb_ref, nm_ref, end_ref,
):
    rows = tokens * slots
    gain = gain_row(wts_ref[...])
    start = two(start_ref[...])
    states = [mm(two(m_ref[n]), start) + c_ref[n] for n in range(per)]
    mapped = [two(qm_ref[n]) for n in range(per)]
    raws = [mm(mapped[n], two(states[n])) + ol_ref[n] for n in range(per)]
    local = []
    for n in range(per):
        st_ref[n] = states[n]
        raw = raws[n]
        scale = lax.rsqrt(jnp.mean(raw * raw, axis=-1, keepdims=True) + EPS)
        hat = raw * scale
        nm_ref[n] = (hat * gain).astype(BF16)
        dn = vq_ref[n, pl.ds(rows + tokens, tokens), :].astype(F32) * gain
        dr = scale * (dn - hat * jnp.mean(dn * hat, axis=-1, keepdims=True))
        dr_ref[n] = dr
        local.append(mm(mapped[n], two(dr), COLS_COLS))
    ir, ic = grid_of(HEAD, 2 * HEAD)
    state = (ir == ic).astype(F32)
    for n in range(per - 1, -1, -1):
        mb_ref[n] = state
        moved = mm(two(a_ref[n]), two(state), COLS_COLS)
        state = moved + jnp.concatenate([jnp.zeros((HEAD, HEAD), F32), local[n]], axis=1)
    end_ref[...] = state


def query_grads_kernel(
    per, tokens, slots, hid, wts_ref, nm_ref, kh_ref, kl_ref, wh_ref, wl_ref, u_ref, q_ref, sc_ref, dr_ref, st_ref,
    fq_ref, mb_ref, d_ref, dk_ref, dd_ref, stf_ref, mbf_ref, nq_ref, pad,
):
    taps = query_taps(wts_ref[...])
    seen = visible(tokens, slots)
    for n in range(per):
        q, k2 = q_ref[n], (kh_ref[n], kl_ref[n])
        stf_ref[n], mbf_ref[n] = st_ref[n], mb_ref[n]
        state, dr = two(st_ref[n]), two(dr_ref[n])
        d = u_ref[n] - mm((wh_ref[n], wl_ref[n]), state)
        d_ref[n] = d
        ds = two(jnp.where(seen, mm(dr, two(d), ROWS_ROWS), 0.0))
        dq = mm(dr, state, ROWS_ROWS) + mm(ds, k2)
        dk_ref[n] = mm(ds, two(q), COLS_COLS)
        dd_ref[n] = mm(two(sc_ref[n]), dr, COLS_COLS)
        inner, rim = conv_back(fq_ref[n] * (dq - q * jnp.sum(q * dq, axis=-1, keepdims=True)), taps, pad.at[n], 1)
        nq_ref[n, pl.ds(0, tokens), :] = nm_ref[n]
        nq_ref[n, pl.ds(tokens, tokens), :] = inner.astype(BF16)
        nq_ref[n, pl.ds(2 * tokens, EDGE), :] = jnp.concatenate([rim, jnp.zeros((8, HEAD), F32)], axis=0).astype(BF16)


def grads_kernel(
    per, tokens, slots, hid, beta_ref, wts_ref, end_ref, mb_ref, kh_ref, kl_ref, th_ref, tl_ref, d_ref, dk_ref, dd_ref,
    st_ref, fk_ref, fv_ref, out_ref, pad,
):
    rows = tokens * slots
    wts = wts_ref[...]
    order = before(rows)
    end = two(end_ref[...])
    for n in range(per):
        d, k2 = d_ref[n], (kh_ref[n], kl_ref[n])
        d2 = two(d)
        k = k2[0].astype(F32) + k2[1].astype(F32)
        g2 = two(mm(two(mb_ref[n, :, pl.ds(0, HEAD)]), end) + mb_ref[n, :, pl.ds(HEAD, HEAD)])
        y = mm((th_ref[n], tl_ref[n]), two(dd_ref[n] + mm(k2, g2)))
        betas = beta_rows(beta_ref[n].astype(F32), slots)
        de = 2.0 * sigmoid(column(betas, tokens, slots)) * y
        de2 = two(de)
        dgram = jnp.where(order, mm_half(de2, d2, ROWS_ROWS), 0.0)
        dk = dk_ref[n] + mm(d2, g2, ROWS_ROWS) - mm(de2, two(st_ref[n]), ROWS_ROWS)
        dk = dk - mm(two(dgram + dgram.T), k2)
        along = jnp.sum(y * d, axis=1, keepdims=True)
        marks = []
        for j in range(slots):
            gb = jnp.sum(jnp.where(places(tokens, slots, j), along, 0.0), axis=0, keepdims=True) * sigmoid(-betas[j])
            high = gb.astype(BF16).astype(F32)
            marks += [high, gb - high]
        marks.append(jnp.zeros((EDGE - 2 * slots, tokens), F32))
        value, value_rim = conv_back(fv_ref[n] * de, slot_taps(wts, 1), pad.at[2 * n], slots)
        part = fk_ref[n] * (dk - k * jnp.sum(k * dk, axis=-1, keepdims=True))
        key, key_rim = conv_back(part, slot_taps(wts, 0), pad.at[2 * n + 1], slots)
        out_ref[n, pl.ds(0, rows), :] = key.astype(BF16)
        out_ref[n, pl.ds(rows, rows), :] = value.astype(BF16)
        out_ref[n, pl.ds(2 * rows, EDGE), :] = jnp.concatenate(marks, axis=0).astype(BF16)
        out_ref[n, pl.ds(2 * rows + EDGE, EDGE), :] = jnp.concatenate([key_rim, value_rim], axis=0).astype(BF16)


def unpack_kernel(tokens, slots, got_ref, gk_ref, gv_ref):
    rows = tokens * slots
    for a, out_ref in enumerate((gk_ref, gv_ref)):
        out_ref[...] = got_ref[0, pl.ds(a * rows, rows), :].astype(F32).reshape(tokens, slots, HEAD)


def unpack_query_kernel(tokens, got_ref, gq_ref):
    gq_ref[...] = got_ref[0, pl.ds(tokens, tokens), :].astype(F32)


def rims_kernel(heads, slots, rim_ref, gq_ref, gk_ref, gv_ref, nq_ref, nk_ref, nv_ref):
    for h in range(heads):
        part = pl.ds(h * HEAD, HEAD)
        rim = rim_ref[h].astype(F32)
        nq_ref[:, part] = gq_ref[:, part] + rim[:8]
        nk_ref[:, :, part] = gk_ref[:, :, part] + rim[8:16].reshape(8 // slots, slots, HEAD)
        nv_ref[:, :, part] = gv_ref[:, :, part] + rim[16:].reshape(8 // slots, slots, HEAD)


FAR = ("kh", "kl", "xh", "xl", "th", "tl", "wh", "wl", "a", "m", "fk", "fv", "stf", "mbf", "d", "dk", "dd")


def call(kernel, hid, steps, live, ins, reads, outs, scratch=(), us=1.0, grant=24):
    def spec(shape, how):
        if how == "weights":
            return pl.BlockSpec((shape[0], HEAD), lambda i, h: (0, h[0]))
        if how is None:
            return pl.BlockSpec(shape, lambda i, h: (0,) * len(shape))
        if isinstance(how, tuple):
            kind, count, row = how
            if kind == "prev":
                return pl.BlockSpec((1, EDGE, HEAD), lambda i, h: (jnp.maximum(i * count - 1, 0), row // EDGE, 0))
            return pl.BlockSpec((count, EDGE, HEAD), lambda i, h: (i, row // EDGE, 0))
        return pl.BlockSpec((how,) + tuple(shape[1:]), lambda i, h: (i,) + (0,) * (len(shape) - 1))

    def home(name):
        return pltpu.HBM if name in FAR else pltpu.VMEM

    operands = [a for a, _ in ins]
    operands += [pltpu.with_memory_space_constraint(live[name], home(name)) for name, _ in reads]
    hows = [how for _, how in ins + reads]
    results = pl.pallas_call(
        kernel,
        grid_spec=pltpu.PrefetchScalarGridSpec(
            num_scalar_prefetch=1,
            grid=(steps,),
            in_specs=[spec(a.shape, how) for a, how in zip(operands, hows)],
            out_specs=[spec(shape, how) for _, shape, _, how in outs],
            scratch_shapes=list(scratch),
        ),
        out_shape=[
            jax.ShapeDtypeStruct(shape, dtype) if name is None else home(name)(shape, dtype)
            for name, shape, dtype, _ in outs
        ],
        compiler_params=pltpu.CompilerParams(dimension_semantics=("arbitrary",), vmem_limit_bytes=grant << 20),
        cost_estimate=pl.CostEstimate(flops=int(us * 1.1e9), bytes_accessed=1 << 16, transcendentals=0),
    )(hid, *operands)
    for (name, _, _, _), result in zip(outs, results):
        if name is not None:
            live[name] = result
    return [r for (name, _, _, _), r in zip(outs, results) if name is None]


def shards(
    query_in,
    key_in,
    value_in,
    beta_logit,
    query_conv,
    key_conv,
    value_conv,
    norm_gain,
    out_weight,
    grad_out,
):
    tokens, slots = key_in.shape[0], key_in.shape[1]
    width = query_in.shape[1]
    heads = width // HEAD
    shard_count = lax.axis_size("ctx")
    place = lax.axis_index("ctx")
    groups = shard_count // heads
    group_lists = [[b * heads + i for i in range(heads)] for b in range(groups)]
    rows = tokens * slots
    g = heads
    hid = (place % heads).astype(jnp.int32).reshape(1)

    def exchange(x):
        return lax.all_to_all(x, "ctx", 0, 0, axis_index_groups=group_lists, tiled=True)

    def by_head(x):
        return x.reshape(x.shape[0], heads, HEAD).transpose(1, 0, 2)

    def slots_by_head(x):
        return x.reshape(x.shape[0], slots, heads, HEAD).transpose(2, 0, 1, 3).reshape(heads, -1, HEAD)

    high = lax.reduce_precision(beta_logit, 8, 7)
    rest = beta_logit - high
    middle = lax.reduce_precision(rest, 8, 7)
    betas = jnp.stack([high, middle, rest - middle], axis=2)
    betas = betas.transpose(3, 1, 2, 0).reshape(heads, 3 * slots, tokens).astype(BF16)
    betas = jnp.pad(betas, ((0, 0), (0, EDGE - 3 * slots), (0, 0)))
    last = EDGE // slots
    kb = exchange(
        jnp.concatenate(
            [slots_by_head(key_in), betas, slots_by_head(value_in[-last:]), by_head(query_in[-EDGE:])], axis=1
        )
    )

    group = place // heads
    tail = jnp.concatenate([kb[g - 1, rows - EDGE : rows], kb[g - 1, rows + EDGE :]], axis=0)
    tail = lax.ppermute(tail, "ctx", [(i, i + heads) for i in range(shard_count - heads)])

    grad_normed = jnp.dot(grad_out, out_weight.T, preferred_element_type=F32).astype(BF16)
    vq = jnp.concatenate([slots_by_head(value_in), by_head(query_in), by_head(grad_normed)], axis=1)
    vq, tail = lax.optimization_barrier((vq, tail))
    vq = exchange(vq)

    wts = jnp.concatenate(
        [
            jnp.tile(key_conv, (1, 8 // slots, 1)).reshape(8 * TAPS, width),
            jnp.tile(value_conv, (1, 8 // slots, 1)).reshape(8 * TAPS, width),
            query_conv,
            norm_gain.reshape(1, width),
            jnp.zeros((3, width), F32),
        ],
        axis=0,
    )
    per = 2 if g % 2 == 0 else 1
    steps = g // per

    def pad(n):
        return [pltpu.VMEM((per, n + EDGE + 8, HEAD), F32)]

    def big(name, *shape, per=per, kind=F32):
        return (name, (g,) + shape, kind, per)

    live = {}
    wide = 4 if g % 4 == 0 else per
    (m_end,) = call(
        functools.partial(inverse_kernel, wide, tokens, slots),
        hid,
        g // wide,
        live,
        [(kb, wide), (kb, ("prev", wide, rows - EDGE)), (tail, None), (wts, "weights")],
        [],
        [big(name, rows, HEAD, per=wide, kind=BF16) for name in ("kh", "kl")]
        + [big(name, rows, rows, per=wide, kind=BF16) for name in ("xh", "xl", "th", "tl")]
        + [big(name, rows, HEAD, per=wide, kind=BF16) for name in ("wh", "wl")]
        + [
            big("fk", rows, HEAD, per=wide), big("a", HEAD, HEAD, per=wide), big("m", HEAD, HEAD, per=wide),
            (None, (HEAD, HEAD), F32, None),
        ],
        scratch=[pltpu.VMEM((wide, rows + EDGE + 8, HEAD), F32), pltpu.VMEM((HEAD, HEAD), F32)],
        us=11.0,
        grant=40,
    )
    beta = (kb, ("rows", per, rows))
    (c_end,) = call(
        functools.partial(maps_kernel, per, tokens, slots),
        hid,
        steps,
        live,
        [(vq, per), (vq, ("prev", per, rows - EDGE)), beta, (tail, None), (wts, "weights")],
        [(name, per) for name in ("kh", "kl", "xh", "xl", "a", "m")],
        [
            big("u", rows, HEAD), big("c", HEAD, HEAD), big("an", HEAD, HEAD), big("mn", HEAD, HEAD),
            big("fv", rows, HEAD), (None, (HEAD, HEAD), F32, None),
        ],
        scratch=pad(rows) + [pltpu.VMEM((HEAD, HEAD), F32)],
        us=6.0,
    )

    def across(last, towards):
        if groups == 1:
            return jnp.zeros((HEAD, HEAD), F32)
        if groups == 2:
            moves = [(i, i + towards * heads) for i in range(shard_count) if 0 <= i + towards * heads < shard_count]
            return lax.ppermute(last[1], "ctx", moves)
        every = lax.all_gather(jnp.concatenate(last, axis=1), "ctx")
        head = place % heads
        ahead = group if towards > 0 else groups - 1 - group

        def advance(i, state):
            source = i if towards > 0 else groups - 1 - i
            item = lax.dynamic_index_in_dim(every, source * heads + head, 0, False)
            return jnp.dot(item[:, :HEAD], state, precision=lax.Precision.HIGHEST) + item[:, HEAD:]

        return lax.fori_loop(0, ahead, advance, jnp.zeros((HEAD, HEAD), F32))

    start = across((m_end, c_end), 1)
    call(
        functools.partial(queries_kernel, per, tokens, slots),
        hid,
        steps,
        live,
        [(vq, per), (vq, ("prev", per, rows + tokens - EDGE)), (tail, None), (wts, "weights")],
        [(name, per) for name in ("kh", "kl", "wh", "wl", "u")],
        [
            big("q", tokens, HEAD), big("sc", tokens, rows), big("qm", tokens, HEAD), big("ol", tokens, HEAD),
            big("fq", tokens, HEAD),
        ],
        scratch=pad(tokens),
        us=8.0,
    )
    normed, back_end = call(
        functools.partial(outs_kernel, g, tokens, slots),
        hid,
        1,
        live,
        [(vq, g), (wts, "weights"), (start, None)],
        [(name, g) for name in ("mn", "c", "qm", "ol", "an")],
        [
            big("st", HEAD, HEAD, per=g), big("dr", tokens, HEAD, per=g), big("mb", HEAD, 2 * HEAD, per=g),
            (None, (g, tokens, HEAD), BF16, g), (None, (HEAD, 2 * HEAD), F32, None),
        ],
        us=4.0,
    )
    finish = across((back_end[:, :HEAD], back_end[:, HEAD:]), -1)
    (nq,) = call(
        functools.partial(query_grads_kernel, per, tokens, slots),
        hid,
        steps,
        live,
        [(wts, "weights"), (normed, per)],
        [(name, per) for name in ("kh", "kl", "wh", "wl", "u", "q", "sc", "dr", "st", "fq", "mb")],
        [
            big("d", rows, HEAD), big("dk", rows, HEAD), big("dd", rows, HEAD), big("stf", HEAD, HEAD),
            big("mbf", HEAD, 2 * HEAD), (None, (g, 2 * tokens + EDGE, HEAD), BF16, per),
        ],
        scratch=pad(tokens),
        us=20.0,
    )
    nq = exchange(nq)
    (grads,) = call(
        functools.partial(grads_kernel, per, tokens, slots),
        hid,
        steps,
        live,
        [beta, (wts, "weights"), (finish, None)],
        [(name, per) for name in ("mbf", "kh", "kl", "th", "tl", "d", "dk", "dd", "stf", "fk", "fv")],
        [(None, (g, 2 * rows + 2 * EDGE, HEAD), BF16, per)],
        scratch=[pltpu.VMEM((2 * per, rows + EDGE + 8, HEAD), F32)],
        us=20.0,
    )
    grads = exchange(grads)

    normed_bf = nq[:, :tokens].transpose(1, 0, 2).reshape(tokens, width)
    partial = jnp.dot(normed_bf, out_weight, preferred_element_type=F32)
    if lax.axis_size("head") == 2:
        half = tokens // 2
        mine = lax.axis_index("head")
        pieces = partial.reshape(2, half, partial.shape[1])
        kept = lax.dynamic_index_in_dim(pieces, mine, 0, False)
        sent = lax.dynamic_index_in_dim(pieces, 1 - mine, 0, False).astype(BF16)
        layer_out = (kept + lax.ppermute(sent, "head", [(0, 1), (1, 0)]).astype(F32)).astype(BF16)
    else:
        layer_out = lax.psum_scatter(partial.astype(BF16), "head", scatter_dimension=0, tiled=True)

    rim = jnp.concatenate([nq[:, 2 * tokens : 2 * tokens + 8], grads[:, 2 * rows + EDGE :]], axis=1)
    rim = lax.ppermute(rim, "ctx", [(i, i - 1) for i in range(1, shard_count)])
    part = lambda x: pl.BlockSpec((1,) + x.shape[1:], lambda h: (h, 0, 0))
    small = pltpu.CompilerParams(vmem_limit_bytes=8 << 20)
    cost = lambda us: pl.CostEstimate(flops=int(us * 1.1e9), bytes_accessed=1 << 16, transcendentals=0)
    grad_query = pl.pallas_call(
        functools.partial(unpack_query_kernel, tokens),
        grid=(heads,),
        in_specs=[part(nq)],
        out_specs=pl.BlockSpec((tokens, HEAD), lambda h: (0, h)),
        out_shape=jax.ShapeDtypeStruct((tokens, width), F32),
        compiler_params=small,
        cost_estimate=cost(2.0),
    )(nq)
    grad_key, grad_value = pl.pallas_call(
        functools.partial(unpack_kernel, tokens, slots),
        grid=(heads,),
        in_specs=[part(grads)],
        out_specs=[pl.BlockSpec((tokens, slots, HEAD), lambda h: (0, 0, h))] * 2,
        out_shape=[jax.ShapeDtypeStruct((tokens, slots, width), F32)] * 2,
        compiler_params=small,
        cost_estimate=cost(10.0),
    )(grads)
    flat = pl.BlockSpec((8, width), lambda i: (tokens // 8 - 1, 0))
    deep = pl.BlockSpec((8 // slots, slots, width), lambda i: (tokens * slots // 8 - 1, 0, 0))
    grad_query, grad_key, grad_value = pl.pallas_call(
        functools.partial(rims_kernel, heads, slots),
        grid=(1,),
        in_specs=[pl.BlockSpec(rim.shape, lambda i: (0, 0, 0)), flat, deep, deep],
        out_specs=[flat, deep, deep],
        out_shape=[jax.ShapeDtypeStruct(x.shape, F32) for x in (grad_query, grad_key, grad_value)],
        input_output_aliases={1: 0, 2: 1, 3: 2},
        compiler_params=small,
    )(rim, grad_query, grad_key, grad_value)
    marks = grads[:, 2 * rows : 2 * rows + 2 * slots].astype(F32)
    grad_beta = marks.reshape(heads, slots, 2, tokens).sum(axis=2).transpose(2, 1, 0)
    return (layer_out, grad_query, grad_key, grad_value, grad_beta)


def solution(mesh):
    placed = (
        P("ctx", "head"),
        P("ctx", None, "head"),
        P("ctx", None, "head"),
        P("ctx", None, "head"),
        P(None, "head"),
        P(None, None, "head"),
        P(None, None, "head"),
        P("head"),
        P("head", None),
        P("ctx", None),
    )
    return jax.shard_map(
        shards,
        mesh=mesh,
        in_specs=placed,
        out_specs=(
            P(("ctx", "head"), None),
            P("ctx", "head"),
            P("ctx", None, "head"),
            P("ctx", None, "head"),
            P("ctx", None, "head"),
        ),
        check_vma=False,
    )
```

```python
import functools

import jax
import jax.numpy as jnp
from jax import lax
from jax.experimental import pallas as pl
from jax.experimental.pallas import tpu as pltpu
from jax.sharding import PartitionSpec as P

HEAD = 128
TAPS = 4
RIM = TAPS - 1
EDGE = 16
EPS = 1e-06
BEFORE = 1 << 16
AFTER = 1 << 17
F32 = jnp.float32
BF16 = jnp.bfloat16

ROWS_COLS = (((1,), (0,)), ((), ()))
ROWS_ROWS = (((1,), (1,)), ((), ()))
COLS_COLS = (((0,), (0,)), ((), ()))


def two(x):
    high = x.astype(BF16)
    return high, (x - high.astype(F32)).astype(BF16)


def dot(a, b, dims):
    return lax.dot_general(a, b, dims, preferred_element_type=F32)


def mm(left, right, dims=ROWS_COLS):
    (ah, al), (bh, bl) = left, right
    ka, kb = dims[0][0][0], dims[0][1][0]
    nb = 1 - kb
    depth, cols = ah.shape[ka], bh.shape[nb]
    if depth <= HEAD:
        a = jnp.concatenate([ah, al], axis=ka)
        high, low = jnp.concatenate([bh, bh], axis=kb), jnp.concatenate([bl, bl], axis=kb)
        if cols <= HEAD:
            out = dot(a, jnp.concatenate([high, low], axis=nb), dims)
            return out[:, :cols] + out[:, cols:]
        return dot(a, high, dims) + dot(a, low, dims)
    if cols <= HEAD:
        out = dot(ah, jnp.concatenate([bh, bl], axis=nb), dims)
        return out[:, :cols] + out[:, cols:] + dot(al, bh, dims)
    return dot(ah, bh, dims) + dot(ah, bl, dims) + dot(al, bh, dims)


def piece(x, row, col=None):
    cols = slice(None) if col is None else slice(col * HEAD, (col + 1) * HEAD)
    return tuple(p[row * HEAD : (row + 1) * HEAD, cols] for p in x)


def lower_times(x, b):
    count = x[0].shape[0] // HEAD
    return jnp.concatenate(
        [sum(mm(piece(x, i, j), piece(b, j)) for j in range(i + 1)) for i in range(count)], axis=0
    )


def mm_half(left, right, dims=ROWS_COLS):
    (ah, al), (bh, _) = left, right
    ka, kb = dims[0][0][0], dims[0][1][0]
    return dot(jnp.concatenate([ah, al], axis=ka), jnp.concatenate([bh, bh], axis=kb), dims)


def grid_of(rows, cols):
    return lax.broadcasted_iota(jnp.int32, (rows, cols), 0), lax.broadcasted_iota(jnp.int32, (rows, cols), 1)


def before(rows):
    r, c = grid_of(rows, rows)
    return c < r


def level_pairs(rows, level):
    r, c = grid_of(rows, rows)
    return ((r >> (level + 1)) == (c >> (level + 1))) & (((r >> level) & 1) == 1) & (((c >> level) & 1) == 0)


def visible(tokens, slots):
    t, c = grid_of(tokens, tokens * slots)
    return c < slots * (t + 1)


def times(pattern, x):
    if pattern.shape[0] == 1:
        return pattern * x
    return (x.reshape(-1, 8, HEAD) * pattern[None]).reshape(x.shape)


def conv_rows(x, edge, taps, pad, stride):
    rows = x.shape[0]
    pad[pl.ds(0, EDGE), :] = edge
    pad[pl.ds(EDGE, rows), :] = x
    total = None
    for i in range(TAPS):
        part = times(taps[i], pad[pl.ds(EDGE - stride * (RIM - i), rows), :])
        total = part if total is None else total + part
    return total


def conv_back(grad, taps, pad, stride):
    rows = grad.shape[0]
    pad[pl.ds(8, 8), :] = jnp.zeros((8, HEAD), F32)
    pad[pl.ds(EDGE, rows), :] = grad
    pad[pl.ds(EDGE + rows, 8), :] = jnp.zeros((8, HEAD), F32)
    inner, rim = None, None
    for i in range(TAPS):
        part = times(taps[i], pad[pl.ds(EDGE + stride * (RIM - i), rows), :])
        edge = times(taps[i], pad[pl.ds(8 + stride * (RIM - i), 8), :])
        inner = part if inner is None else inner + part
        rim = edge if rim is None else rim + edge
    return inner, rim


def sigmoid(x):
    return 1.0 / (1.0 + jnp.exp(-x))


def silu(s):
    sg = sigmoid(s)
    return s * sg, sg * (1.0 + s * (1.0 - sg))


def unit(values):
    scale = lax.rsqrt(jnp.sum(values * values, axis=-1, keepdims=True) + EPS)
    return values * scale, scale


def beta_rows(tile, slots):
    return [tile[3 * j : 3 * j + 1] + tile[3 * j + 1 : 3 * j + 2] + tile[3 * j + 2 : 3 * j + 3] for j in range(slots)]


def places(tokens, slots, j):
    r, t = grid_of(tokens * slots, tokens)
    return r == slots * t + j


def column(rows, tokens, slots):
    spread = jnp.zeros((tokens * slots, tokens), F32)
    for j in range(slots):
        spread = jnp.where(places(tokens, slots, j), rows[j], spread)
    return jnp.sum(spread, axis=1, keepdims=True)


def slot_taps(wts, kind):
    return [wts[8 * (TAPS * kind + i) : 8 * (TAPS * kind + i + 1)] for i in range(TAPS)]


def query_taps(wts):
    return [wts[16 * TAPS + i : 16 * TAPS + i + 1] for i in range(TAPS)]


def gain_row(wts):
    return wts[17 * TAPS : 17 * TAPS + 1]


def edges(hid, ref, first, rows, per, tail, prev_ref):
    tail = jnp.where((hid[0] & BEFORE) > 0, tail, 0.0)
    prev = jnp.where(pl.program_id(0) == 0, tail, prev_ref[0].astype(F32))
    return [prev] + [ref[n, pl.ds(first + rows - EDGE, EDGE), :].astype(F32) for n in range(per - 1)]


def inverse_kernel(
    per, tokens, slots, hid, kb_ref, prev_ref, tail_ref, wts_ref,
    kh_ref, kl_ref, xh_ref, xl_ref, th_ref, tl_ref, wh_ref, wl_ref, fk_ref, a_ref, m_ref, end_ref, pad, carry,
):
    rows = tokens * slots
    step = pl.program_id(0)
    taps = slot_taps(wts_ref[...], 0)
    tops = edges(hid, kb_ref, 0, rows, per, tail_ref[pl.ds(0, EDGE), :].astype(F32), prev_ref)
    order = before(HEAD)
    blocks = rows // HEAD
    ir, ic = grid_of(HEAD, HEAD)

    @pl.when(step == 0)
    def _():
        carry[...] = (ir == ic).astype(F32)

    grams, keys, scaled = [], [], []
    for n in range(per):
        s = conv_rows(kb_ref[n, pl.ds(0, rows), :].astype(F32), tops[n], taps, pad.at[n], slots)
        c, slope = silu(s)
        k, scale = unit(c)
        fk_ref[n] = scale * slope
        betas = beta_rows(kb_ref[n, pl.ds(rows, EDGE), :].astype(F32), slots)
        strength = 2.0 * sigmoid(column(betas, tokens, slots))
        k2 = two(k)
        kh_ref[n], kl_ref[n] = k2
        keys.append(k2)
        scaled.append(two(strength * k))
        gram = {}
        for i in range(blocks):
            for j in range(i + 1):
                part = mm(piece(k2, i), piece(k2, j), ROWS_ROWS) * strength[i * HEAD : (i + 1) * HEAD]
                gram[i, j] = jnp.where(order, part, 0.0) if i == j else part
        grams.append(gram)
    eye = (ir == ic).astype(F32)
    zero = jnp.zeros((HEAD, HEAD), BF16)
    diagonal = [gram[b, b] for gram in grams for b in range(blocks)]
    systems = [two(x) for x in diagonal]
    pairs = level_pairs(HEAD, 0)
    inverse = [eye - jnp.where(pairs, x, 0.0) for x in diagonal]
    level = 1
    while (1 << level) < HEAD:
        pairs = level_pairs(HEAD, level)
        split = [two(x) for x in inverse]
        crossed = [mm(tuple(jnp.where(pairs, p, zero) for p in s), x) for s, x in zip(systems, split)]
        inverse = [x - mm(s, two(y)) for x, s, y in zip(inverse, split, crossed)]
        level += 1
    for n in range(per):
        done = {(b, b): inverse[n * blocks + b] for b in range(blocks)}
        halves = {(b, b): two(done[b, b]) for b in range(blocks)}
        for j in range(blocks):
            for i in range(j + 1, blocks):
                cross = sum(mm(two(grams[n][i, m]), halves[m, j]) for m in range(j, i))
                done[i, j] = -mm(halves[i, i], two(cross))
                halves[i, j] = two(done[i, j])
        nothing = jnp.zeros((HEAD, HEAD), BF16)
        x2 = tuple(
            jnp.concatenate(
                [
                    jnp.concatenate([halves[i, j][p] if j <= i else nothing for j in range(blocks)], axis=1)
                    for i in range(blocks)
                ],
                axis=0,
            )
            for p in range(2)
        )
        xh_ref[n], xl_ref[n] = x2
        th_ref[n], tl_ref[n] = x2[0].T, x2[1].T
        w2 = two(lower_times(x2, scaled[n]))
        wh_ref[n], wl_ref[n] = w2
        a_ref[n] = eye - mm(keys[n], w2, COLS_COLS)
    state = carry[...]
    for n in range(per):
        m_ref[n] = state
        state = mm(two(a_ref[n]), two(state))
    carry[...] = state
    end_ref[...] = state


def maps_kernel(
    per, tokens, slots, hid, vq_ref, prev_ref, beta_ref, tail_ref, wts_ref, kh_ref, kl_ref, xh_ref, xl_ref, a_ref,
    m_ref,
    u_ref, c_ref, an_ref, mn_ref, fv_ref, end_ref, pad, carry,
):
    rows = tokens * slots
    taps = slot_taps(wts_ref[...], 1)

    @pl.when(pl.program_id(0) == 0)
    def _():
        carry[...] = jnp.zeros((HEAD, HEAD), F32)

    tail = tail_ref[pl.ds(EDGE, EDGE), :].astype(F32)
    tops = edges(hid, vq_ref, 0, rows, per, tail, prev_ref)
    maps = []
    for n in range(per):
        s = conv_rows(vq_ref[n, pl.ds(0, rows), :].astype(F32), tops[n], taps, pad.at[n], slots)
        v, fv_ref[n] = silu(s)
        betas = beta_rows(beta_ref[n].astype(F32), slots)
        strength = 2.0 * sigmoid(column(betas, tokens, slots))
        u = lower_times((xh_ref[n], xl_ref[n]), two(strength * v))
        u_ref[n] = u
        maps.append(mm((kh_ref[n], kl_ref[n]), two(u), COLS_COLS))
    state = carry[...]
    for n in range(per):
        c_ref[n] = state
        an_ref[n], mn_ref[n] = a_ref[n], m_ref[n]
        state = mm(two(a_ref[n]), two(state)) + maps[n]
    carry[...] = state
    end_ref[...] = state


def queries_kernel(
    per, tokens, slots, hid, vq_ref, prev_ref, tail_ref, wts_ref, kh_ref, kl_ref, wh_ref, wl_ref, u_ref,
    q_ref, sc_ref, qm_ref, ol_ref, fq_ref, pad,
):
    rows = tokens * slots
    taps = query_taps(wts_ref[...])
    tail = tail_ref[pl.ds(2 * EDGE, EDGE), :].astype(F32)
    tops = edges(hid, vq_ref, rows, tokens, per, tail, prev_ref)
    seen = visible(tokens, slots)
    for n in range(per):
        s = conv_rows(vq_ref[n, pl.ds(rows, tokens), :].astype(F32), tops[n], taps, pad.at[n], 1)
        c, slope = silu(s)
        q, scale = unit(c)
        fq_ref[n] = scale * slope
        scores = jnp.where(seen, mm(two(q), (kh_ref[n], kl_ref[n]), ROWS_ROWS), 0.0)
        uh, ul = two(u_ref[n])
        both = jnp.concatenate([wh_ref[n], uh], axis=1), jnp.concatenate([wl_ref[n], ul], axis=1)
        mapped = mm(two(scores), both)
        q_ref[n] = q
        sc_ref[n] = scores
        qm_ref[n] = q - mapped[:, :HEAD]
        ol_ref[n] = mapped[:, HEAD:]


def outs_kernel(
    per, tokens, slots, hid, vq_ref, wts_ref, start_ref, m_ref, c_ref, qm_ref, ol_ref, a_ref,
    st_ref, dr_ref, mb_ref, nm_ref, end_ref,
):
    rows = tokens * slots
    gain = gain_row(wts_ref[...])
    start = two(jnp.where((hid[0] & BEFORE) > 0, start_ref[...], 0.0))
    states = [mm(two(m_ref[n]), start) + c_ref[n] for n in range(per)]
    mapped = [two(qm_ref[n]) for n in range(per)]
    raws = [mm(mapped[n], two(states[n])) + ol_ref[n] for n in range(per)]
    local = []
    for n in range(per):
        st_ref[n] = states[n]
        raw = raws[n]
        scale = lax.rsqrt(jnp.mean(raw * raw, axis=-1, keepdims=True) + EPS)
        hat = raw * scale
        nm_ref[n] = (hat * gain).astype(BF16)
        dn = vq_ref[n, pl.ds(rows + tokens, tokens), :].astype(F32) * gain
        dr = scale * (dn - hat * jnp.mean(dn * hat, axis=-1, keepdims=True))
        dr_ref[n] = dr
        local.append(mm(mapped[n], two(dr), COLS_COLS))
    ir, ic = grid_of(HEAD, 2 * HEAD)
    state = (ir == ic).astype(F32)
    for n in range(per - 1, -1, -1):
        mb_ref[n] = state
        moved = mm(two(a_ref[n]), two(state), COLS_COLS)
        state = moved + jnp.concatenate([jnp.zeros((HEAD, HEAD), F32), local[n]], axis=1)
    end_ref[...] = state


def query_grads_kernel(
    per, tokens, slots, hid, wts_ref, nm_ref, kh_ref, kl_ref, wh_ref, wl_ref, u_ref, q_ref, sc_ref, dr_ref, st_ref,
    fq_ref, mb_ref, d_ref, dk_ref, dd_ref, stf_ref, mbf_ref, nq_ref, pad,
):
    taps = query_taps(wts_ref[...])
    seen = visible(tokens, slots)
    for n in range(per):
        q, k2 = q_ref[n], (kh_ref[n], kl_ref[n])
        stf_ref[n], mbf_ref[n] = st_ref[n], mb_ref[n]
        state, dr = two(st_ref[n]), two(dr_ref[n])
        d = u_ref[n] - mm((wh_ref[n], wl_ref[n]), state)
        d_ref[n] = d
        ds = two(jnp.where(seen, mm(dr, two(d), ROWS_ROWS), 0.0))
        dq = mm(dr, state, ROWS_ROWS) + mm(ds, k2)
        dk_ref[n] = mm(ds, two(q), COLS_COLS)
        dd_ref[n] = mm(two(sc_ref[n]), dr, COLS_COLS)
        inner, rim = conv_back(fq_ref[n] * (dq - q * jnp.sum(q * dq, axis=-1, keepdims=True)), taps, pad.at[n], 1)
        nq_ref[n, pl.ds(0, tokens), :] = nm_ref[n]
        nq_ref[n, pl.ds(tokens, tokens), :] = inner.astype(BF16)
        nq_ref[n, pl.ds(2 * tokens, EDGE), :] = jnp.concatenate([rim, jnp.zeros((8, HEAD), F32)], axis=0).astype(BF16)


def grads_kernel(
    per, tokens, slots, hid, beta_ref, wts_ref, end_ref, mb_ref, kh_ref, kl_ref, th_ref, tl_ref, d_ref, dk_ref, dd_ref,
    st_ref, fk_ref, fv_ref, out_ref, pad,
):
    rows = tokens * slots
    wts = wts_ref[...]
    order = before(rows)
    end = two(jnp.where((hid[0] & AFTER) > 0, end_ref[...], 0.0))
    for n in range(per):
        d, k2 = d_ref[n], (kh_ref[n], kl_ref[n])
        d2 = two(d)
        k = k2[0].astype(F32) + k2[1].astype(F32)
        g2 = two(mm(two(mb_ref[n, :, pl.ds(0, HEAD)]), end) + mb_ref[n, :, pl.ds(HEAD, HEAD)])
        y = mm((th_ref[n], tl_ref[n]), two(dd_ref[n] + mm(k2, g2)))
        betas = beta_rows(beta_ref[n].astype(F32), slots)
        de = 2.0 * sigmoid(column(betas, tokens, slots)) * y
        de2 = two(de)
        dk = dk_ref[n] + mm(d2, g2, ROWS_ROWS) - mm(de2, two(st_ref[n]), ROWS_ROWS)
        dgram = jnp.where(order, mm_half(de2, d2, ROWS_ROWS), 0.0)
        dk = dk - mm(two(dgram + dgram.T), k2)
        along = jnp.sum(y * d, axis=1, keepdims=True)
        marks = []
        for j in range(slots):
            gb = jnp.sum(jnp.where(places(tokens, slots, j), along, 0.0), axis=0, keepdims=True) * sigmoid(-betas[j])
            high = gb.astype(BF16).astype(F32)
            marks += [high, gb - high]
        marks.append(jnp.zeros((EDGE - 2 * slots, tokens), F32))
        value, value_rim = conv_back(fv_ref[n] * de, slot_taps(wts, 1), pad.at[2 * n], slots)
        part = fk_ref[n] * (dk - k * jnp.sum(k * dk, axis=-1, keepdims=True))
        key, key_rim = conv_back(part, slot_taps(wts, 0), pad.at[2 * n + 1], slots)
        out_ref[n, pl.ds(0, rows), :] = key.astype(BF16)
        out_ref[n, pl.ds(rows, rows), :] = value.astype(BF16)
        out_ref[n, pl.ds(2 * rows, EDGE), :] = jnp.concatenate(marks, axis=0).astype(BF16)
        out_ref[n, pl.ds(2 * rows + EDGE, EDGE), :] = jnp.concatenate([key_rim, value_rim], axis=0).astype(BF16)


def unpack_kernel(per, tokens, slots, got_ref, gk_ref, gv_ref):
    rows = tokens * slots
    for n in range(per):
        for a, out_ref in enumerate((gk_ref, gv_ref)):
            main = got_ref[n, pl.ds(a * rows, rows), :].astype(F32)
            out_ref[:, :, pl.ds(n * HEAD, HEAD)] = main.reshape(tokens, slots, HEAD)


def unpack_query_kernel(tokens, got_ref, gq_ref):
    gq_ref[...] = got_ref[0, pl.ds(tokens, tokens), :].astype(F32)


def rims_kernel(heads, slots, rim_ref, gq_ref, gk_ref, gv_ref, mark_ref, nq_ref, nk_ref, nv_ref, gb_ref):
    for h in range(heads):
        part = pl.ds(h * HEAD, HEAD)
        rim = rim_ref[h].astype(F32)
        nq_ref[:, part] = gq_ref[:, part] + rim[:8]
        nk_ref[:, :, part] = gk_ref[:, :, part] + rim[8:16].reshape(8 // slots, slots, HEAD)
        nv_ref[:, :, part] = gv_ref[:, :, part] + rim[16:].reshape(8 // slots, slots, HEAD)
        mark = mark_ref[h].astype(F32)
        for j in range(slots):
            gb_ref[j, pl.ds(h, 1), :] = mark[2 * j : 2 * j + 1] + mark[2 * j + 1 : 2 * j + 2]


FAR = ("kh", "kl", "xh", "xl", "th", "tl", "wh", "wl", "a", "m", "fk", "fv", "stf", "mbf", "d", "dk", "dd")


def call(kernel, hid, steps, live, ins, reads, outs, scratch=(), us=1.0, grant=24):
    def spec(shape, how):
        if how == "weights":
            return pl.BlockSpec((shape[0], HEAD), lambda i, h: (0, h[0] & (BEFORE - 1)))
        if how is None:
            return pl.BlockSpec(shape, lambda i, h: (0,) * len(shape))
        if isinstance(how, tuple):
            kind, count, row = how
            if kind == "prev":
                return pl.BlockSpec((1, EDGE, HEAD), lambda i, h: (jnp.maximum(i * count - 1, 0), row // EDGE, 0))
            return pl.BlockSpec((count, EDGE, HEAD), lambda i, h: (i, row // EDGE, 0))
        return pl.BlockSpec((how,) + tuple(shape[1:]), lambda i, h: (i,) + (0,) * (len(shape) - 1))

    def home(name):
        return pltpu.HBM if name in FAR else pltpu.VMEM

    operands = [a for a, _ in ins]
    operands += [pltpu.with_memory_space_constraint(live[name], home(name)) for name, _ in reads]
    hows = [how for _, how in ins + reads]
    results = pl.pallas_call(
        kernel,
        grid_spec=pltpu.PrefetchScalarGridSpec(
            num_scalar_prefetch=1,
            grid=(steps,),
            in_specs=[spec(a.shape, how) for a, how in zip(operands, hows)],
            out_specs=[spec(shape, how) for _, shape, _, how in outs],
            scratch_shapes=list(scratch),
        ),
        out_shape=[
            jax.ShapeDtypeStruct(shape, dtype) if name is None else home(name)(shape, dtype)
            for name, shape, dtype, _ in outs
        ],
        compiler_params=pltpu.CompilerParams(dimension_semantics=("arbitrary",), vmem_limit_bytes=grant << 20),
        cost_estimate=pl.CostEstimate(flops=int(us * 1.1e9), bytes_accessed=1 << 16, transcendentals=0),
    )(hid, *operands)
    for (name, _, _, _), result in zip(outs, results):
        if name is not None:
            live[name] = result
    return [r for (name, _, _, _), r in zip(outs, results) if name is None]


def shards(
    query_in,
    key_in,
    value_in,
    beta_logit,
    query_conv,
    key_conv,
    value_conv,
    norm_gain,
    out_weight,
    grad_out,
):
    tokens, slots = key_in.shape[0], key_in.shape[1]
    width = query_in.shape[1]
    heads = width // HEAD
    shard_count = lax.axis_size("ctx")
    place = lax.axis_index("ctx")
    groups = shard_count // heads
    group_lists = [[b * heads + i for i in range(heads)] for b in range(groups)]
    rows = tokens * slots
    g = heads
    first, final = place < heads, place >= shard_count - heads
    hid = (place % heads + jnp.where(first, 0, BEFORE) + jnp.where(final, 0, AFTER)).astype(jnp.int32).reshape(1)

    def exchange(x):
        return lax.all_to_all(x, "ctx", 0, 0, axis_index_groups=group_lists, tiled=True)

    def by_head(x):
        return x.reshape(x.shape[0], heads, HEAD).transpose(1, 0, 2)

    def slots_by_head(x):
        return x.reshape(x.shape[0], slots, heads, HEAD).transpose(2, 0, 1, 3).reshape(heads, -1, HEAD)

    high = lax.reduce_precision(beta_logit, 8, 7)
    rest = beta_logit - high
    middle = lax.reduce_precision(rest, 8, 7)
    betas = jnp.stack([high, middle, rest - middle], axis=2)
    betas = betas.transpose(3, 1, 2, 0).reshape(heads, 3 * slots, tokens).astype(BF16)
    betas = jnp.pad(betas, ((0, 0), (0, EDGE - 3 * slots), (0, 0)))
    last = EDGE // slots
    kb = exchange(
        jnp.concatenate(
            [slots_by_head(key_in), betas, slots_by_head(value_in[-last:]), by_head(query_in[-EDGE:])], axis=1
        )
    )

    group = place // heads
    tail = jnp.concatenate([kb[g - 1, rows - EDGE : rows], kb[g - 1, rows + EDGE :]], axis=0)

    grad_normed = jnp.dot(grad_out, out_weight.T, preferred_element_type=F32).astype(BF16)
    vq = jnp.concatenate([slots_by_head(value_in), by_head(query_in), by_head(grad_normed)], axis=1)
    vq, tail = lax.optimization_barrier((vq, tail))
    tail = lax.ppermute(tail, "ctx", [(i, (i + heads) % shard_count) for i in range(shard_count)])
    vq, tail = lax.optimization_barrier((vq, tail))
    vq = exchange(vq)

    wts = jnp.concatenate(
        [
            jnp.tile(key_conv, (1, 8 // slots, 1)).reshape(8 * TAPS, width),
            jnp.tile(value_conv, (1, 8 // slots, 1)).reshape(8 * TAPS, width),
            query_conv,
            norm_gain.reshape(1, width),
            jnp.zeros((3, width), F32),
        ],
        axis=0,
    )
    per = 2 if g % 2 == 0 else 1
    steps = g // per

    def pad(n):
        return [pltpu.VMEM((per, n + EDGE + 8, HEAD), F32)]

    def big(name, *shape, per=per, kind=F32):
        return (name, (g,) + shape, kind, per)

    live = {}
    wide = 4 if g % 4 == 0 else per
    (m_end,) = call(
        functools.partial(inverse_kernel, wide, tokens, slots),
        hid,
        g // wide,
        live,
        [(kb, wide), (kb, ("prev", wide, rows - EDGE)), (tail, None), (wts, "weights")],
        [],
        [big(name, rows, HEAD, per=wide, kind=BF16) for name in ("kh", "kl")]
        + [big(name, rows, rows, per=wide, kind=BF16) for name in ("xh", "xl", "th", "tl")]
        + [big(name, rows, HEAD, per=wide, kind=BF16) for name in ("wh", "wl")]
        + [
            big("fk", rows, HEAD, per=wide), big("a", HEAD, HEAD, per=wide), big("m", HEAD, HEAD, per=wide),
            (None, (HEAD, HEAD), F32, None),
        ],
        scratch=[pltpu.VMEM((wide, rows + EDGE + 8, HEAD), F32), pltpu.VMEM((HEAD, HEAD), F32)],
        us=11.0,
        grant=40,
    )
    beta = (kb, ("rows", per, rows))
    (c_end,) = call(
        functools.partial(maps_kernel, per, tokens, slots),
        hid,
        steps,
        live,
        [(vq, per), (vq, ("prev", per, rows - EDGE)), beta, (tail, None), (wts, "weights")],
        [(name, per) for name in ("kh", "kl", "xh", "xl", "a", "m")],
        [
            big("u", rows, HEAD), big("c", HEAD, HEAD), big("an", HEAD, HEAD), big("mn", HEAD, HEAD),
            big("fv", rows, HEAD), (None, (HEAD, HEAD), F32, None),
        ],
        scratch=pad(rows) + [pltpu.VMEM((HEAD, HEAD), F32)],
        us=6.0,
    )

    def across(last, towards):
        if groups == 1:
            return jnp.zeros((HEAD, HEAD), F32)
        if groups == 2:
            moves = [(i, (i + towards * heads) % shard_count) for i in range(shard_count)]
            return lax.ppermute(last[1], "ctx", moves)
        every = lax.all_gather(jnp.concatenate(last, axis=1), "ctx")
        head = place % heads
        ahead = group if towards > 0 else groups - 1 - group

        def advance(i, state):
            source = i if towards > 0 else groups - 1 - i
            item = lax.dynamic_index_in_dim(every, source * heads + head, 0, False)
            return jnp.dot(item[:, :HEAD], state, precision=lax.Precision.HIGHEST) + item[:, HEAD:]

        return lax.fori_loop(0, ahead, advance, jnp.zeros((HEAD, HEAD), F32))

    start = across((m_end, c_end), 1)
    call(
        functools.partial(queries_kernel, per, tokens, slots),
        hid,
        steps,
        live,
        [(vq, per), (vq, ("prev", per, rows + tokens - EDGE)), (tail, None), (wts, "weights")],
        [(name, per) for name in ("kh", "kl", "wh", "wl", "u")],
        [
            big("q", tokens, HEAD), big("sc", tokens, rows), big("qm", tokens, HEAD), big("ol", tokens, HEAD),
            big("fq", tokens, HEAD),
        ],
        scratch=pad(tokens),
        us=8.0,
    )
    normed, back_end = call(
        functools.partial(outs_kernel, g, tokens, slots),
        hid,
        1,
        live,
        [(vq, g), (wts, "weights"), (start, None)],
        [(name, g) for name in ("mn", "c", "qm", "ol", "an")],
        [
            big("st", HEAD, HEAD, per=g), big("dr", tokens, HEAD, per=g), big("mb", HEAD, 2 * HEAD, per=g),
            (None, (g, tokens, HEAD), BF16, g), (None, (HEAD, 2 * HEAD), F32, None),
        ],
        us=4.0,
    )
    finish = across((back_end[:, :HEAD], back_end[:, HEAD:]), -1)
    (nq,) = call(
        functools.partial(query_grads_kernel, per, tokens, slots),
        hid,
        steps,
        live,
        [(wts, "weights"), (normed, per)],
        [(name, per) for name in ("kh", "kl", "wh", "wl", "u", "q", "sc", "dr", "st", "fq", "mb")],
        [
            big("d", rows, HEAD), big("dk", rows, HEAD), big("dd", rows, HEAD), big("stf", HEAD, HEAD),
            big("mbf", HEAD, 2 * HEAD), (None, (g, 2 * tokens + EDGE, HEAD), BF16, per),
        ],
        scratch=pad(tokens),
        us=20.0,
    )
    nq = exchange(nq)
    (grads,) = call(
        functools.partial(grads_kernel, per, tokens, slots),
        hid,
        steps,
        live,
        [beta, (wts, "weights"), (finish, None)],
        [(name, per) for name in ("mbf", "kh", "kl", "th", "tl", "d", "dk", "dd", "stf", "fk", "fv")],
        [(None, (g, 2 * rows + 2 * EDGE, HEAD), BF16, per)],
        scratch=[pltpu.VMEM((2 * per, rows + EDGE + 8, HEAD), F32)],
        us=20.0,
    )
    grads = exchange(grads)

    normed_bf = nq[:, :tokens].transpose(1, 0, 2).reshape(tokens, width)
    partial = jnp.dot(normed_bf, out_weight, preferred_element_type=F32)
    if lax.axis_size("head") == 2:
        half = tokens // 2
        mine = lax.axis_index("head")
        pieces = partial.reshape(2, half, partial.shape[1])
        kept = lax.dynamic_index_in_dim(pieces, mine, 0, False)
        sent = lax.dynamic_index_in_dim(pieces, 1 - mine, 0, False).astype(BF16)
        layer_out = (kept + lax.ppermute(sent, "head", [(0, 1), (1, 0)]).astype(F32)).astype(BF16)
    else:
        layer_out = lax.psum_scatter(partial.astype(BF16), "head", scatter_dimension=0, tiled=True)

    rim = jnp.concatenate([nq[:, 2 * tokens : 2 * tokens + 8], grads[:, 2 * rows + EDGE :]], axis=1)
    rim = lax.ppermute(rim, "ctx", [(i, i - 1) for i in range(1, shard_count)])
    part = lambda x: pl.BlockSpec((1,) + x.shape[1:], lambda h: (h, 0, 0))
    small = pltpu.CompilerParams(vmem_limit_bytes=8 << 20)
    cost = lambda us: pl.CostEstimate(flops=int(us * 1.1e9), bytes_accessed=1 << 16, transcendentals=0)
    grad_query = pl.pallas_call(
        functools.partial(unpack_query_kernel, tokens),
        grid=(heads,),
        in_specs=[part(nq)],
        out_specs=pl.BlockSpec((tokens, HEAD), lambda h: (0, h)),
        out_shape=jax.ShapeDtypeStruct((tokens, width), F32),
        compiler_params=small,
        cost_estimate=cost(2.0),
    )(nq)
    grad_key, grad_value = pl.pallas_call(
        functools.partial(unpack_kernel, per, tokens, slots),
        grid=(steps,),
        in_specs=[pl.BlockSpec((per,) + grads.shape[1:], lambda h: (h, 0, 0))],
        out_specs=[pl.BlockSpec((tokens, slots, per * HEAD), lambda h: (0, 0, h))] * 2,
        out_shape=[jax.ShapeDtypeStruct((tokens, slots, width), F32)] * 2,
        compiler_params=small,
        cost_estimate=cost(10.0),
    )(grads)
    flat = pl.BlockSpec((8, width), lambda i: (tokens // 8 - 1, 0))
    deep = pl.BlockSpec((8 // slots, slots, width), lambda i: (tokens * slots // 8 - 1, 0, 0))
    mark = pl.BlockSpec((heads, EDGE, tokens), lambda i: (0, 2 * rows // EDGE, 0))
    beta_spec = pl.BlockSpec((slots, heads, tokens), lambda i: (0, 0, 0))
    grad_query, grad_key, grad_value, grad_beta = pl.pallas_call(
        functools.partial(rims_kernel, heads, slots),
        grid=(1,),
        in_specs=[pl.BlockSpec(rim.shape, lambda i: (0, 0, 0)), flat, deep, deep, mark],
        out_specs=[flat, deep, deep, beta_spec],
        out_shape=[jax.ShapeDtypeStruct(x.shape, F32) for x in (grad_query, grad_key, grad_value)]
        + [jax.ShapeDtypeStruct((slots, heads, tokens), F32)],
        input_output_aliases={1: 0, 2: 1, 3: 2},
        compiler_params=small,
    )(rim, grad_query, grad_key, grad_value, grads)
    grad_beta = grad_beta.transpose(2, 0, 1)
    return (layer_out, grad_query, grad_key, grad_value, grad_beta)


def solution(mesh):
    placed = (
        P("ctx", "head"),
        P("ctx", None, "head"),
        P("ctx", None, "head"),
        P("ctx", None, "head"),
        P(None, "head"),
        P(None, None, "head"),
        P(None, None, "head"),
        P("head"),
        P("head", None),
        P("ctx", None),
    )
    return jax.shard_map(
        shards,
        mesh=mesh,
        in_specs=placed,
        out_specs=(
            P(("ctx", "head"), None),
            P("ctx", "head"),
            P("ctx", None, "head"),
            P("ctx", None, "head"),
            P("ctx", None, "head"),
        ),
        check_vma=False,
    )
```

```python
import functools

import jax
import jax.numpy as jnp
from jax import lax
from jax.experimental import pallas as pl
from jax.experimental.pallas import tpu as pltpu
from jax.sharding import PartitionSpec as P

HEAD = 128
TAPS = 4
RIM = TAPS - 1
EDGE = 16
EPS = 1e-06
BEFORE = 1 << 16
AFTER = 1 << 17
F32 = jnp.float32
BF16 = jnp.bfloat16

ROWS_COLS = (((1,), (0,)), ((), ()))
ROWS_ROWS = (((1,), (1,)), ((), ()))
COLS_COLS = (((0,), (0,)), ((), ()))


def two(x):
    high = x.astype(BF16)
    return high, (x - high.astype(F32)).astype(BF16)


def dot(a, b, dims):
    return lax.dot_general(a, b, dims, preferred_element_type=F32)


def mm(left, right, dims=ROWS_COLS):
    (ah, al), (bh, bl) = left, right
    ka, kb = dims[0][0][0], dims[0][1][0]
    nb = 1 - kb
    depth, cols = ah.shape[ka], bh.shape[nb]
    if depth <= HEAD:
        a = jnp.concatenate([ah, al], axis=ka)
        high, low = jnp.concatenate([bh, bh], axis=kb), jnp.concatenate([bl, bl], axis=kb)
        if cols <= HEAD:
            out = dot(a, jnp.concatenate([high, low], axis=nb), dims)
            return out[:, :cols] + out[:, cols:]
        return dot(a, high, dims) + dot(a, low, dims)
    if cols <= HEAD:
        out = dot(ah, jnp.concatenate([bh, bl], axis=nb), dims)
        return out[:, :cols] + out[:, cols:] + dot(al, bh, dims)
    return dot(ah, bh, dims) + dot(ah, bl, dims) + dot(al, bh, dims)


def piece(x, row, col=None):
    cols = slice(None) if col is None else slice(col * HEAD, (col + 1) * HEAD)
    return tuple(p[row * HEAD : (row + 1) * HEAD, cols] for p in x)


def lower_times(x, b):
    count = x[0].shape[0] // HEAD
    return jnp.concatenate(
        [sum(mm(piece(x, i, j), piece(b, j)) for j in range(i + 1)) for i in range(count)], axis=0
    )


def mm_half(left, right, dims=ROWS_COLS):
    (ah, al), (bh, _) = left, right
    ka, kb = dims[0][0][0], dims[0][1][0]
    return dot(jnp.concatenate([ah, al], axis=ka), jnp.concatenate([bh, bh], axis=kb), dims)


def grid_of(rows, cols):
    return lax.broadcasted_iota(jnp.int32, (rows, cols), 0), lax.broadcasted_iota(jnp.int32, (rows, cols), 1)


def before(rows):
    r, c = grid_of(rows, rows)
    return c < r


def level_pairs(rows, level):
    r, c = grid_of(rows, rows)
    return ((r >> (level + 1)) == (c >> (level + 1))) & (((r >> level) & 1) == 1) & (((c >> level) & 1) == 0)


def visible(tokens, slots):
    t, c = grid_of(tokens, tokens * slots)
    return c < slots * (t + 1)


def times(pattern, x):
    if pattern.shape[0] == 1:
        return pattern * x
    return (x.reshape(-1, 8, HEAD) * pattern[None]).reshape(x.shape)


def conv_rows(x, edge, taps, pad, stride):
    rows = x.shape[0]
    pad[pl.ds(0, EDGE), :] = edge
    pad[pl.ds(EDGE, rows), :] = x
    total = None
    for i in range(TAPS):
        part = times(taps[i], pad[pl.ds(EDGE - stride * (RIM - i), rows), :])
        total = part if total is None else total + part
    return total


def conv_back(grad, taps, pad, stride):
    rows = grad.shape[0]
    pad[pl.ds(8, 8), :] = jnp.zeros((8, HEAD), F32)
    pad[pl.ds(EDGE, rows), :] = grad
    pad[pl.ds(EDGE + rows, 8), :] = jnp.zeros((8, HEAD), F32)
    inner, rim = None, None
    for i in range(TAPS):
        part = times(taps[i], pad[pl.ds(EDGE + stride * (RIM - i), rows), :])
        edge = times(taps[i], pad[pl.ds(8 + stride * (RIM - i), 8), :])
        inner = part if inner is None else inner + part
        rim = edge if rim is None else rim + edge
    return inner, rim


def sigmoid(x):
    return 1.0 / (1.0 + jnp.exp(-x))


def silu(s):
    sg = sigmoid(s)
    return s * sg, sg * (1.0 + s * (1.0 - sg))


def unit(values):
    scale = lax.rsqrt(jnp.sum(values * values, axis=-1, keepdims=True) + EPS)
    return values * scale, scale


def beta_rows(tile, slots):
    return [tile[3 * j : 3 * j + 1] + tile[3 * j + 1 : 3 * j + 2] + tile[3 * j + 2 : 3 * j + 3] for j in range(slots)]


def places(tokens, slots, j):
    r, t = grid_of(tokens * slots, tokens)
    return r == slots * t + j


def column(rows, tokens, slots):
    spread = jnp.zeros((tokens * slots, tokens), F32)
    for j in range(slots):
        spread = jnp.where(places(tokens, slots, j), rows[j], spread)
    return jnp.sum(spread, axis=1, keepdims=True)


def slot_taps(wts, kind):
    return [wts[8 * (TAPS * kind + i) : 8 * (TAPS * kind + i + 1)] for i in range(TAPS)]


def query_taps(wts):
    return [wts[16 * TAPS + i : 16 * TAPS + i + 1] for i in range(TAPS)]


def gain_row(wts):
    return wts[17 * TAPS : 17 * TAPS + 1]


def edges(hid, ref, first, rows, per, tail, prev_ref):
    tail = jnp.where((hid[0] & BEFORE) > 0, tail, 0.0)
    prev = jnp.where(pl.program_id(0) == 0, tail, prev_ref[0].astype(F32))
    return [prev] + [ref[n, pl.ds(first + rows - EDGE, EDGE), :].astype(F32) for n in range(per - 1)]


def inverse_kernel(
    per, tokens, slots, hid, kb_ref, prev_ref, tail_ref, wts_ref,
    kh_ref, kl_ref, xh_ref, xl_ref, th_ref, tl_ref, wh_ref, wl_ref, fk_ref, a_ref, m_ref, end_ref, pad, carry,
):
    rows = tokens * slots
    step = pl.program_id(0)
    taps = slot_taps(wts_ref[...], 0)
    tops = edges(hid, kb_ref, 0, rows, per, tail_ref[pl.ds(0, EDGE), :].astype(F32), prev_ref)
    order = before(HEAD)
    blocks = rows // HEAD
    ir, ic = grid_of(HEAD, HEAD)

    @pl.when(step == 0)
    def _():
        carry[...] = (ir == ic).astype(F32)

    grams, keys, scaled = [], [], []
    for n in range(per):
        s = conv_rows(kb_ref[n, pl.ds(0, rows), :].astype(F32), tops[n], taps, pad.at[n], slots)
        c, slope = silu(s)
        k, scale = unit(c)
        fk_ref[n] = scale * slope
        betas = beta_rows(kb_ref[n, pl.ds(rows, EDGE), :].astype(F32), slots)
        strength = 2.0 * sigmoid(column(betas, tokens, slots))
        k2 = two(k)
        kh_ref[n], kl_ref[n] = k2
        keys.append(k2)
        scaled.append(two(strength * k))
        gram = {}
        for i in range(blocks):
            for j in range(i + 1):
                part = mm(piece(k2, i), piece(k2, j), ROWS_ROWS) * strength[i * HEAD : (i + 1) * HEAD]
                gram[i, j] = jnp.where(order, part, 0.0) if i == j else part
        grams.append(gram)
    eye = (ir == ic).astype(F32)
    zero = jnp.zeros((HEAD, HEAD), BF16)
    diagonal = [gram[b, b] for gram in grams for b in range(blocks)]
    systems = [two(x) for x in diagonal]
    pairs = level_pairs(HEAD, 0)
    inverse = [eye - jnp.where(pairs, x, 0.0) for x in diagonal]
    level = 1
    while (1 << level) < HEAD:
        pairs = level_pairs(HEAD, level)
        split = [two(x) for x in inverse]
        crossed = [mm(tuple(jnp.where(pairs, p, zero) for p in s), x) for s, x in zip(systems, split)]
        inverse = [x - mm(s, two(y)) for x, s, y in zip(inverse, split, crossed)]
        level += 1
    for n in range(per):
        done = {(b, b): inverse[n * blocks + b] for b in range(blocks)}
        halves = {(b, b): two(done[b, b]) for b in range(blocks)}
        for j in range(blocks):
            for i in range(j + 1, blocks):
                cross = sum(mm(two(grams[n][i, m]), halves[m, j]) for m in range(j, i))
                done[i, j] = -mm(halves[i, i], two(cross))
                halves[i, j] = two(done[i, j])
        nothing = jnp.zeros((HEAD, HEAD), BF16)
        x2 = tuple(
            jnp.concatenate(
                [
                    jnp.concatenate([halves[i, j][p] if j <= i else nothing for j in range(blocks)], axis=1)
                    for i in range(blocks)
                ],
                axis=0,
            )
            for p in range(2)
        )
        xh_ref[n], xl_ref[n] = x2
        th_ref[n], tl_ref[n] = x2[0].T, x2[1].T
        w2 = two(lower_times(x2, scaled[n]))
        wh_ref[n], wl_ref[n] = w2
        a_ref[n] = eye - mm(keys[n], w2, COLS_COLS)
    state = carry[...]
    for n in range(per):
        m_ref[n] = state
        state = mm(two(a_ref[n]), two(state))
    carry[...] = state
    end_ref[...] = state


def maps_kernel(
    per, tokens, slots, hid, vq_ref, prev_ref, beta_ref, tail_ref, wts_ref, kh_ref, kl_ref, xh_ref, xl_ref, a_ref,
    m_ref,
    u_ref, c_ref, an_ref, mn_ref, fv_ref, end_ref, pad, carry,
):

    rows = tokens * slots
    taps = slot_taps(wts_ref[...], 1)

    @pl.when(pl.program_id(0) == 0)
    def _():
        carry[...] = jnp.zeros((HEAD, HEAD), F32)

    tail = tail_ref[pl.ds(EDGE, EDGE), :].astype(F32)
    tops = edges(hid, vq_ref, 0, rows, per, tail, prev_ref)
    rights = []
    for n in range(per):
        s = conv_rows(vq_ref[n, pl.ds(0, rows), :].astype(F32), tops[n], taps, pad.at[n], slots)
        v, fv_ref[n] = silu(s)
        betas = beta_rows(beta_ref[n].astype(F32), slots)
        rights.append(two(2.0 * sigmoid(column(betas, tokens, slots)) * v))
    us = [lower_times((xh_ref[n], xl_ref[n]), rights[n]) for n in range(per)]
    maps = [mm((kh_ref[n], kl_ref[n]), two(us[n]), COLS_COLS) for n in range(per)]
    state = carry[...]
    for n in range(per):
        u_ref[n] = us[n]
        c_ref[n] = state
        an_ref[n], mn_ref[n] = a_ref[n], m_ref[n]
        state = mm(two(a_ref[n]), two(state)) + maps[n]
    carry[...] = state
    end_ref[...] = state


def queries_kernel(
    per, tokens, slots, hid, vq_ref, prev_ref, tail_ref, wts_ref, kh_ref, kl_ref, wh_ref, wl_ref, u_ref,
    q_ref, sc_ref, qm_ref, ol_ref, fq_ref, pad,
):
    rows = tokens * slots
    taps = query_taps(wts_ref[...])
    tail = tail_ref[pl.ds(2 * EDGE, EDGE), :].astype(F32)
    tops = edges(hid, vq_ref, rows, tokens, per, tail, prev_ref)
    seen = visible(tokens, slots)
    qs = []
    for n in range(per):
        s = conv_rows(vq_ref[n, pl.ds(rows, tokens), :].astype(F32), tops[n], taps, pad.at[n], 1)
        c, slope = silu(s)
        q, scale = unit(c)
        fq_ref[n] = scale * slope
        q_ref[n] = q
        qs.append(q)
    scores = [
        jnp.where(seen, mm(two(qs[n]), (kh_ref[n], kl_ref[n]), ROWS_ROWS), 0.0) for n in range(per)
    ]
    mapped = []
    for n in range(per):
        uh, ul = two(u_ref[n])
        both = jnp.concatenate([wh_ref[n], uh], axis=1), jnp.concatenate([wl_ref[n], ul], axis=1)
        mapped.append(mm(two(scores[n]), both))
    for n in range(per):
        sc_ref[n] = scores[n]
        qm_ref[n] = qs[n] - mapped[n][:, :HEAD]
        ol_ref[n] = mapped[n][:, HEAD:]


def outs_kernel(
    per, tokens, slots, hid, vq_ref, wts_ref, start_ref, m_ref, c_ref, qm_ref, ol_ref, a_ref,
    st_ref, dr_ref, mb_ref, nm_ref, end_ref,
):
    rows = tokens * slots
    gain = gain_row(wts_ref[...])
    start = two(jnp.where((hid[0] & BEFORE) > 0, start_ref[...], 0.0))
    states = [mm(two(m_ref[n]), start) + c_ref[n] for n in range(per)]
    mapped = [two(qm_ref[n]) for n in range(per)]
    raws = [mm(mapped[n], two(states[n])) + ol_ref[n] for n in range(per)]
    local = []
    for n in range(per):
        st_ref[n] = states[n]
        raw = raws[n]
        scale = lax.rsqrt(jnp.mean(raw * raw, axis=-1, keepdims=True) + EPS)
        hat = raw * scale
        nm_ref[n] = (hat * gain).astype(BF16)
        dn = vq_ref[n, pl.ds(rows + tokens, tokens), :].astype(F32) * gain
        dr = scale * (dn - hat * jnp.mean(dn * hat, axis=-1, keepdims=True))
        dr_ref[n] = dr
        local.append(mm(mapped[n], two(dr), COLS_COLS))
    ir, ic = grid_of(HEAD, 2 * HEAD)
    state = (ir == ic).astype(F32)
    for n in range(per - 1, -1, -1):
        mb_ref[n] = state
        moved = mm(two(a_ref[n]), two(state), COLS_COLS)
        state = moved + jnp.concatenate([jnp.zeros((HEAD, HEAD), F32), local[n]], axis=1)
    end_ref[...] = state


def query_grads_kernel(
    per, tokens, slots, hid, wts_ref, nm_ref, kh_ref, kl_ref, wh_ref, wl_ref, u_ref, q_ref, sc_ref, dr_ref, st_ref,
    fq_ref, mb_ref, d_ref, dk_ref, dd_ref, stf_ref, mbf_ref, nq_ref, pad,
):
    taps = query_taps(wts_ref[...])
    seen = visible(tokens, slots)
    chunks = range(per)
    for n in chunks:
        stf_ref[n], mbf_ref[n] = st_ref[n], mb_ref[n]
    states = [two(st_ref[n]) for n in chunks]
    drs = [two(dr_ref[n]) for n in chunks]
    keys = [(kh_ref[n], kl_ref[n]) for n in chunks]
    qs = [q_ref[n] for n in chunks]
    found = [u_ref[n] - mm((wh_ref[n], wl_ref[n]), states[n]) for n in chunks]
    dss = [two(jnp.where(seen, mm(drs[n], two(found[n]), ROWS_ROWS), 0.0)) for n in chunks]
    for n in chunks:
        d_ref[n] = found[n]
        dd_ref[n] = mm(two(sc_ref[n]), drs[n], COLS_COLS)
    dqs = [mm(drs[n], states[n], ROWS_ROWS) + mm(dss[n], keys[n]) for n in chunks]
    for n in chunks:
        dk_ref[n] = mm(dss[n], two(qs[n]), COLS_COLS)
    for n in chunks:
        part = fq_ref[n] * (dqs[n] - qs[n] * jnp.sum(qs[n] * dqs[n], axis=-1, keepdims=True))
        inner, rim = conv_back(part, taps, pad.at[n], 1)
        nq_ref[n, pl.ds(0, tokens), :] = nm_ref[n]
        nq_ref[n, pl.ds(tokens, tokens), :] = inner.astype(BF16)
        nq_ref[n, pl.ds(2 * tokens, EDGE), :] = jnp.concatenate([rim, jnp.zeros((8, HEAD), F32)], axis=0).astype(BF16)


def grads_kernel(
    per, tokens, slots, hid, beta_ref, wts_ref, end_ref, mb_ref, kh_ref, kl_ref, th_ref, tl_ref, d_ref, dk_ref, dd_ref,
    st_ref, fk_ref, fv_ref, out_ref, pad,
):
    rows = tokens * slots
    wts = wts_ref[...]
    order = before(rows)
    end = two(jnp.where((hid[0] & AFTER) > 0, end_ref[...], 0.0))
    chunks = range(per)
    keys = [(kh_ref[n], kl_ref[n]) for n in chunks]
    gs = [two(mm(two(mb_ref[n, :, pl.ds(0, HEAD)]), end) + mb_ref[n, :, pl.ds(HEAD, HEAD)]) for n in chunks]
    dds = [two(dd_ref[n] + mm(keys[n], gs[n])) for n in chunks]
    ys = [mm((th_ref[n], tl_ref[n]), dds[n]) for n in chunks]
    betas = [beta_rows(beta_ref[n].astype(F32), slots) for n in chunks]
    des = [2.0 * sigmoid(column(betas[n], tokens, slots)) * ys[n] for n in chunks]
    halves = [two(des[n]) for n in chunks]
    ds = [two(d_ref[n]) for n in chunks]
    grams = [jnp.where(order, mm_half(halves[n], ds[n], ROWS_ROWS), 0.0) for n in chunks]
    direct = [
        dk_ref[n] + mm(ds[n], gs[n], ROWS_ROWS) - mm(halves[n], two(st_ref[n]), ROWS_ROWS) for n in chunks
    ]
    dks = [direct[n] - mm(two(grams[n] + grams[n].T), keys[n]) for n in chunks]
    for n in chunks:
        along = jnp.sum(ys[n] * d_ref[n], axis=1, keepdims=True)
        marks = []
        for j in range(slots):
            gb = jnp.sum(jnp.where(places(tokens, slots, j), along, 0.0), axis=0, keepdims=True)
            gb = gb * sigmoid(-betas[n][j])
            high = gb.astype(BF16).astype(F32)
            marks += [high, gb - high]
        marks.append(jnp.zeros((EDGE - 2 * slots, tokens), F32))
        value, value_rim = conv_back(fv_ref[n] * des[n], slot_taps(wts, 1), pad.at[2 * n], slots)
        k = keys[n][0].astype(F32) + keys[n][1].astype(F32)
        part = fk_ref[n] * (dks[n] - k * jnp.sum(k * dks[n], axis=-1, keepdims=True))
        key, key_rim = conv_back(part, slot_taps(wts, 0), pad.at[2 * n + 1], slots)
        out_ref[n, pl.ds(0, rows), :] = key.astype(BF16)
        out_ref[n, pl.ds(rows, rows), :] = value.astype(BF16)
        out_ref[n, pl.ds(2 * rows, EDGE), :] = jnp.concatenate(marks, axis=0).astype(BF16)
        out_ref[n, pl.ds(2 * rows + EDGE, EDGE), :] = jnp.concatenate([key_rim, value_rim], axis=0).astype(BF16)


def unpack_kernel(per, tokens, slots, got_ref, gk_ref, gv_ref):
    rows = tokens * slots
    for n in range(per):
        for a, out_ref in enumerate((gk_ref, gv_ref)):
            main = got_ref[n, pl.ds(a * rows, rows), :].astype(F32)
            out_ref[:, :, pl.ds(n * HEAD, HEAD)] = main.reshape(tokens, slots, HEAD)


def unpack_query_kernel(tokens, got_ref, gq_ref):
    gq_ref[...] = got_ref[0, pl.ds(tokens, tokens), :].astype(F32)


def rims_kernel(heads, slots, rim_ref, gq_ref, gk_ref, gv_ref, mark_ref, nq_ref, nk_ref, nv_ref, gb_ref):
    for h in range(heads):
        part = pl.ds(h * HEAD, HEAD)
        rim = rim_ref[h].astype(F32)
        nq_ref[:, part] = gq_ref[:, part] + rim[:8]
        nk_ref[:, :, part] = gk_ref[:, :, part] + rim[8:16].reshape(8 // slots, slots, HEAD)
        nv_ref[:, :, part] = gv_ref[:, :, part] + rim[16:].reshape(8 // slots, slots, HEAD)
        mark = mark_ref[h].astype(F32)
        for j in range(slots):
            gb_ref[j, pl.ds(h, 1), :] = mark[2 * j : 2 * j + 1] + mark[2 * j + 1 : 2 * j + 2]


FAR = ("kh", "kl", "xh", "xl", "th", "tl", "wh", "wl", "a", "m", "fk", "fv", "stf", "mbf", "d", "dk", "dd")


def call(kernel, hid, steps, live, ins, reads, outs, scratch=(), us=1.0, grant=40):
    def spec(shape, how):
        if how == "weights":
            return pl.BlockSpec((shape[0], HEAD), lambda i, h: (0, h[0] & (BEFORE - 1)))
        if how is None:
            return pl.BlockSpec(shape, lambda i, h: (0,) * len(shape))
        if isinstance(how, tuple):
            kind, count, row = how
            if kind == "prev":
                return pl.BlockSpec((1, EDGE, HEAD), lambda i, h: (jnp.maximum(i * count - 1, 0), row // EDGE, 0))
            return pl.BlockSpec((count, EDGE, HEAD), lambda i, h: (i, row // EDGE, 0))
        return pl.BlockSpec((how,) + tuple(shape[1:]), lambda i, h: (i,) + (0,) * (len(shape) - 1))

    def home(name):
        return pltpu.HBM if name in FAR else pltpu.VMEM

    operands = [a for a, _ in ins]
    operands += [pltpu.with_memory_space_constraint(live[name], home(name)) for name, _ in reads]
    hows = [how for _, how in ins + reads]
    results = pl.pallas_call(
        kernel,
        grid_spec=pltpu.PrefetchScalarGridSpec(
            num_scalar_prefetch=1,
            grid=(steps,),
            in_specs=[spec(a.shape, how) for a, how in zip(operands, hows)],
            out_specs=[spec(shape, how) for _, shape, _, how in outs],
            scratch_shapes=list(scratch),
        ),
        out_shape=[
            jax.ShapeDtypeStruct(shape, dtype) if name is None else home(name)(shape, dtype)
            for name, shape, dtype, _ in outs
        ],
        compiler_params=pltpu.CompilerParams(dimension_semantics=("arbitrary",), vmem_limit_bytes=grant << 20),
        cost_estimate=pl.CostEstimate(flops=int(us * 1.1e9), bytes_accessed=1 << 16, transcendentals=0),
    )(hid, *operands)
    for (name, _, _, _), result in zip(outs, results):
        if name is not None:
            live[name] = result
    return [r for (name, _, _, _), r in zip(outs, results) if name is None]


def shards(
    query_in,
    key_in,
    value_in,
    beta_logit,
    query_conv,
    key_conv,
    value_conv,
    norm_gain,
    out_weight,
    grad_out,
):
    tokens, slots = key_in.shape[0], key_in.shape[1]
    width = query_in.shape[1]
    heads = width // HEAD
    shard_count = lax.axis_size("ctx")
    place = lax.axis_index("ctx")
    groups = shard_count // heads
    group_lists = [[b * heads + i for i in range(heads)] for b in range(groups)]
    rows = tokens * slots
    g = heads
    first, final = place < heads, place >= shard_count - heads
    hid = (place % heads + jnp.where(first, 0, BEFORE) + jnp.where(final, 0, AFTER)).astype(jnp.int32).reshape(1)

    def exchange(x):
        return lax.all_to_all(x, "ctx", 0, 0, axis_index_groups=group_lists, tiled=True)

    def by_head(x):
        return x.reshape(x.shape[0], heads, HEAD).transpose(1, 0, 2)

    def slots_by_head(x):
        return x.reshape(x.shape[0], slots, heads, HEAD).transpose(2, 0, 1, 3).reshape(heads, -1, HEAD)

    high = lax.reduce_precision(beta_logit, 8, 7)
    rest = beta_logit - high
    middle = lax.reduce_precision(rest, 8, 7)
    betas = jnp.stack([high, middle, rest - middle], axis=2)
    betas = betas.transpose(3, 1, 2, 0).reshape(heads, 3 * slots, tokens).astype(BF16)
    betas = jnp.pad(betas, ((0, 0), (0, EDGE - 3 * slots), (0, 0)))
    last = EDGE // slots
    kb = exchange(
        jnp.concatenate(
            [slots_by_head(key_in), betas, slots_by_head(value_in[-last:]), by_head(query_in[-EDGE:])], axis=1
        )
    )

    group = place // heads
    tail = jnp.concatenate([kb[g - 1, rows - EDGE : rows], kb[g - 1, rows + EDGE :]], axis=0)

    grad_normed = jnp.dot(grad_out, out_weight.T, preferred_element_type=F32).astype(BF16)
    vq = jnp.concatenate([slots_by_head(value_in), by_head(query_in), by_head(grad_normed)], axis=1)
    vq, tail = lax.optimization_barrier((vq, tail))
    tail = lax.ppermute(tail, "ctx", [(i, (i + heads) % shard_count) for i in range(shard_count)])
    vq, tail = lax.optimization_barrier((vq, tail))
    vq = exchange(vq)

    wts = jnp.concatenate(
        [
            jnp.tile(key_conv, (1, 8 // slots, 1)).reshape(8 * TAPS, width),
            jnp.tile(value_conv, (1, 8 // slots, 1)).reshape(8 * TAPS, width),
            query_conv,
            norm_gain.reshape(1, width),
            jnp.zeros((3, width), F32),
        ],
        axis=0,
    )
    per = 4 if g % 4 == 0 else 1
    steps = g // per

    def pad(n):
        return [pltpu.VMEM((per, n + EDGE + 8, HEAD), F32)]

    def big(name, *shape, per=per, kind=F32):
        return (name, (g,) + shape, kind, per)

    live = {}
    wide = 4 if g % 4 == 0 else per
    (m_end,) = call(
        functools.partial(inverse_kernel, wide, tokens, slots),
        hid,
        g // wide,
        live,
        [(kb, wide), (kb, ("prev", wide, rows - EDGE)), (tail, None), (wts, "weights")],
        [],
        [big(name, rows, HEAD, per=wide, kind=BF16) for name in ("kh", "kl")]
        + [big(name, rows, rows, per=wide, kind=BF16) for name in ("xh", "xl", "th", "tl")]
        + [big(name, rows, HEAD, per=wide, kind=BF16) for name in ("wh", "wl")]
        + [
            big("fk", rows, HEAD, per=wide), big("a", HEAD, HEAD, per=wide), big("m", HEAD, HEAD, per=wide),
            (None, (HEAD, HEAD), F32, None),
        ],
        scratch=[pltpu.VMEM((wide, rows + EDGE + 8, HEAD), F32), pltpu.VMEM((HEAD, HEAD), F32)],
        us=11.0,
        grant=40,
    )
    beta = (kb, ("rows", per, rows))
    (c_end,) = call(
        functools.partial(maps_kernel, per, tokens, slots),
        hid,
        steps,
        live,
        [(vq, per), (vq, ("prev", per, rows - EDGE)), beta, (tail, None), (wts, "weights")],
        [(name, per) for name in ("kh", "kl", "xh", "xl", "a", "m")],
        [
            big("u", rows, HEAD), big("c", HEAD, HEAD), big("an", HEAD, HEAD), big("mn", HEAD, HEAD),
            big("fv", rows, HEAD), (None, (HEAD, HEAD), F32, None),
        ],
        scratch=pad(rows) + [pltpu.VMEM((HEAD, HEAD), F32)],
        us=6.0,
    )

    def across(last, towards):
        if groups == 1:
            return jnp.zeros((HEAD, HEAD), F32)
        if groups == 2:
            moves = [(i, (i + towards * heads) % shard_count) for i in range(shard_count)]
            return lax.ppermute(last[1], "ctx", moves)
        every = lax.all_gather(jnp.concatenate(last, axis=1), "ctx")
        head = place % heads
        ahead = group if towards > 0 else groups - 1 - group

        def advance(i, state):
            source = i if towards > 0 else groups - 1 - i
            item = lax.dynamic_index_in_dim(every, source * heads + head, 0, False)
            return jnp.dot(item[:, :HEAD], state, precision=lax.Precision.HIGHEST) + item[:, HEAD:]

        return lax.fori_loop(0, ahead, advance, jnp.zeros((HEAD, HEAD), F32))

    start = across((m_end, c_end), 1)
    call(
        functools.partial(queries_kernel, per, tokens, slots),
        hid,
        steps,
        live,
        [(vq, per), (vq, ("prev", per, rows + tokens - EDGE)), (tail, None), (wts, "weights")],
        [(name, per) for name in ("kh", "kl", "wh", "wl", "u")],
        [
            big("q", tokens, HEAD), big("sc", tokens, rows), big("qm", tokens, HEAD), big("ol", tokens, HEAD),
            big("fq", tokens, HEAD),
        ],
        scratch=pad(tokens),
        us=8.0,
    )
    normed, back_end = call(
        functools.partial(outs_kernel, g, tokens, slots),
        hid,
        1,
        live,
        [(vq, g), (wts, "weights"), (start, None)],
        [(name, g) for name in ("mn", "c", "qm", "ol", "an")],
        [
            big("st", HEAD, HEAD, per=g), big("dr", tokens, HEAD, per=g), big("mb", HEAD, 2 * HEAD, per=g),
            (None, (g, tokens, HEAD), BF16, g), (None, (HEAD, 2 * HEAD), F32, None),
        ],
        us=4.0,
    )
    finish = across((back_end[:, :HEAD], back_end[:, HEAD:]), -1)
    (nq,) = call(
        functools.partial(query_grads_kernel, per, tokens, slots),
        hid,
        steps,
        live,
        [(wts, "weights"), (normed, per)],
        [(name, per) for name in ("kh", "kl", "wh", "wl", "u", "q", "sc", "dr", "st", "fq", "mb")],
        [
            big("d", rows, HEAD), big("dk", rows, HEAD), big("dd", rows, HEAD), big("stf", HEAD, HEAD),
            big("mbf", HEAD, 2 * HEAD), (None, (g, 2 * tokens + EDGE, HEAD), BF16, per),
        ],
        scratch=pad(tokens),
        us=20.0,
    )
    nq = exchange(nq)
    (grads,) = call(
        functools.partial(grads_kernel, per, tokens, slots),
        hid,
        steps,
        live,
        [beta, (wts, "weights"), (finish, None)],
        [(name, per) for name in ("mbf", "kh", "kl", "th", "tl", "d", "dk", "dd", "stf", "fk", "fv")],
        [(None, (g, 2 * rows + 2 * EDGE, HEAD), BF16, per)],
        scratch=[pltpu.VMEM((2 * per, rows + EDGE + 8, HEAD), F32)],
        us=20.0,
    )
    grads = exchange(grads)

    normed_bf = nq[:, :tokens].transpose(1, 0, 2).reshape(tokens, width)
    partial = jnp.dot(normed_bf, out_weight, preferred_element_type=F32)
    if lax.axis_size("head") == 2:
        half = tokens // 2
        mine = lax.axis_index("head")
        pieces = partial.reshape(2, half, partial.shape[1])
        kept = lax.dynamic_index_in_dim(pieces, mine, 0, False)
        sent = lax.dynamic_index_in_dim(pieces, 1 - mine, 0, False).astype(BF16)
        layer_out = (kept + lax.ppermute(sent, "head", [(0, 1), (1, 0)]).astype(F32)).astype(BF16)
    else:
        layer_out = lax.psum_scatter(partial.astype(BF16), "head", scatter_dimension=0, tiled=True)

    rim = jnp.concatenate([nq[:, 2 * tokens : 2 * tokens + 8], grads[:, 2 * rows + EDGE :]], axis=1)
    rim = lax.ppermute(rim, "ctx", [(i, i - 1) for i in range(1, shard_count)])
    part = lambda x: pl.BlockSpec((1,) + x.shape[1:], lambda h: (h, 0, 0))
    small = pltpu.CompilerParams(vmem_limit_bytes=8 << 20)
    cost = lambda us: pl.CostEstimate(flops=int(us * 1.1e9), bytes_accessed=1 << 16, transcendentals=0)
    grad_query = pl.pallas_call(
        functools.partial(unpack_query_kernel, tokens),
        grid=(heads,),
        in_specs=[part(nq)],
        out_specs=pl.BlockSpec((tokens, HEAD), lambda h: (0, h)),
        out_shape=jax.ShapeDtypeStruct((tokens, width), F32),
        compiler_params=small,
        cost_estimate=cost(2.0),
    )(nq)
    grad_key, grad_value = pl.pallas_call(
        functools.partial(unpack_kernel, per, tokens, slots),
        grid=(steps,),
        in_specs=[pl.BlockSpec((per,) + grads.shape[1:], lambda h: (h, 0, 0))],
        out_specs=[pl.BlockSpec((tokens, slots, per * HEAD), lambda h: (0, 0, h))] * 2,
        out_shape=[jax.ShapeDtypeStruct((tokens, slots, width), F32)] * 2,
        compiler_params=small,
        cost_estimate=cost(10.0),
    )(grads)
    flat = pl.BlockSpec((8, width), lambda i: (tokens // 8 - 1, 0))
    deep = pl.BlockSpec((8 // slots, slots, width), lambda i: (tokens * slots // 8 - 1, 0, 0))
    mark = pl.BlockSpec((heads, EDGE, tokens), lambda i: (0, 2 * rows // EDGE, 0))
    beta_spec = pl.BlockSpec((slots, heads, tokens), lambda i: (0, 0, 0))
    grad_query, grad_key, grad_value, grad_beta = pl.pallas_call(
        functools.partial(rims_kernel, heads, slots),
        grid=(1,),
        in_specs=[pl.BlockSpec(rim.shape, lambda i: (0, 0, 0)), flat, deep, deep, mark],
        out_specs=[flat, deep, deep, beta_spec],
        out_shape=[jax.ShapeDtypeStruct(x.shape, F32) for x in (grad_query, grad_key, grad_value)]
        + [jax.ShapeDtypeStruct((slots, heads, tokens), F32)],
        input_output_aliases={1: 0, 2: 1, 3: 2},
        compiler_params=small,
    )(rim, grad_query, grad_key, grad_value, grads)
    grad_beta = grad_beta.transpose(2, 0, 1)
    return (layer_out, grad_query, grad_key, grad_value, grad_beta)


def solution(mesh):
    placed = (
        P("ctx", "head"),
        P("ctx", None, "head"),
        P("ctx", None, "head"),
        P("ctx", None, "head"),
        P(None, "head"),
        P(None, None, "head"),
        P(None, None, "head"),
        P("head"),
        P("head", None),
        P("ctx", None),
    )
    return jax.shard_map(
        shards,
        mesh=mesh,
        in_specs=placed,
        out_specs=(
            P(("ctx", "head"), None),
            P("ctx", "head"),
            P("ctx", None, "head"),
            P("ctx", None, "head"),
            P("ctx", None, "head"),
        ),
        check_vma=False,
    )
```

```python
import functools

import jax
import jax.numpy as jnp
from jax import lax
from jax.experimental import pallas as pl
from jax.experimental.pallas import tpu as pltpu
from jax.sharding import PartitionSpec as P

HEAD = 128
TAPS = 4
RIM = TAPS - 1
EDGE = 16
EPS = 1e-06
BEFORE = 1 << 16
AFTER = 1 << 17
F32 = jnp.float32
BF16 = jnp.bfloat16

ROWS_COLS = (((1,), (0,)), ((), ()))
ROWS_ROWS = (((1,), (1,)), ((), ()))
COLS_COLS = (((0,), (0,)), ((), ()))


def two(x):
    high = x.astype(BF16)
    return high, (x - high.astype(F32)).astype(BF16)


def dot(a, b, dims):
    return lax.dot_general(a, b, dims, preferred_element_type=F32)


def mm(left, right, dims=ROWS_COLS):
    (ah, al), (bh, bl) = left, right
    ka, kb = dims[0][0][0], dims[0][1][0]
    nb = 1 - kb
    depth, cols = ah.shape[ka], bh.shape[nb]
    if depth <= HEAD:
        a = jnp.concatenate([ah, al], axis=ka)
        high, low = jnp.concatenate([bh, bh], axis=kb), jnp.concatenate([bl, bl], axis=kb)
        if cols <= HEAD:
            out = dot(a, jnp.concatenate([high, low], axis=nb), dims)
            return out[:, :cols] + out[:, cols:]
        return dot(a, high, dims) + dot(a, low, dims)
    if cols <= HEAD:
        out = dot(ah, jnp.concatenate([bh, bl], axis=nb), dims)
        return out[:, :cols] + out[:, cols:] + dot(al, bh, dims)
    return dot(ah, bh, dims) + dot(ah, bl, dims) + dot(al, bh, dims)


def piece(x, row, col=None):
    cols = slice(None) if col is None else slice(col * HEAD, (col + 1) * HEAD)
    return tuple(p[row * HEAD : (row + 1) * HEAD, cols] for p in x)


def lower_times(x, b):
    count = x[0].shape[0] // HEAD
    return jnp.concatenate(
        [sum(mm(piece(x, i, j), piece(b, j)) for j in range(i + 1)) for i in range(count)], axis=0
    )


def mm_half(left, right, dims=ROWS_COLS):
    (ah, al), (bh, _) = left, right
    ka, kb = dims[0][0][0], dims[0][1][0]
    return dot(jnp.concatenate([ah, al], axis=ka), jnp.concatenate([bh, bh], axis=kb), dims)


def grid_of(rows, cols):
    return lax.broadcasted_iota(jnp.int32, (rows, cols), 0), lax.broadcasted_iota(jnp.int32, (rows, cols), 1)


def before(rows):
    r, c = grid_of(rows, rows)
    return c < r


def level_pairs(rows, level):
    r, c = grid_of(rows, rows)
    return ((r >> (level + 1)) == (c >> (level + 1))) & (((r >> level) & 1) == 1) & (((c >> level) & 1) == 0)


def visible(tokens, slots):
    t, c = grid_of(tokens, tokens * slots)
    return c < slots * (t + 1)


def times(pattern, x):
    if pattern.shape[0] == 1:
        return pattern * x
    return (x.reshape(-1, 8, HEAD) * pattern[None]).reshape(x.shape)


def conv_rows(x, edge, taps, pad, stride):
    rows = x.shape[0]
    pad[pl.ds(0, EDGE), :] = edge
    pad[pl.ds(EDGE, rows), :] = x
    total = None
    for i in range(TAPS):
        part = times(taps[i], pad[pl.ds(EDGE - stride * (RIM - i), rows), :])
        total = part if total is None else total + part
    return total


def conv_back(grad, taps, pad, stride):
    rows = grad.shape[0]
    pad[pl.ds(8, 8), :] = jnp.zeros((8, HEAD), F32)
    pad[pl.ds(EDGE, rows), :] = grad
    pad[pl.ds(EDGE + rows, 8), :] = jnp.zeros((8, HEAD), F32)
    inner, rim = None, None
    for i in range(TAPS):
        part = times(taps[i], pad[pl.ds(EDGE + stride * (RIM - i), rows), :])
        edge = times(taps[i], pad[pl.ds(8 + stride * (RIM - i), 8), :])
        inner = part if inner is None else inner + part
        rim = edge if rim is None else rim + edge
    return inner, rim


def sigmoid(x):
    return 1.0 / (1.0 + jnp.exp(-x))


def silu(s):
    sg = sigmoid(s)
    return s * sg, sg * (1.0 + s * (1.0 - sg))


def unit(values):
    scale = lax.rsqrt(jnp.sum(values * values, axis=-1, keepdims=True) + EPS)
    return values * scale, scale


def beta_rows(tile, slots):
    return [tile[3 * j : 3 * j + 1] + tile[3 * j + 1 : 3 * j + 2] + tile[3 * j + 2 : 3 * j + 3] for j in range(slots)]


def places(tokens, slots, j):
    r, t = grid_of(tokens * slots, tokens)
    return r == slots * t + j


def column(rows, tokens, slots):
    spread = jnp.zeros((tokens * slots, tokens), F32)
    for j in range(slots):
        spread = jnp.where(places(tokens, slots, j), rows[j], spread)
    return jnp.sum(spread, axis=1, keepdims=True)


def slot_taps(wts, kind):
    return [wts[8 * (TAPS * kind + i) : 8 * (TAPS * kind + i + 1)] for i in range(TAPS)]


def query_taps(wts):
    return [wts[16 * TAPS + i : 16 * TAPS + i + 1] for i in range(TAPS)]


def gain_row(wts):
    return wts[17 * TAPS : 17 * TAPS + 1]


def edges(hid, ref, first, rows, per, tail, prev_ref):
    tail = jnp.where((hid[0] & BEFORE) > 0, tail, 0.0)
    prev = jnp.where(pl.program_id(0) == 0, tail, prev_ref[0].astype(F32))
    return [prev] + [ref[n, pl.ds(first + rows - EDGE, EDGE), :].astype(F32) for n in range(per - 1)]


def inverse_kernel(
    per, tokens, slots, hid, kb_ref, prev_ref, tail_ref, wts_ref,
    kh_ref, kl_ref, xh_ref, xl_ref, th_ref, tl_ref, wh_ref, wl_ref, fk_ref, a_ref, m_ref, end_ref, pad, carry,
):
    rows = tokens * slots
    step = pl.program_id(0)
    taps = slot_taps(wts_ref[...], 0)
    tops = edges(hid, kb_ref, 0, rows, per, tail_ref[pl.ds(0, EDGE), :].astype(F32), prev_ref)
    order = before(HEAD)
    blocks = rows // HEAD
    ir, ic = grid_of(HEAD, HEAD)

    @pl.when(step == 0)
    def _():
        carry[...] = (ir == ic).astype(F32)

    grams, keys, scaled, strengths = [], [], [], []
    for n in range(per):
        s = conv_rows(kb_ref[n, pl.ds(0, rows), :].astype(F32), tops[n], taps, pad.at[n], slots)
        c, slope = silu(s)
        k, scale = unit(c)
        fk_ref[n] = scale * slope
        betas = beta_rows(kb_ref[n, pl.ds(rows, EDGE), :].astype(F32), slots)
        strength = 2.0 * sigmoid(column(betas, tokens, slots))
        k2 = two(k)
        kh_ref[n], kl_ref[n] = k2
        keys.append(k2)
        scaled.append(two(strength * k))
        strengths.append(strength)
        grams.append({})
    for i in range(blocks):
        for j in range(i + 1):
            for n in range(per):
                part = mm(piece(keys[n], i), piece(keys[n], j), ROWS_ROWS) * strengths[n][i * HEAD : (i + 1) * HEAD]
                grams[n][i, j] = jnp.where(order, part, 0.0) if i == j else part
    eye = (ir == ic).astype(F32)
    zero = jnp.zeros((HEAD, HEAD), BF16)
    diagonal = [gram[b, b] for gram in grams for b in range(blocks)]
    systems = [two(x) for x in diagonal]
    pairs = level_pairs(HEAD, 0)
    inverse = [eye - jnp.where(pairs, x, 0.0) for x in diagonal]
    level = 1
    while (1 << level) < HEAD:
        pairs = level_pairs(HEAD, level)
        split = [two(x) for x in inverse]
        crossed = [mm(tuple(jnp.where(pairs, p, zero) for p in s), x) for s, x in zip(systems, split)]
        inverse = [x - mm(s, two(y)) for x, s, y in zip(inverse, split, crossed)]
        level += 1
    halves = [{(b, b): two(inverse[n * blocks + b]) for b in range(blocks)} for n in range(per)]
    for j in range(blocks):
        for i in range(j + 1, blocks):
            cross = [
                two(sum(mm(two(grams[n][i, m]), halves[n][m, j]) for m in range(j, i))) for n in range(per)
            ]
            found = [two(-mm(halves[n][i, i], cross[n])) for n in range(per)]
            for n in range(per):
                halves[n][i, j] = found[n]
    nothing = jnp.zeros((HEAD, HEAD), BF16)
    whole = [
        tuple(
            jnp.concatenate(
                [
                    jnp.concatenate([halves[n][i, j][p] if j <= i else nothing for j in range(blocks)], axis=1)
                    for i in range(blocks)
                ],
                axis=0,
            )
            for p in range(2)
        )
        for n in range(per)
    ]
    ws = [two(lower_times(whole[n], scaled[n])) for n in range(per)]
    steps = [eye - mm(keys[n], ws[n], COLS_COLS) for n in range(per)]
    for n in range(per):
        xh_ref[n], xl_ref[n] = whole[n]
        th_ref[n], tl_ref[n] = whole[n][0].T, whole[n][1].T
        wh_ref[n], wl_ref[n] = ws[n]
        a_ref[n] = steps[n]
    state = carry[...]
    for n in range(per):
        m_ref[n] = state
        state = mm(two(steps[n]), two(state))
    carry[...] = state
    end_ref[...] = state


def maps_kernel(
    per, tokens, slots, hid, vq_ref, prev_ref, beta_ref, tail_ref, wts_ref, kh_ref, kl_ref, xh_ref, xl_ref, a_ref,
    m_ref,
    u_ref, c_ref, an_ref, mn_ref, fv_ref, end_ref, pad, carry,
):

    rows = tokens * slots
    taps = slot_taps(wts_ref[...], 1)

    @pl.when(pl.program_id(0) == 0)
    def _():
        carry[...] = jnp.zeros((HEAD, HEAD), F32)

    tail = tail_ref[pl.ds(EDGE, EDGE), :].astype(F32)
    tops = edges(hid, vq_ref, 0, rows, per, tail, prev_ref)
    rights = []
    for n in range(per):
        s = conv_rows(vq_ref[n, pl.ds(0, rows), :].astype(F32), tops[n], taps, pad.at[n], slots)
        v, fv_ref[n] = silu(s)
        betas = beta_rows(beta_ref[n].astype(F32), slots)
        rights.append(two(2.0 * sigmoid(column(betas, tokens, slots)) * v))
    us = [lower_times((xh_ref[n], xl_ref[n]), rights[n]) for n in range(per)]
    maps = [mm((kh_ref[n], kl_ref[n]), two(us[n]), COLS_COLS) for n in range(per)]
    state = carry[...]
    for n in range(per):
        u_ref[n] = us[n]
        c_ref[n] = state
        an_ref[n], mn_ref[n] = a_ref[n], m_ref[n]
        state = mm(two(a_ref[n]), two(state)) + maps[n]
    carry[...] = state
    end_ref[...] = state


def queries_kernel(
    per, tokens, slots, hid, vq_ref, prev_ref, tail_ref, wts_ref, kh_ref, kl_ref, wh_ref, wl_ref, u_ref,
    q_ref, sc_ref, qm_ref, ol_ref, fq_ref, pad,
):
    rows = tokens * slots
    taps = query_taps(wts_ref[...])
    tail = tail_ref[pl.ds(2 * EDGE, EDGE), :].astype(F32)
    tops = edges(hid, vq_ref, rows, tokens, per, tail, prev_ref)
    seen = visible(tokens, slots)
    qs = []
    for n in range(per):
        s = conv_rows(vq_ref[n, pl.ds(rows, tokens), :].astype(F32), tops[n], taps, pad.at[n], 1)
        c, slope = silu(s)
        q, scale = unit(c)
        fq_ref[n] = scale * slope
        q_ref[n] = q
        qs.append(q)
    scores = [
        jnp.where(seen, mm(two(qs[n]), (kh_ref[n], kl_ref[n]), ROWS_ROWS), 0.0) for n in range(per)
    ]
    mapped = []
    for n in range(per):
        uh, ul = two(u_ref[n])
        both = jnp.concatenate([wh_ref[n], uh], axis=1), jnp.concatenate([wl_ref[n], ul], axis=1)
        mapped.append(mm(two(scores[n]), both))
    for n in range(per):
        sc_ref[n] = scores[n]
        qm_ref[n] = qs[n] - mapped[n][:, :HEAD]
        ol_ref[n] = mapped[n][:, HEAD:]


def outs_kernel(
    per, tokens, slots, hid, vq_ref, wts_ref, start_ref, m_ref, c_ref, qm_ref, ol_ref, a_ref,
    st_ref, dr_ref, mb_ref, nm_ref, end_ref,
):
    rows = tokens * slots
    gain = gain_row(wts_ref[...])
    start = two(jnp.where((hid[0] & BEFORE) > 0, start_ref[...], 0.0))
    states = [mm(two(m_ref[n]), start) + c_ref[n] for n in range(per)]
    mapped = [two(qm_ref[n]) for n in range(per)]
    raws = [mm(mapped[n], two(states[n])) + ol_ref[n] for n in range(per)]
    local = []
    for n in range(per):
        st_ref[n] = states[n]
        raw = raws[n]
        scale = lax.rsqrt(jnp.mean(raw * raw, axis=-1, keepdims=True) + EPS)
        hat = raw * scale
        nm_ref[n] = (hat * gain).astype(BF16)
        dn = vq_ref[n, pl.ds(rows + tokens, tokens), :].astype(F32) * gain
        dr = scale * (dn - hat * jnp.mean(dn * hat, axis=-1, keepdims=True))
        dr_ref[n] = dr
        local.append(mm(mapped[n], two(dr), COLS_COLS))
    ir, ic = grid_of(HEAD, 2 * HEAD)
    state = (ir == ic).astype(F32)
    for n in range(per - 1, -1, -1):
        mb_ref[n] = state
        moved = mm(two(a_ref[n]), two(state), COLS_COLS)
        state = moved + jnp.concatenate([jnp.zeros((HEAD, HEAD), F32), local[n]], axis=1)
    end_ref[...] = state


def query_grads_kernel(
    per, tokens, slots, hid, wts_ref, nm_ref, kh_ref, kl_ref, wh_ref, wl_ref, u_ref, q_ref, sc_ref, dr_ref, st_ref,
    fq_ref, mb_ref, d_ref, dk_ref, dd_ref, stf_ref, mbf_ref, nq_ref, pad,
):
    taps = query_taps(wts_ref[...])
    seen = visible(tokens, slots)
    chunks = range(per)
    for n in chunks:
        stf_ref[n], mbf_ref[n] = st_ref[n], mb_ref[n]
    states = [two(st_ref[n]) for n in chunks]
    drs = [two(dr_ref[n]) for n in chunks]
    keys = [(kh_ref[n], kl_ref[n]) for n in chunks]
    qs = [q_ref[n] for n in chunks]
    found = [u_ref[n] - mm((wh_ref[n], wl_ref[n]), states[n]) for n in chunks]
    dss = [two(jnp.where(seen, mm(drs[n], two(found[n]), ROWS_ROWS), 0.0)) for n in chunks]
    for n in chunks:
        d_ref[n] = found[n]
        dd_ref[n] = mm(two(sc_ref[n]), drs[n], COLS_COLS)
    dqs = [mm(drs[n], states[n], ROWS_ROWS) + mm(dss[n], keys[n]) for n in chunks]
    for n in chunks:
        dk_ref[n] = mm(dss[n], two(qs[n]), COLS_COLS)
    for n in chunks:
        part = fq_ref[n] * (dqs[n] - qs[n] * jnp.sum(qs[n] * dqs[n], axis=-1, keepdims=True))
        inner, rim = conv_back(part, taps, pad.at[n], 1)
        nq_ref[n, pl.ds(0, tokens), :] = nm_ref[n]
        nq_ref[n, pl.ds(tokens, tokens), :] = inner.astype(BF16)
        nq_ref[n, pl.ds(2 * tokens, EDGE), :] = jnp.concatenate([rim, jnp.zeros((8, HEAD), F32)], axis=0).astype(BF16)


def grads_kernel(
    per, tokens, slots, hid, beta_ref, wts_ref, end_ref, mb_ref, kh_ref, kl_ref, th_ref, tl_ref, d_ref, dk_ref, dd_ref,
    st_ref, fk_ref, fv_ref, out_ref, pad,
):
    rows = tokens * slots
    wts = wts_ref[...]
    order = before(rows)
    end = two(jnp.where((hid[0] & AFTER) > 0, end_ref[...], 0.0))
    chunks = range(per)
    keys = [(kh_ref[n], kl_ref[n]) for n in chunks]
    gs = [two(mm(two(mb_ref[n, :, pl.ds(0, HEAD)]), end) + mb_ref[n, :, pl.ds(HEAD, HEAD)]) for n in chunks]
    dds = [two(dd_ref[n] + mm(keys[n], gs[n])) for n in chunks]
    ys = [mm((th_ref[n], tl_ref[n]), dds[n]) for n in chunks]
    betas = [beta_rows(beta_ref[n].astype(F32), slots) for n in chunks]
    des = [2.0 * sigmoid(column(betas[n], tokens, slots)) * ys[n] for n in chunks]
    halves = [two(des[n]) for n in chunks]
    ds = [two(d_ref[n]) for n in chunks]
    grams = [jnp.where(order, mm_half(halves[n], ds[n], ROWS_ROWS), 0.0) for n in chunks]
    direct = [
        dk_ref[n] + mm(ds[n], gs[n], ROWS_ROWS) - mm(halves[n], two(st_ref[n]), ROWS_ROWS) for n in chunks
    ]
    dks = [direct[n] - mm(two(grams[n] + grams[n].T), keys[n]) for n in chunks]
    for n in chunks:
        along = jnp.sum(ys[n] * d_ref[n], axis=1, keepdims=True)
        marks = []
        for j in range(slots):
            gb = jnp.sum(jnp.where(places(tokens, slots, j), along, 0.0), axis=0, keepdims=True)
            gb = gb * sigmoid(-betas[n][j])
            high = gb.astype(BF16).astype(F32)
            marks += [high, gb - high]
        marks.append(jnp.zeros((EDGE - 2 * slots, tokens), F32))
        value, value_rim = conv_back(fv_ref[n] * des[n], slot_taps(wts, 1), pad.at[2 * n], slots)
        k = keys[n][0].astype(F32) + keys[n][1].astype(F32)
        part = fk_ref[n] * (dks[n] - k * jnp.sum(k * dks[n], axis=-1, keepdims=True))
        key, key_rim = conv_back(part, slot_taps(wts, 0), pad.at[2 * n + 1], slots)
        out_ref[n, pl.ds(0, rows), :] = key.astype(BF16)
        out_ref[n, pl.ds(rows, rows), :] = value.astype(BF16)
        out_ref[n, pl.ds(2 * rows, EDGE), :] = jnp.concatenate(marks, axis=0).astype(BF16)
        out_ref[n, pl.ds(2 * rows + EDGE, EDGE), :] = jnp.concatenate([key_rim, value_rim], axis=0).astype(BF16)


def unpack_kernel(per, tokens, slots, got_ref, gk_ref, gv_ref):
    rows = tokens * slots
    for n in range(per):
        for a, out_ref in enumerate((gk_ref, gv_ref)):
            main = got_ref[n, pl.ds(a * rows, rows), :].astype(F32)
            out_ref[:, :, pl.ds(n * HEAD, HEAD)] = main.reshape(tokens, slots, HEAD)


def unpack_query_kernel(per, tokens, got_ref, gq_ref):
    for n in range(per):
        gq_ref[:, pl.ds(n * HEAD, HEAD)] = got_ref[n, pl.ds(tokens, tokens), :].astype(F32)


def rims_kernel(heads, slots, rim_ref, gq_ref, gk_ref, gv_ref, mark_ref, nq_ref, nk_ref, nv_ref, gb_ref):
    for h in range(heads):
        part = pl.ds(h * HEAD, HEAD)
        rim = rim_ref[h].astype(F32)
        nq_ref[:, part] = gq_ref[:, part] + rim[:8]
        nk_ref[:, :, part] = gk_ref[:, :, part] + rim[8:16].reshape(8 // slots, slots, HEAD)
        nv_ref[:, :, part] = gv_ref[:, :, part] + rim[16:].reshape(8 // slots, slots, HEAD)
        mark = mark_ref[h].astype(F32)
        for j in range(slots):
            gb_ref[j, pl.ds(h, 1), :] = mark[2 * j : 2 * j + 1] + mark[2 * j + 1 : 2 * j + 2]


FAR = ("kh", "kl", "xh", "xl", "th", "tl", "wh", "wl", "a", "m", "fk", "fv", "stf", "mbf", "d", "dk", "dd")


def call(kernel, hid, steps, live, ins, reads, outs, scratch=(), us=1.0, grant=40):
    def spec(shape, how):
        if how == "weights":
            return pl.BlockSpec((shape[0], HEAD), lambda i, h: (0, h[0] & (BEFORE - 1)))
        if how is None:
            return pl.BlockSpec(shape, lambda i, h: (0,) * len(shape))
        if isinstance(how, tuple):
            kind, count, row = how
            if kind == "prev":
                return pl.BlockSpec((1, EDGE, HEAD), lambda i, h: (jnp.maximum(i * count - 1, 0), row // EDGE, 0))
            return pl.BlockSpec((count, EDGE, HEAD), lambda i, h: (i, row // EDGE, 0))
        return pl.BlockSpec((how,) + tuple(shape[1:]), lambda i, h: (i,) + (0,) * (len(shape) - 1))

    def home(name):
        return pltpu.HBM if name in FAR else pltpu.VMEM

    operands = [a for a, _ in ins]
    operands += [pltpu.with_memory_space_constraint(live[name], home(name)) for name, _ in reads]
    hows = [how for _, how in ins + reads]
    results = pl.pallas_call(
        kernel,
        grid_spec=pltpu.PrefetchScalarGridSpec(
            num_scalar_prefetch=1,
            grid=(steps,),
            in_specs=[spec(a.shape, how) for a, how in zip(operands, hows)],
            out_specs=[spec(shape, how) for _, shape, _, how in outs],
            scratch_shapes=list(scratch),
        ),
        out_shape=[
            jax.ShapeDtypeStruct(shape, dtype) if name is None else home(name)(shape, dtype)
            for name, shape, dtype, _ in outs
        ],
        compiler_params=pltpu.CompilerParams(dimension_semantics=("arbitrary",), vmem_limit_bytes=grant << 20),
        cost_estimate=pl.CostEstimate(flops=int(us * 1.1e9), bytes_accessed=1 << 16, transcendentals=0),
    )(hid, *operands)
    for (name, _, _, _), result in zip(outs, results):
        if name is not None:
            live[name] = result
    return [r for (name, _, _, _), r in zip(outs, results) if name is None]


def shards(
    query_in,
    key_in,
    value_in,
    beta_logit,
    query_conv,
    key_conv,
    value_conv,
    norm_gain,
    out_weight,
    grad_out,
):
    tokens, slots = key_in.shape[0], key_in.shape[1]
    width = query_in.shape[1]
    heads = width // HEAD
    shard_count = lax.axis_size("ctx")
    place = lax.axis_index("ctx")
    groups = shard_count // heads
    group_lists = [[b * heads + i for i in range(heads)] for b in range(groups)]
    rows = tokens * slots
    g = heads
    first, final = place < heads, place >= shard_count - heads
    hid = (place % heads + jnp.where(first, 0, BEFORE) + jnp.where(final, 0, AFTER)).astype(jnp.int32).reshape(1)

    def exchange(x):
        return lax.all_to_all(x, "ctx", 0, 0, axis_index_groups=group_lists, tiled=True)

    def by_head(x):
        return x.reshape(x.shape[0], heads, HEAD).transpose(1, 0, 2)

    def slots_by_head(x):
        return x.reshape(x.shape[0], slots, heads, HEAD).transpose(2, 0, 1, 3).reshape(heads, -1, HEAD)

    high = lax.reduce_precision(beta_logit, 8, 7)
    rest = beta_logit - high
    middle = lax.reduce_precision(rest, 8, 7)
    betas = jnp.stack([high, middle, rest - middle], axis=2)
    betas = betas.transpose(3, 1, 2, 0).reshape(heads, 3 * slots, tokens).astype(BF16)
    betas = jnp.pad(betas, ((0, 0), (0, EDGE - 3 * slots), (0, 0)))
    last = EDGE // slots
    kb = exchange(
        jnp.concatenate(
            [slots_by_head(key_in), betas, slots_by_head(value_in[-last:]), by_head(query_in[-EDGE:])], axis=1
        )
    )

    group = place // heads
    tail = jnp.concatenate([kb[g - 1, rows - EDGE : rows], kb[g - 1, rows + EDGE :]], axis=0)

    grad_normed = jnp.dot(grad_out, out_weight.T, preferred_element_type=F32).astype(BF16)
    vq = jnp.concatenate([slots_by_head(value_in), by_head(query_in), by_head(grad_normed)], axis=1)
    vq, tail = lax.optimization_barrier((vq, tail))
    tail = lax.ppermute(tail, "ctx", [(i, (i + heads) % shard_count) for i in range(shard_count)])
    vq, tail = lax.optimization_barrier((vq, tail))
    vq = exchange(vq)

    wts = jnp.concatenate(
        [
            jnp.tile(key_conv, (1, 8 // slots, 1)).reshape(8 * TAPS, width),
            jnp.tile(value_conv, (1, 8 // slots, 1)).reshape(8 * TAPS, width),
            query_conv,
            norm_gain.reshape(1, width),
            jnp.zeros((3, width), F32),
        ],
        axis=0,
    )
    per = 4 if g % 4 == 0 else 1
    steps = g // per

    def pad(n):
        return [pltpu.VMEM((per, n + EDGE + 8, HEAD), F32)]

    def big(name, *shape, per=per, kind=F32):
        return (name, (g,) + shape, kind, per)

    live = {}
    wide = 4 if g % 4 == 0 else per
    (m_end,) = call(
        functools.partial(inverse_kernel, wide, tokens, slots),
        hid,
        g // wide,
        live,
        [(kb, wide), (kb, ("prev", wide, rows - EDGE)), (tail, None), (wts, "weights")],
        [],
        [big(name, rows, HEAD, per=wide, kind=BF16) for name in ("kh", "kl")]
        + [big(name, rows, rows, per=wide, kind=BF16) for name in ("xh", "xl", "th", "tl")]
        + [big(name, rows, HEAD, per=wide, kind=BF16) for name in ("wh", "wl")]
        + [
            big("fk", rows, HEAD, per=wide), big("a", HEAD, HEAD, per=wide), big("m", HEAD, HEAD, per=wide),
            (None, (HEAD, HEAD), F32, None),
        ],
        scratch=[pltpu.VMEM((wide, rows + EDGE + 8, HEAD), F32), pltpu.VMEM((HEAD, HEAD), F32)],
        us=11.0,
        grant=40,
    )
    beta = (kb, ("rows", per, rows))
    (c_end,) = call(
        functools.partial(maps_kernel, per, tokens, slots),
        hid,
        steps,
        live,
        [(vq, per), (vq, ("prev", per, rows - EDGE)), beta, (tail, None), (wts, "weights")],
        [(name, per) for name in ("kh", "kl", "xh", "xl", "a", "m")],
        [
            big("u", rows, HEAD), big("c", HEAD, HEAD), big("an", HEAD, HEAD), big("mn", HEAD, HEAD),
            big("fv", rows, HEAD), (None, (HEAD, HEAD), F32, None),
        ],
        scratch=pad(rows) + [pltpu.VMEM((HEAD, HEAD), F32)],
        us=6.0,
    )

    def across(last, towards):
        if groups == 1:
            return jnp.zeros((HEAD, HEAD), F32)
        if groups == 2:
            moves = [(i, (i + towards * heads) % shard_count) for i in range(shard_count)]
            return lax.ppermute(last[1], "ctx", moves)
        every = lax.all_gather(jnp.concatenate(last, axis=1), "ctx")
        head = place % heads
        ahead = group if towards > 0 else groups - 1 - group

        def advance(i, state):
            source = i if towards > 0 else groups - 1 - i
            item = lax.dynamic_index_in_dim(every, source * heads + head, 0, False)
            return jnp.dot(item[:, :HEAD], state, precision=lax.Precision.HIGHEST) + item[:, HEAD:]

        return lax.fori_loop(0, ahead, advance, jnp.zeros((HEAD, HEAD), F32))

    start = across((m_end, c_end), 1)
    call(
        functools.partial(queries_kernel, per, tokens, slots),
        hid,
        steps,
        live,
        [(vq, per), (vq, ("prev", per, rows + tokens - EDGE)), (tail, None), (wts, "weights")],
        [(name, per) for name in ("kh", "kl", "wh", "wl", "u")],
        [
            big("q", tokens, HEAD), big("sc", tokens, rows), big("qm", tokens, HEAD), big("ol", tokens, HEAD),
            big("fq", tokens, HEAD),
        ],
        scratch=pad(tokens),
        us=8.0,
    )
    normed, back_end = call(
        functools.partial(outs_kernel, g, tokens, slots),
        hid,
        1,
        live,
        [(vq, g), (wts, "weights"), (start, None)],
        [(name, g) for name in ("mn", "c", "qm", "ol", "an")],
        [
            big("st", HEAD, HEAD, per=g), big("dr", tokens, HEAD, per=g), big("mb", HEAD, 2 * HEAD, per=g),
            (None, (g, tokens, HEAD), BF16, g), (None, (HEAD, 2 * HEAD), F32, None),
        ],
        us=4.0,
    )
    finish = across((back_end[:, :HEAD], back_end[:, HEAD:]), -1)
    (nq,) = call(
        functools.partial(query_grads_kernel, per, tokens, slots),
        hid,
        steps,
        live,
        [(wts, "weights"), (normed, per)],
        [(name, per) for name in ("kh", "kl", "wh", "wl", "u", "q", "sc", "dr", "st", "fq", "mb")],
        [
            big("d", rows, HEAD), big("dk", rows, HEAD), big("dd", rows, HEAD), big("stf", HEAD, HEAD),
            big("mbf", HEAD, 2 * HEAD), (None, (g, 2 * tokens + EDGE, HEAD), BF16, per),
        ],
        scratch=pad(tokens),
        us=20.0,
    )
    nq = exchange(nq)
    (grads,) = call(
        functools.partial(grads_kernel, per, tokens, slots),
        hid,
        steps,
        live,
        [beta, (wts, "weights"), (finish, None)],
        [(name, per) for name in ("mbf", "kh", "kl", "th", "tl", "d", "dk", "dd", "stf", "fk", "fv")],
        [(None, (g, 2 * rows + 2 * EDGE, HEAD), BF16, per)],
        scratch=[pltpu.VMEM((2 * per, rows + EDGE + 8, HEAD), F32)],
        us=20.0,
    )
    grads = exchange(grads)

    normed_bf = nq[:, :tokens].transpose(1, 0, 2).reshape(tokens, width)
    partial = jnp.dot(normed_bf, out_weight, preferred_element_type=F32)
    if lax.axis_size("head") == 2:
        half = tokens // 2
        mine = lax.axis_index("head")
        pieces = partial.reshape(2, half, partial.shape[1])
        kept = lax.dynamic_index_in_dim(pieces, mine, 0, False)
        sent = lax.dynamic_index_in_dim(pieces, 1 - mine, 0, False).astype(BF16)
        layer_out = (kept + lax.ppermute(sent, "head", [(0, 1), (1, 0)]).astype(F32)).astype(BF16)
    else:
        layer_out = lax.psum_scatter(partial.astype(BF16), "head", scatter_dimension=0, tiled=True)

    rim = jnp.concatenate([nq[:, 2 * tokens : 2 * tokens + 8], grads[:, 2 * rows + EDGE :]], axis=1)
    rim = lax.ppermute(rim, "ctx", [(i, i - 1) for i in range(1, shard_count)])
    small = pltpu.CompilerParams(vmem_limit_bytes=8 << 20)
    cost = lambda us: pl.CostEstimate(flops=int(us * 1.1e9), bytes_accessed=1 << 16, transcendentals=0)
    grad_query = pl.pallas_call(
        functools.partial(unpack_query_kernel, per, tokens),
        grid=(steps,),
        in_specs=[pl.BlockSpec((per,) + nq.shape[1:], lambda h: (h, 0, 0))],
        out_specs=pl.BlockSpec((tokens, per * HEAD), lambda h: (0, h)),
        out_shape=jax.ShapeDtypeStruct((tokens, width), F32),
        compiler_params=small,
        cost_estimate=cost(2.0),
    )(nq)
    grad_key, grad_value = pl.pallas_call(
        functools.partial(unpack_kernel, per, tokens, slots),
        grid=(steps,),
        in_specs=[pl.BlockSpec((per,) + grads.shape[1:], lambda h: (h, 0, 0))],
        out_specs=[pl.BlockSpec((tokens, slots, per * HEAD), lambda h: (0, 0, h))] * 2,
        out_shape=[jax.ShapeDtypeStruct((tokens, slots, width), F32)] * 2,
        compiler_params=small,
        cost_estimate=cost(10.0),
    )(grads)
    flat = pl.BlockSpec((8, width), lambda i: (tokens // 8 - 1, 0))
    deep = pl.BlockSpec((8 // slots, slots, width), lambda i: (tokens * slots // 8 - 1, 0, 0))
    mark = pl.BlockSpec((heads, EDGE, tokens), lambda i: (0, 2 * rows // EDGE, 0))
    beta_spec = pl.BlockSpec((slots, heads, tokens), lambda i: (0, 0, 0))
    grad_query, grad_key, grad_value, grad_beta = pl.pallas_call(
        functools.partial(rims_kernel, heads, slots),
        grid=(1,),
        in_specs=[pl.BlockSpec(rim.shape, lambda i: (0, 0, 0)), flat, deep, deep, mark],
        out_specs=[flat, deep, deep, beta_spec],
        out_shape=[jax.ShapeDtypeStruct(x.shape, F32) for x in (grad_query, grad_key, grad_value)]
        + [jax.ShapeDtypeStruct((slots, heads, tokens), F32)],
        input_output_aliases={1: 0, 2: 1, 3: 2},
        compiler_params=small,
    )(rim, grad_query, grad_key, grad_value, grads)
    grad_beta = grad_beta.transpose(2, 0, 1)
    return (layer_out, grad_query, grad_key, grad_value, grad_beta)


def solution(mesh):
    placed = (
        P("ctx", "head"),
        P("ctx", None, "head"),
        P("ctx", None, "head"),
        P("ctx", None, "head"),
        P(None, "head"),
        P(None, None, "head"),
        P(None, None, "head"),
        P("head"),
        P("head", None),
        P("ctx", None),
    )
    return jax.shard_map(
        shards,
        mesh=mesh,
        in_specs=placed,
        out_specs=(
            P(("ctx", "head"), None),
            P("ctx", "head"),
            P("ctx", None, "head"),
            P("ctx", None, "head"),
            P("ctx", None, "head"),
        ),
        check_vma=False,
    )
```

```python
import functools

import jax
import jax.numpy as jnp
from jax import lax
from jax.experimental import pallas as pl
from jax.experimental.pallas import tpu as pltpu
from jax.sharding import PartitionSpec as P

HEAD = 128
TAPS = 4
RIM = TAPS - 1
EDGE = 16
EPS = 1e-06
BEFORE = 1 << 16
AFTER = 1 << 17
F32 = jnp.float32
BF16 = jnp.bfloat16

ROWS_COLS = (((1,), (0,)), ((), ()))
ROWS_ROWS = (((1,), (1,)), ((), ()))
COLS_COLS = (((0,), (0,)), ((), ()))


def two(x):
    high = x.astype(BF16)
    return high, (x - high.astype(F32)).astype(BF16)


def dot(a, b, dims):
    return lax.dot_general(a, b, dims, preferred_element_type=F32)


def mm(left, right, dims=ROWS_COLS):
    (ah, al), (bh, bl) = left, right
    ka, kb = dims[0][0][0], dims[0][1][0]
    nb = 1 - kb
    depth, cols = ah.shape[ka], bh.shape[nb]
    if depth <= HEAD:
        a = jnp.concatenate([ah, al], axis=ka)
        high, low = jnp.concatenate([bh, bh], axis=kb), jnp.concatenate([bl, bl], axis=kb)
        if cols <= HEAD:
            out = dot(a, jnp.concatenate([high, low], axis=nb), dims)
            return out[:, :cols] + out[:, cols:]
        return dot(a, high, dims) + dot(a, low, dims)
    if cols <= HEAD:
        out = dot(ah, jnp.concatenate([bh, bl], axis=nb), dims)
        return out[:, :cols] + out[:, cols:] + dot(al, bh, dims)
    return dot(ah, bh, dims) + dot(ah, bl, dims) + dot(al, bh, dims)


def piece(x, row, col=None):
    cols = slice(None) if col is None else slice(col * HEAD, (col + 1) * HEAD)
    return tuple(p[row * HEAD : (row + 1) * HEAD, cols] for p in x)


def lower_times(x, b):
    count = x[0].shape[0] // HEAD
    return jnp.concatenate(
        [sum(mm(piece(x, i, j), piece(b, j)) for j in range(i + 1)) for i in range(count)], axis=0
    )


def mm_half(left, right, dims=ROWS_COLS):
    (ah, al), (bh, _) = left, right
    ka, kb = dims[0][0][0], dims[0][1][0]
    return dot(jnp.concatenate([ah, al], axis=ka), jnp.concatenate([bh, bh], axis=kb), dims)


def grid_of(rows, cols):
    return lax.broadcasted_iota(jnp.int32, (rows, cols), 0), lax.broadcasted_iota(jnp.int32, (rows, cols), 1)


def before(rows):
    r, c = grid_of(rows, rows)
    return c < r


def level_pairs(rows, level):
    r, c = grid_of(rows, rows)
    return ((r >> (level + 1)) == (c >> (level + 1))) & (((r >> level) & 1) == 1) & (((c >> level) & 1) == 0)


def visible(tokens, slots):
    t, c = grid_of(tokens, tokens * slots)
    return c < slots * (t + 1)


def times(pattern, x):
    if pattern.shape[0] == 1:
        return pattern * x
    return (x.reshape(-1, 8, HEAD) * pattern[None]).reshape(x.shape)


def conv_rows(x, edge, taps, pad, stride):
    rows = x.shape[0]
    pad[pl.ds(0, EDGE), :] = edge
    pad[pl.ds(EDGE, rows), :] = x
    total = None
    for i in range(TAPS):
        part = times(taps[i], pad[pl.ds(EDGE - stride * (RIM - i), rows), :])
        total = part if total is None else total + part
    return total


def conv_back(grad, taps, pad, stride):
    rows = grad.shape[0]
    pad[pl.ds(8, 8), :] = jnp.zeros((8, HEAD), F32)
    pad[pl.ds(EDGE, rows), :] = grad
    pad[pl.ds(EDGE + rows, 8), :] = jnp.zeros((8, HEAD), F32)
    inner, rim = None, None
    for i in range(TAPS):
        part = times(taps[i], pad[pl.ds(EDGE + stride * (RIM - i), rows), :])
        edge = times(taps[i], pad[pl.ds(8 + stride * (RIM - i), 8), :])
        inner = part if inner is None else inner + part
        rim = edge if rim is None else rim + edge
    return inner, rim


def sigmoid(x):
    return 1.0 / (1.0 + jnp.exp(-x))


def silu(s):
    sg = sigmoid(s)
    return s * sg, sg * (1.0 + s * (1.0 - sg))


def unit(values):
    scale = lax.rsqrt(jnp.sum(values * values, axis=-1, keepdims=True) + EPS)
    return values * scale, scale


def beta_rows(tile, slots):
    return [tile[3 * j : 3 * j + 1] + tile[3 * j + 1 : 3 * j + 2] + tile[3 * j + 2 : 3 * j + 3] for j in range(slots)]


def places(tokens, slots, j):
    r, t = grid_of(tokens * slots, tokens)
    return r == slots * t + j


def column(rows, tokens, slots):
    spread = jnp.zeros((tokens * slots, tokens), F32)
    for j in range(slots):
        spread = jnp.where(places(tokens, slots, j), rows[j], spread)
    return jnp.sum(spread, axis=1, keepdims=True)


def slot_taps(wts, kind):
    return [wts[8 * (TAPS * kind + i) : 8 * (TAPS * kind + i + 1)] for i in range(TAPS)]


def query_taps(wts):
    return [wts[16 * TAPS + i : 16 * TAPS + i + 1] for i in range(TAPS)]


def gain_row(wts):
    return wts[17 * TAPS : 17 * TAPS + 1]


def edges(hid, ref, first, rows, per, tail, prev_ref):
    tail = jnp.where((hid[0] & BEFORE) > 0, tail, 0.0)
    prev = jnp.where(pl.program_id(0) == 0, tail, prev_ref[0].astype(F32))
    return [prev] + [ref[n, pl.ds(first + rows - EDGE, EDGE), :].astype(F32) for n in range(per - 1)]


def inverse_kernel(
    per, tokens, slots, hid, kb_ref, prev_ref, tail_ref, wts_ref,
    kh_ref, kl_ref, xh_ref, xl_ref, th_ref, tl_ref, wh_ref, wl_ref, fk_ref, a_ref, m_ref, end_ref, pad, carry,
):
    rows = tokens * slots
    step = pl.program_id(0)
    taps = slot_taps(wts_ref[...], 0)
    tops = edges(hid, kb_ref, 0, rows, per, tail_ref[pl.ds(0, EDGE), :].astype(F32), prev_ref)
    order = before(HEAD)
    blocks = rows // HEAD
    ir, ic = grid_of(HEAD, HEAD)

    @pl.when(step == 0)
    def _():
        carry[...] = (ir == ic).astype(F32)

    grams, keys, scaled, strengths = [], [], [], []
    for n in range(per):
        s = conv_rows(kb_ref[n, pl.ds(0, rows), :].astype(F32), tops[n], taps, pad.at[n], slots)
        c, slope = silu(s)
        k, scale = unit(c)
        fk_ref[n] = scale * slope
        betas = beta_rows(kb_ref[n, pl.ds(rows, EDGE), :].astype(F32), slots)
        strength = 2.0 * sigmoid(column(betas, tokens, slots))
        k2 = two(k)
        kh_ref[n], kl_ref[n] = k2
        keys.append(k2)
        scaled.append(two(strength * k))
        strengths.append(strength)
        grams.append({})
    for i in range(blocks):
        for j in range(i + 1):
            for n in range(per):
                part = mm(piece(keys[n], i), piece(keys[n], j), ROWS_ROWS) * strengths[n][i * HEAD : (i + 1) * HEAD]
                grams[n][i, j] = jnp.where(order, part, 0.0) if i == j else part
    eye = (ir == ic).astype(F32)
    zero = jnp.zeros((HEAD, HEAD), BF16)
    diagonal = [gram[b, b] for gram in grams for b in range(blocks)]
    systems = [two(x) for x in diagonal]
    pairs = level_pairs(HEAD, 0)
    inverse = [eye - jnp.where(pairs, x, 0.0) for x in diagonal]
    level = 1
    while (1 << level) < HEAD:
        pairs = level_pairs(HEAD, level)
        split = [two(x) for x in inverse]
        crossed = [mm(tuple(jnp.where(pairs, p, zero) for p in s), x) for s, x in zip(systems, split)]
        inverse = [x - mm(s, two(y)) for x, s, y in zip(inverse, split, crossed)]
        level += 1
    halves = [{(b, b): two(inverse[n * blocks + b]) for b in range(blocks)} for n in range(per)]
    for j in range(blocks):
        for i in range(j + 1, blocks):
            cross = [
                two(sum(mm(two(grams[n][i, m]), halves[n][m, j]) for m in range(j, i))) for n in range(per)
            ]
            found = [two(-mm(halves[n][i, i], cross[n])) for n in range(per)]
            for n in range(per):
                halves[n][i, j] = found[n]
    nothing = jnp.zeros((HEAD, HEAD), BF16)
    whole = [
        tuple(
            jnp.concatenate(
                [
                    jnp.concatenate([halves[n][i, j][p] if j <= i else nothing for j in range(blocks)], axis=1)
                    for i in range(blocks)
                ],
                axis=0,
            )
            for p in range(2)
        )
        for n in range(per)
    ]
    ws = [two(lower_times(whole[n], scaled[n])) for n in range(per)]
    steps = [eye - mm(keys[n], ws[n], COLS_COLS) for n in range(per)]
    for n in range(per):
        xh_ref[n], xl_ref[n] = whole[n]
        th_ref[n], tl_ref[n] = whole[n][0].T, whole[n][1].T
        wh_ref[n], wl_ref[n] = ws[n]
        a_ref[n] = steps[n]
    state = carry[...]
    for n in range(per):
        m_ref[n] = state
        state = mm(two(steps[n]), two(state))
    carry[...] = state
    end_ref[...] = state


def maps_kernel(
    per, tokens, slots, hid, vq_ref, prev_ref, beta_ref, tail_ref, wts_ref, kh_ref, kl_ref, xh_ref, xl_ref, a_ref,
    u_ref, c_ref, fv_ref, end_ref, pad, carry,
):

    rows = tokens * slots
    taps = slot_taps(wts_ref[...], 1)

    @pl.when(pl.program_id(0) == 0)
    def _():
        carry[...] = jnp.zeros((HEAD, HEAD), F32)

    tail = tail_ref[pl.ds(EDGE, EDGE), :].astype(F32)
    tops = edges(hid, vq_ref, 0, rows, per, tail, prev_ref)
    rights = []
    for n in range(per):
        s = conv_rows(vq_ref[n, pl.ds(0, rows), :].astype(F32), tops[n], taps, pad.at[n], slots)
        v, fv_ref[n] = silu(s)
        betas = beta_rows(beta_ref[n].astype(F32), slots)
        rights.append(two(2.0 * sigmoid(column(betas, tokens, slots)) * v))
    us = [lower_times((xh_ref[n], xl_ref[n]), rights[n]) for n in range(per)]
    maps = [mm((kh_ref[n], kl_ref[n]), two(us[n]), COLS_COLS) for n in range(per)]
    state = carry[...]
    for n in range(per):
        u_ref[n] = us[n]
        c_ref[n] = state
        state = mm(two(a_ref[n]), two(state)) + maps[n]
    carry[...] = state
    end_ref[...] = state


def queries_kernel(
    per, tokens, slots, hid, vq_ref, prev_ref, tail_ref, wts_ref, kh_ref, kl_ref, wh_ref, wl_ref, u_ref,
    a_ref, m_ref, q_ref, sc_ref, qm_ref, ol_ref, fq_ref, an_ref, mn_ref, pad,
):
    rows = tokens * slots
    taps = query_taps(wts_ref[...])
    tail = tail_ref[pl.ds(2 * EDGE, EDGE), :].astype(F32)
    tops = edges(hid, vq_ref, rows, tokens, per, tail, prev_ref)
    seen = visible(tokens, slots)
    qs = []
    for n in range(per):
        s = conv_rows(vq_ref[n, pl.ds(rows, tokens), :].astype(F32), tops[n], taps, pad.at[n], 1)
        c, slope = silu(s)
        q, scale = unit(c)
        fq_ref[n] = scale * slope
        q_ref[n] = q
        qs.append(q)
    scores = [
        jnp.where(seen, mm(two(qs[n]), (kh_ref[n], kl_ref[n]), ROWS_ROWS), 0.0) for n in range(per)
    ]
    mapped = []
    for n in range(per):
        uh, ul = two(u_ref[n])
        both = jnp.concatenate([wh_ref[n], uh], axis=1), jnp.concatenate([wl_ref[n], ul], axis=1)
        mapped.append(mm(two(scores[n]), both))
    for n in range(per):
        an_ref[n], mn_ref[n] = a_ref[n], m_ref[n]
        sc_ref[n] = scores[n]
        qm_ref[n] = qs[n] - mapped[n][:, :HEAD]
        ol_ref[n] = mapped[n][:, HEAD:]


def outs_kernel(
    per, tokens, slots, hid, vq_ref, wts_ref, start_ref, m_ref, c_ref, qm_ref, ol_ref, a_ref,
    st_ref, dr_ref, mb_ref, nm_ref, end_ref,
):
    rows = tokens * slots
    gain = gain_row(wts_ref[...])
    start = two(jnp.where((hid[0] & BEFORE) > 0, start_ref[...], 0.0))
    states = [mm(two(m_ref[n]), start) + c_ref[n] for n in range(per)]
    mapped = [two(qm_ref[n]) for n in range(per)]
    raws = [mm(mapped[n], two(states[n])) + ol_ref[n] for n in range(per)]
    local = []
    for n in range(per):
        st_ref[n] = states[n]
        raw = raws[n]
        scale = lax.rsqrt(jnp.mean(raw * raw, axis=-1, keepdims=True) + EPS)
        hat = raw * scale
        nm_ref[n] = (hat * gain).astype(BF16)
        dn = vq_ref[n, pl.ds(rows + tokens, tokens), :].astype(F32) * gain
        dr = scale * (dn - hat * jnp.mean(dn * hat, axis=-1, keepdims=True))
        dr_ref[n] = dr
        local.append(mm(mapped[n], two(dr), COLS_COLS))
    ir, ic = grid_of(HEAD, 2 * HEAD)
    state = (ir == ic).astype(F32)
    for n in range(per - 1, -1, -1):
        mb_ref[n] = state
        moved = mm(two(a_ref[n]), two(state), COLS_COLS)
        state = moved + jnp.concatenate([jnp.zeros((HEAD, HEAD), F32), local[n]], axis=1)
    end_ref[...] = state


def query_grads_kernel(
    per, tokens, slots, hid, wts_ref, nm_ref, kh_ref, kl_ref, wh_ref, wl_ref, u_ref, q_ref, sc_ref, dr_ref, st_ref,
    fq_ref, mb_ref, d_ref, dk_ref, dd_ref, stf_ref, mbf_ref, nq_ref, pad,
):
    taps = query_taps(wts_ref[...])
    seen = visible(tokens, slots)
    chunks = range(per)
    for n in chunks:
        stf_ref[n], mbf_ref[n] = st_ref[n], mb_ref[n]
    states = [two(st_ref[n]) for n in chunks]
    drs = [two(dr_ref[n]) for n in chunks]
    keys = [(kh_ref[n], kl_ref[n]) for n in chunks]
    qs = [q_ref[n] for n in chunks]
    found = [u_ref[n] - mm((wh_ref[n], wl_ref[n]), states[n]) for n in chunks]
    dss = [two(jnp.where(seen, mm(drs[n], two(found[n]), ROWS_ROWS), 0.0)) for n in chunks]
    for n in chunks:
        d_ref[n] = found[n]
        dd_ref[n] = mm(two(sc_ref[n]), drs[n], COLS_COLS)
    dqs = [mm(drs[n], states[n], ROWS_ROWS) + mm(dss[n], keys[n]) for n in chunks]
    for n in chunks:
        dk_ref[n] = mm(dss[n], two(qs[n]), COLS_COLS)
    for n in chunks:
        part = fq_ref[n] * (dqs[n] - qs[n] * jnp.sum(qs[n] * dqs[n], axis=-1, keepdims=True))
        inner, rim = conv_back(part, taps, pad.at[n], 1)
        nq_ref[n, pl.ds(0, tokens), :] = nm_ref[n]
        nq_ref[n, pl.ds(tokens, tokens), :] = inner.astype(BF16)
        nq_ref[n, pl.ds(2 * tokens, EDGE), :] = jnp.concatenate([rim, jnp.zeros((8, HEAD), F32)], axis=0).astype(BF16)


def grads_kernel(
    per, tokens, slots, hid, beta_ref, wts_ref, end_ref, mb_ref, kh_ref, kl_ref, th_ref, tl_ref, d_ref, dk_ref, dd_ref,
    st_ref, fk_ref, fv_ref, out_ref, pad,
):
    rows = tokens * slots
    wts = wts_ref[...]
    order = before(rows)
    end = two(jnp.where((hid[0] & AFTER) > 0, end_ref[...], 0.0))
    chunks = range(per)
    keys = [(kh_ref[n], kl_ref[n]) for n in chunks]
    gs = [two(mm(two(mb_ref[n, :, pl.ds(0, HEAD)]), end) + mb_ref[n, :, pl.ds(HEAD, HEAD)]) for n in chunks]
    dds = [two(dd_ref[n] + mm(keys[n], gs[n])) for n in chunks]
    ys = [mm((th_ref[n], tl_ref[n]), dds[n]) for n in chunks]
    betas = [beta_rows(beta_ref[n].astype(F32), slots) for n in chunks]
    des = [2.0 * sigmoid(column(betas[n], tokens, slots)) * ys[n] for n in chunks]
    halves = [two(des[n]) for n in chunks]
    ds = [two(d_ref[n]) for n in chunks]
    grams = [jnp.where(order, mm_half(halves[n], ds[n], ROWS_ROWS), 0.0) for n in chunks]
    direct = [
        dk_ref[n] + mm(ds[n], gs[n], ROWS_ROWS) - mm(halves[n], two(st_ref[n]), ROWS_ROWS) for n in chunks
    ]
    dks = [direct[n] - mm(two(grams[n] + grams[n].T), keys[n]) for n in chunks]
    for n in chunks:
        along = jnp.sum(ys[n] * d_ref[n], axis=1, keepdims=True)
        marks = []
        for j in range(slots):
            gb = jnp.sum(jnp.where(places(tokens, slots, j), along, 0.0), axis=0, keepdims=True)
            gb = gb * sigmoid(-betas[n][j])
            high = gb.astype(BF16).astype(F32)
            marks += [high, gb - high]
        marks.append(jnp.zeros((EDGE - 2 * slots, tokens), F32))
        value, value_rim = conv_back(fv_ref[n] * des[n], slot_taps(wts, 1), pad.at[2 * n], slots)
        k = keys[n][0].astype(F32) + keys[n][1].astype(F32)
        part = fk_ref[n] * (dks[n] - k * jnp.sum(k * dks[n], axis=-1, keepdims=True))
        key, key_rim = conv_back(part, slot_taps(wts, 0), pad.at[2 * n + 1], slots)
        out_ref[n, pl.ds(0, rows), :] = key.astype(BF16)
        out_ref[n, pl.ds(rows, rows), :] = value.astype(BF16)
        out_ref[n, pl.ds(2 * rows, EDGE), :] = jnp.concatenate(marks, axis=0).astype(BF16)
        out_ref[n, pl.ds(2 * rows + EDGE, EDGE), :] = jnp.concatenate([key_rim, value_rim], axis=0).astype(BF16)


def unpack_kernel(per, tokens, slots, got_ref, gk_ref, gv_ref):
    rows = tokens * slots
    for n in range(per):
        for a, out_ref in enumerate((gk_ref, gv_ref)):
            main = got_ref[n, pl.ds(a * rows, rows), :].astype(F32)
            out_ref[:, :, pl.ds(n * HEAD, HEAD)] = main.reshape(tokens, slots, HEAD)


def unpack_query_kernel(per, tokens, got_ref, gq_ref):
    for n in range(per):
        gq_ref[:, pl.ds(n * HEAD, HEAD)] = got_ref[n, pl.ds(tokens, tokens), :].astype(F32)


def rims_kernel(heads, slots, rim_ref, gq_ref, gk_ref, gv_ref, mark_ref, nq_ref, nk_ref, nv_ref, gb_ref):
    for h in range(heads):
        part = pl.ds(h * HEAD, HEAD)
        rim = rim_ref[h].astype(F32)
        nq_ref[:, part] = gq_ref[:, part] + rim[:8]
        nk_ref[:, :, part] = gk_ref[:, :, part] + rim[8:16].reshape(8 // slots, slots, HEAD)
        nv_ref[:, :, part] = gv_ref[:, :, part] + rim[16:].reshape(8 // slots, slots, HEAD)
        mark = mark_ref[h].astype(F32)
        for j in range(slots):
            gb_ref[j, pl.ds(h, 1), :] = mark[2 * j : 2 * j + 1] + mark[2 * j + 1 : 2 * j + 2]


FAR = ("kh", "kl", "xh", "xl", "th", "tl", "wh", "wl", "a", "m", "fk", "fv", "stf", "mbf", "d", "dk", "dd")


def call(kernel, hid, steps, live, ins, reads, outs, scratch=(), us=1.0, grant=40):
    def spec(shape, how):
        if how == "weights":
            return pl.BlockSpec((shape[0], HEAD), lambda i, h: (0, h[0] & (BEFORE - 1)))
        if how is None:
            return pl.BlockSpec(shape, lambda i, h: (0,) * len(shape))
        if isinstance(how, tuple):
            kind, count, row = how
            if kind == "prev":
                return pl.BlockSpec((1, EDGE, HEAD), lambda i, h: (jnp.maximum(i * count - 1, 0), row // EDGE, 0))
            return pl.BlockSpec((count, EDGE, HEAD), lambda i, h: (i, row // EDGE, 0))
        return pl.BlockSpec((how,) + tuple(shape[1:]), lambda i, h: (i,) + (0,) * (len(shape) - 1))

    def home(name):
        return pltpu.HBM if name in FAR else pltpu.VMEM

    operands = [a for a, _ in ins]
    operands += [pltpu.with_memory_space_constraint(live[name], home(name)) for name, _ in reads]
    hows = [how for _, how in ins + reads]
    results = pl.pallas_call(
        kernel,
        grid_spec=pltpu.PrefetchScalarGridSpec(
            num_scalar_prefetch=1,
            grid=(steps,),
            in_specs=[spec(a.shape, how) for a, how in zip(operands, hows)],
            out_specs=[spec(shape, how) for _, shape, _, how in outs],
            scratch_shapes=list(scratch),
        ),
        out_shape=[
            jax.ShapeDtypeStruct(shape, dtype) if name is None else home(name)(shape, dtype)
            for name, shape, dtype, _ in outs
        ],
        compiler_params=pltpu.CompilerParams(dimension_semantics=("arbitrary",), vmem_limit_bytes=grant << 20),
        cost_estimate=pl.CostEstimate(flops=int(us * 1.1e9), bytes_accessed=1 << 16, transcendentals=0),
    )(hid, *operands)
    for (name, _, _, _), result in zip(outs, results):
        if name is not None:
            live[name] = result
    return [r for (name, _, _, _), r in zip(outs, results) if name is None]


def shards(
    query_in,
    key_in,
    value_in,
    beta_logit,
    query_conv,
    key_conv,
    value_conv,
    norm_gain,
    out_weight,
    grad_out,
):
    tokens, slots = key_in.shape[0], key_in.shape[1]
    width = query_in.shape[1]
    heads = width // HEAD
    shard_count = lax.axis_size("ctx")
    place = lax.axis_index("ctx")
    groups = shard_count // heads
    group_lists = [[b * heads + i for i in range(heads)] for b in range(groups)]
    rows = tokens * slots
    g = heads
    first, final = place < heads, place >= shard_count - heads
    hid = (place % heads + jnp.where(first, 0, BEFORE) + jnp.where(final, 0, AFTER)).astype(jnp.int32).reshape(1)

    def exchange(x):
        return lax.all_to_all(x, "ctx", 0, 0, axis_index_groups=group_lists, tiled=True)

    def by_head(x):
        return x.reshape(x.shape[0], heads, HEAD).transpose(1, 0, 2)

    def slots_by_head(x):
        return x.reshape(x.shape[0], slots, heads, HEAD).transpose(2, 0, 1, 3).reshape(heads, -1, HEAD)

    high = lax.reduce_precision(beta_logit, 8, 7)
    rest = beta_logit - high
    middle = lax.reduce_precision(rest, 8, 7)
    betas = jnp.stack([high, middle, rest - middle], axis=2)
    betas = betas.transpose(3, 1, 2, 0).reshape(heads, 3 * slots, tokens).astype(BF16)
    betas = jnp.pad(betas, ((0, 0), (0, EDGE - 3 * slots), (0, 0)))
    last = EDGE // slots
    kb = exchange(
        jnp.concatenate(
            [slots_by_head(key_in), betas, slots_by_head(value_in[-last:]), by_head(query_in[-EDGE:])], axis=1
        )
    )

    group = place // heads
    tail = jnp.concatenate([kb[g - 1, rows - EDGE : rows], kb[g - 1, rows + EDGE :]], axis=0)

    grad_normed = jnp.dot(grad_out, out_weight.T, preferred_element_type=F32).astype(BF16)
    vq = jnp.concatenate([slots_by_head(value_in), by_head(query_in), by_head(grad_normed)], axis=1)
    vq, tail = lax.optimization_barrier((vq, tail))
    tail = lax.ppermute(tail, "ctx", [(i, (i + heads) % shard_count) for i in range(shard_count)])
    vq, tail = lax.optimization_barrier((vq, tail))
    vq = exchange(vq)

    wts = jnp.concatenate(
        [
            jnp.tile(key_conv, (1, 8 // slots, 1)).reshape(8 * TAPS, width),
            jnp.tile(value_conv, (1, 8 // slots, 1)).reshape(8 * TAPS, width),
            query_conv,
            norm_gain.reshape(1, width),
            jnp.zeros((3, width), F32),
        ],
        axis=0,
    )
    per = 4 if g % 4 == 0 else 1
    steps = g // per

    def pad(n):
        return [pltpu.VMEM((per, n + EDGE + 8, HEAD), F32)]

    def big(name, *shape, per=per, kind=F32):
        return (name, (g,) + shape, kind, per)

    live = {}
    wide = 4 if g % 4 == 0 else per
    (m_end,) = call(
        functools.partial(inverse_kernel, wide, tokens, slots),
        hid,
        g // wide,
        live,
        [(kb, wide), (kb, ("prev", wide, rows - EDGE)), (tail, None), (wts, "weights")],
        [],
        [big(name, rows, HEAD, per=wide, kind=BF16) for name in ("kh", "kl")]
        + [big(name, rows, rows, per=wide, kind=BF16) for name in ("xh", "xl", "th", "tl")]
        + [big(name, rows, HEAD, per=wide, kind=BF16) for name in ("wh", "wl")]
        + [
            big("fk", rows, HEAD, per=wide), big("a", HEAD, HEAD, per=wide), big("m", HEAD, HEAD, per=wide),
            (None, (HEAD, HEAD), F32, None),
        ],
        scratch=[pltpu.VMEM((wide, rows + EDGE + 8, HEAD), F32), pltpu.VMEM((HEAD, HEAD), F32)],
        us=11.0,
        grant=40,
    )
    beta = (kb, ("rows", per, rows))
    (c_end,) = call(
        functools.partial(maps_kernel, per, tokens, slots),
        hid,
        steps,
        live,
        [(vq, per), (vq, ("prev", per, rows - EDGE)), beta, (tail, None), (wts, "weights")],
        [(name, per) for name in ("kh", "kl", "xh", "xl", "a")],
        [
            big("u", rows, HEAD), big("c", HEAD, HEAD),
            big("fv", rows, HEAD), (None, (HEAD, HEAD), F32, None),
        ],
        scratch=pad(rows) + [pltpu.VMEM((HEAD, HEAD), F32)],
        us=6.0,
    )

    def across(last, towards):
        if groups == 1:
            return jnp.zeros((HEAD, HEAD), F32)
        if groups == 2:
            moves = [(i, (i + towards * heads) % shard_count) for i in range(shard_count)]
            return lax.ppermute(last[1], "ctx", moves)
        every = lax.all_gather(jnp.concatenate(last, axis=1), "ctx")
        head = place % heads
        ahead = group if towards > 0 else groups - 1 - group

        def advance(i, state):
            source = i if towards > 0 else groups - 1 - i
            item = lax.dynamic_index_in_dim(every, source * heads + head, 0, False)
            return jnp.dot(item[:, :HEAD], state, precision=lax.Precision.HIGHEST) + item[:, HEAD:]

        return lax.fori_loop(0, ahead, advance, jnp.zeros((HEAD, HEAD), F32))

    start = across((m_end, c_end), 1)
    call(
        functools.partial(queries_kernel, per, tokens, slots),
        hid,
        steps,
        live,
        [(vq, per), (vq, ("prev", per, rows + tokens - EDGE)), (tail, None), (wts, "weights")],
        [(name, per) for name in ("kh", "kl", "wh", "wl", "u", "a", "m")],
        [
            big("q", tokens, HEAD), big("sc", tokens, rows), big("qm", tokens, HEAD), big("ol", tokens, HEAD),
            big("fq", tokens, HEAD), big("an", HEAD, HEAD), big("mn", HEAD, HEAD),
        ],
        scratch=pad(tokens),
        us=8.0,
    )
    normed, back_end = call(
        functools.partial(outs_kernel, g, tokens, slots),
        hid,
        1,
        live,
        [(vq, g), (wts, "weights"), (start, None)],
        [(name, g) for name in ("mn", "c", "qm", "ol", "an")],
        [
            big("st", HEAD, HEAD, per=g), big("dr", tokens, HEAD, per=g), big("mb", HEAD, 2 * HEAD, per=g),
            (None, (g, tokens, HEAD), BF16, g), (None, (HEAD, 2 * HEAD), F32, None),
        ],
        us=4.0,
    )
    finish = across((back_end[:, :HEAD], back_end[:, HEAD:]), -1)
    (nq,) = call(
        functools.partial(query_grads_kernel, per, tokens, slots),
        hid,
        steps,
        live,
        [(wts, "weights"), (normed, per)],
        [(name, per) for name in ("kh", "kl", "wh", "wl", "u", "q", "sc", "dr", "st", "fq", "mb")],
        [
            big("d", rows, HEAD), big("dk", rows, HEAD), big("dd", rows, HEAD), big("stf", HEAD, HEAD),
            big("mbf", HEAD, 2 * HEAD), (None, (g, 2 * tokens + EDGE, HEAD), BF16, per),
        ],
        scratch=pad(tokens),
        us=20.0,
    )
    nq = exchange(nq)
    (grads,) = call(
        functools.partial(grads_kernel, per, tokens, slots),
        hid,
        steps,
        live,
        [beta, (wts, "weights"), (finish, None)],
        [(name, per) for name in ("mbf", "kh", "kl", "th", "tl", "d", "dk", "dd", "stf", "fk", "fv")],
        [(None, (g, 2 * rows + 2 * EDGE, HEAD), BF16, per)],
        scratch=[pltpu.VMEM((2 * per, rows + EDGE + 8, HEAD), F32)],
        us=20.0,
    )
    grads = exchange(grads)

    normed_bf = nq[:, :tokens].transpose(1, 0, 2).reshape(tokens, width)
    partial = jnp.dot(normed_bf, out_weight, preferred_element_type=F32)
    if lax.axis_size("head") == 2:
        half = tokens // 2
        mine = lax.axis_index("head")
        pieces = partial.reshape(2, half, partial.shape[1])
        kept = lax.dynamic_index_in_dim(pieces, mine, 0, False)
        sent = lax.dynamic_index_in_dim(pieces, 1 - mine, 0, False).astype(BF16)
        layer_out = (kept + lax.ppermute(sent, "head", [(0, 1), (1, 0)]).astype(F32)).astype(BF16)
    else:
        layer_out = lax.psum_scatter(partial.astype(BF16), "head", scatter_dimension=0, tiled=True)

    rim = jnp.concatenate([nq[:, 2 * tokens : 2 * tokens + 8], grads[:, 2 * rows + EDGE :]], axis=1)
    rim = lax.ppermute(rim, "ctx", [(i, i - 1) for i in range(1, shard_count)])
    small = pltpu.CompilerParams(vmem_limit_bytes=8 << 20)
    cost = lambda us: pl.CostEstimate(flops=int(us * 1.1e9), bytes_accessed=1 << 16, transcendentals=0)
    grad_query = pl.pallas_call(
        functools.partial(unpack_query_kernel, per, tokens),
        grid=(steps,),
        in_specs=[pl.BlockSpec((per,) + nq.shape[1:], lambda h: (h, 0, 0))],
        out_specs=pl.BlockSpec((tokens, per * HEAD), lambda h: (0, h)),
        out_shape=jax.ShapeDtypeStruct((tokens, width), F32),
        compiler_params=small,
        cost_estimate=cost(2.0),
    )(nq)
    grad_key, grad_value = pl.pallas_call(
        functools.partial(unpack_kernel, per, tokens, slots),
        grid=(steps,),
        in_specs=[pl.BlockSpec((per,) + grads.shape[1:], lambda h: (h, 0, 0))],
        out_specs=[pl.BlockSpec((tokens, slots, per * HEAD), lambda h: (0, 0, h))] * 2,
        out_shape=[jax.ShapeDtypeStruct((tokens, slots, width), F32)] * 2,
        compiler_params=small,
        cost_estimate=cost(10.0),
    )(grads)
    flat = pl.BlockSpec((8, width), lambda i: (tokens // 8 - 1, 0))
    deep = pl.BlockSpec((8 // slots, slots, width), lambda i: (tokens * slots // 8 - 1, 0, 0))
    mark = pl.BlockSpec((heads, EDGE, tokens), lambda i: (0, 2 * rows // EDGE, 0))
    beta_spec = pl.BlockSpec((slots, heads, tokens), lambda i: (0, 0, 0))
    grad_query, grad_key, grad_value, grad_beta = pl.pallas_call(
        functools.partial(rims_kernel, heads, slots),
        grid=(1,),
        in_specs=[pl.BlockSpec(rim.shape, lambda i: (0, 0, 0)), flat, deep, deep, mark],
        out_specs=[flat, deep, deep, beta_spec],
        out_shape=[jax.ShapeDtypeStruct(x.shape, F32) for x in (grad_query, grad_key, grad_value)]
        + [jax.ShapeDtypeStruct((slots, heads, tokens), F32)],
        input_output_aliases={1: 0, 2: 1, 3: 2},
        compiler_params=small,
    )(rim, grad_query, grad_key, grad_value, grads)
    grad_beta = grad_beta.transpose(2, 0, 1)
    return (layer_out, grad_query, grad_key, grad_value, grad_beta)


def solution(mesh):
    placed = (
        P("ctx", "head"),
        P("ctx", None, "head"),
        P("ctx", None, "head"),
        P("ctx", None, "head"),
        P(None, "head"),
        P(None, None, "head"),
        P(None, None, "head"),
        P("head"),
        P("head", None),
        P("ctx", None),
    )
    return jax.shard_map(
        shards,
        mesh=mesh,
        in_specs=placed,
        out_specs=(
            P(("ctx", "head"), None),
            P("ctx", "head"),
            P("ctx", None, "head"),
            P("ctx", None, "head"),
            P("ctx", None, "head"),
        ),
        check_vma=False,
    )
```
